32 devices in a mesh: gx: 2 (over x), gy: 4 (over z), gz: 4 (over y, core).
Axes of the slice: x: 2, y: 2, z: 4, core: 2. Of those that a mesh axis runs over, the one named last changes fastest.
Arguments:
- phase_field: int32 [32, 32, 512], P('gz', 'gx', 'gy'), may hold values 0 or 1
- thermal: float32 [32, 32, 512], P('gz', 'gx', 'gy'), may hold values from 0.5 to 1.5
- velocity: float32 [3, 32, 32, 512], P(None, 'gz', 'gx', 'gy'), may hold values from -6 to 6
- transfer_slope: float32 [8, 4], replicated, may hold values from -3 to 3
- transfer_offset: float32 [8, 4], replicated, may hold values from -1 to 1
- transfer_gain: float32 [8], replicated, may hold values from 0.5 to 4
Outputs:
- corrected: float32 [3, 32, 32, 512], P(None, 'gz', 'gx', 'gy')
- images: float32 [8, 4, 32, 512], P('gz', None, 'gx', 'gy')
The draws below stay inside these ranges and needn't reach their ends.
All inputs are finite; a program needn't handle non-finite values. No bound on the sum of `phase_field` on one device may be relied on, other than what follows from the above.
Results may differ from the reference program's by a relative error of at most 0.0001.
Values sent between devices are 32-bit elements; how exact they have to be, the bound alone decides.
No kernel may reach another device: no remote copies, remote signals or barrier semaphores. Data moves between devices by JAX's collectives and lax.ppermute only.
A program may use at most 64 MiB of HBM per device.

```python
import math
import jax
import jax.numpy as jnp
from jax import lax

ITERS = 4
TF = 8
NZ = 32
NX = 32
NY = 512


def touch_ends(drawn, key, low, largest):
    longest = drawn.shape.index(max(drawn.shape))
    spots = []
    for shift in (0, 1):
        where = [jax.random.randint(jax.random.fold_in(key, axis), (), 0, length) for axis, length in enumerate(drawn.shape)]
        where[longest] = (where[longest] + shift) % drawn.shape[longest]
        spots.append(tuple(where))
    return drawn.at[spots[0]].set(low).at[spots[1]].set(largest)


def shard_levels(key, extent, pieces, low, largest):
    level, own = 1.0, jax.random.fold_in(key, 6)
    for position, parts in pieces:
        heights = jnp.exp(jax.random.uniform(jax.random.fold_in(own, position), (parts,), jnp.float32, low / len(pieces), largest / len(pieces)))
        level = level * jnp.repeat(heights, extent[position] // parts).reshape([-1 if axis == position else 1 for axis in range(len(extent))])
    return level


def noise(stream_key, shape, width, most, pieces=(), held_as=jnp.bfloat16):
    level = shard_levels(stream_key, shape, pieces, -0.22, 0.18) if pieces else 1.0
    result = jax.random.normal(stream_key, shape, jnp.float32) * width * level
    return jnp.minimum(jnp.maximum(result, -most), most).astype(held_as)


def setup_inputs(seed: int = 0) -> dict:
    arg_keys = jax.random.split(jax.random.key(seed), 7)
    return {
        "phase_field": touch_ends((jax.random.randint(arg_keys[0], (NZ, NX, NY), 0, 3) < 1).astype(jnp.int32), jax.random.fold_in(arg_keys[0], 1), 0, 1),
        "thermal": jnp.clip(1.0 + 0.1 * jax.random.normal(arg_keys[1], (NZ, NX, NY), jnp.float32), 0.5, 1.5),
        "velocity": noise(arg_keys[2], (3, NZ, NX, NY), 1.0, 6.0, ((1, 4), (2, 2), (3, 4)), jnp.float32),
        "transfer_slope": jnp.clip(jax.random.uniform(arg_keys[3], (TF, 4), jnp.float32, -3.0, 3.0), -3.0, 3.0),
        "transfer_offset": jnp.clip(jax.random.uniform(arg_keys[4], (TF, 4), jnp.float32, -1.0, 1.0), -1.0, 1.0),
        "transfer_gain": jnp.clip(jnp.exp(jax.random.uniform(arg_keys[5], (TF,), jnp.float32, math.log(0.5), math.log(4.0))), 0.5, 4.0),
    }


def below_zero(field, axis):
    edge = jnp.zeros_like(lax.slice_in_dim(field, 0, 1, axis=axis))
    return jnp.concatenate([edge, lax.slice_in_dim(field, 0, field.shape[axis] - 1, axis=axis)], axis=axis)


def above_zero(field, axis):
    edge = jnp.zeros_like(lax.slice_in_dim(field, 0, 1, axis=axis))
    return jnp.concatenate([lax.slice_in_dim(field, 1, field.shape[axis], axis=axis), edge], axis=axis)


def below_edge(field, axis):
    edge = lax.slice_in_dim(field, 0, 1, axis=axis)
    return jnp.concatenate([edge, lax.slice_in_dim(field, 0, field.shape[axis] - 1, axis=axis)], axis=axis)


def above_edge(field, axis):
    count = field.shape[axis]
    edge = lax.slice_in_dim(field, count - 1, count, axis=axis)
    return jnp.concatenate([lax.slice_in_dim(field, 1, count, axis=axis), edge], axis=axis)


def reference(phase_field, thermal, velocity, transfer_slope, transfer_offset, transfer_gain):
    density = (1.0 + 9.0 * phase_field.astype(jnp.float32)) * thermal
    lowers = [2.0 / (density + below_edge(density, which)) for which in range(3)]
    uppers = [2.0 / (density + above_edge(density, which)) for which in range(3)]
    inverse = 1.0 / (lowers[0] + uppers[0] + lowers[1] + uppers[1] + lowers[2] + uppers[2])

    def operate(field):
        total = jnp.zeros_like(field)
        for which in range(3):
            total = total + lowers[which] * (field - below_zero(field, which))
            total = total + uppers[which] * (field - above_zero(field, which))
        return total

    rhs = jnp.zeros_like(density)
    for which in range(3):
        rhs = rhs - (above_zero(velocity[which], which) - velocity[which])
    pressure = jnp.zeros_like(rhs)
    residual = rhs
    precond = inverse * residual
    direction = precond
    norm_now = jnp.sum(residual * precond)
    for iteration in range(ITERS):
        image = operate(direction)
        alpha = norm_now / jnp.sum(direction * image)
        pressure = pressure + alpha * direction
        residual = residual - alpha * image
        if iteration + 1 < ITERS:
            precond = inverse * residual
            norm_next = jnp.sum(residual * precond)
            direction = precond + (norm_next / norm_now) * direction
            norm_now = norm_next
    corrected = jnp.stack([velocity[which] - lowers[which] * (pressure - below_zero(pressure, which)) for which in range(3)])
    scalar = corrected[0] + corrected[1] + corrected[2]

    def render(index):
        slope = transfer_slope[index]
        offset = transfer_offset[index]
        opacity = transfer_gain[index] / NZ * jax.nn.sigmoid(slope[3] * scalar + offset[3])
        keep = 1.0 - opacity
        inclusive = jnp.cumprod(keep, axis=0)
        passed = jnp.concatenate([jnp.ones_like(inclusive[:1]), inclusive[:-1]], axis=0)
        weight = passed * opacity
        planes = [jnp.sum(weight * jax.nn.sigmoid(slope[channel] * scalar + offset[channel]), axis=0) for channel in range(3)]
        planes.append(1.0 - inclusive[-1])
        return jnp.stack(planes)

    images = lax.map(render, jnp.arange(transfer_slope.shape[0]))
    return corrected, images
```

```python
import math

import jax
import jax.numpy as jnp
from jax import lax
from jax.experimental import pallas as pl
from jax.experimental.pallas import tpu as pltpu
from jax.sharding import PartitionSpec as P

ITERS = 4
HALO = ITERS + 1
FIELDS = 4
LANES = 128
LOG2E = math.log2(math.e)
F32 = jnp.float32


def snake(ngx, ngz):
    order = []
    for x in range(ngx):
        depths = range(ngz) if x % 2 == 0 else reversed(range(ngz))
        order.extend((x, z) for z in depths)
    return order


def chain_pairs(ngx, ngy, ngz, hop):
    places = []
    order = snake(ngx, ngz)
    for y in range(ngy):
        for x, z in order if y % 2 == 0 else order[::-1]:
            places.append((x * ngy + y) * ngz + z)
    return list(zip(places[:-hop], places[hop:]))


def roll(value, shift, axis):
    size = value.shape[axis]
    shift = shift % size
    return value if shift == 0 else pltpu.roll(value, shift, axis)


def owner(table, c):
    forward = lax.axis_index("gy") % 2 == 0
    return jnp.where(forward, table[c], table[len(table) - 1 - c])


def pack_kernel(phase_ref, thermal_ref, velocity_ref, out_ref, *, table, chunk):
    zl, xl, yl = thermal_ref.shape
    density = (1.0 + 9.0 * phase_ref[...].astype(F32)) * thermal_ref[...]
    for f in range(FIELDS):
        field = density if f == 0 else velocity_ref[f - 1]
        turned = field.reshape(zl * xl, yl).T
        for c in range(yl // chunk):
            rows = turned[c * chunk : (c + 1) * chunk]
            out_ref[owner(table, c), pl.ds(f, chunk, stride=FIELDS), :] = rows


class Shifts:
    def __init__(self, ngx, ngz, zl, xl):
        self.ngx, self.ngz, self.zl, self.xl = ngx, ngz, zl, xl
        shape = (1, ngx * ngz, zl * xl)
        lane = lax.broadcasted_iota(jnp.int32, shape, 2)
        sub = lax.broadcasted_iota(jnp.int32, shape, 1)
        z, x = lane // xl, lane % xl
        gz, gx = sub // ngx, sub % ngx
        self.z_first, self.z_last = z == 0, z == zl - 1
        self.x_first, self.x_last = x == 0, x == xl - 1
        self.z_low = self.z_first & (gz == 0)
        self.z_high = self.z_last & (gz == ngz - 1)
        self.x_low = self.x_first & (gx == 0)
        self.x_high = self.x_last & (gx == ngx - 1)

    def below_z(self, f):
        near = roll(f, self.xl, 2)
        return jnp.where(self.z_first, roll(near, self.ngx, 1), near)

    def above_z(self, f):
        near = roll(f, -self.xl, 2)
        return jnp.where(self.z_last, roll(near, -self.ngx, 1), near)

    def below_x(self, f):
        far = roll(roll(f, 1 - self.xl, 2), 1, 1)
        return jnp.where(self.x_first, far, roll(f, 1, 2))

    def above_x(self, f):
        far = roll(roll(f, self.xl - 1, 2), -1, 1)
        return jnp.where(self.x_last, far, roll(f, -1, 2))


def krylov_kernel(*refs, ngx, ngz, zl, xl, chunk, hops, margin, step):
    own_ref = refs[0]
    low_refs, high_refs = refs[1 : 1 + hops], refs[1 + hops : 1 + 2 * hops]
    basis_ref, lower_ref, sums_ref, dens, coef, vec, diag, source = refs[1 + 2 * hops :]
    S, L = ngx * ngz, zl * xl
    E = chunk + 2 * HALO
    move = Shifts(ngx, ngz, zl, xl)

    def plane(e, f):
        k = e - HALO
        if 0 <= k < chunk:
            return own_ref[pl.ds(k * FIELDS + f, S, stride=chunk * FIELDS), :]
        far = -k - 1 if k < 0 else k - chunk
        hop, at = far // chunk, far % chunk
        ref = low_refs[hop] if k < 0 else high_refs[hop]
        at = margin - 1 - at if k < 0 else at
        return ref[pl.ds(at * FIELDS + f, S, stride=margin * FIELDS), :]

    def planes(a, b, f):
        return jnp.stack([plane(e, f) for e in range(a, b)])

    def pieces(a, b):
        return [(i, min(i + step, b)) for i in range(a, b, step)]

    for e in range(E):
        dens[e] = plane(e, 0)
    for a, b in pieces(1, E - 1):
        d, before, after = dens[a:b], dens[a - 1 : b - 1], dens[a + 1 : b + 1]
        inside = d > 0.0
        d = jnp.where(inside, d, 1.0)

        def face(missing, other):
            return 2.0 / (d + jnp.where(missing, d, other))

        lz, uz = face(move.z_low, move.below_z(d)), face(move.z_high, move.above_z(d))
        lx, ux = face(move.x_low, move.below_x(d)), face(move.x_high, move.above_x(d))
        ly, uy = face(before <= 0.0, before), face(after <= 0.0, after)
        total = lz + uz + lx + ux + ly + uy
        inverse = jnp.where(inside, 1.0 / total, 0.0)
        coef[0, a:b] = jnp.where(move.z_low, 0.0, inverse * lz)
        coef[1, a:b] = jnp.where(move.z_high, 0.0, inverse * uz)
        coef[2, a:b] = jnp.where(move.x_low, 0.0, inverse * lx)
        coef[3, a:b] = jnp.where(move.x_high, 0.0, inverse * ux)
        coef[4, a:b] = inverse * ly
        coef[5, a:b] = inverse * uy
        vz, vx = planes(a, b, 1), planes(a, b, 2)
        rhs = -(jnp.where(move.z_high, 0.0, move.above_z(vz)) - vz)
        rhs = rhs - (jnp.where(move.x_high, 0.0, move.above_x(vx)) - vx)
        rhs = rhs - (planes(a + 1, b + 1, 3) - planes(a, b, 3))
        vec[0, a:b] = inverse * rhs
        for e in range(max(a, HALO), min(b, HALO + chunk)):
            diag[e - HALO] = total[e - a]
            source[e - HALO] = rhs[e - a]
            for k, faces in enumerate((lz, lx, ly)):
                lower_ref[k, e - HALO] = faces[e - a]

    def applied(k, a, b):
        f = vec[k, a:b]
        out = coef[0, a:b] * move.below_z(f) + coef[1, a:b] * move.above_z(f)
        out = out + (coef[2, a:b] * move.below_x(f) + coef[3, a:b] * move.above_x(f))
        return out + (coef[4, a:b] * vec[k, a - 1 : b - 1] + coef[5, a:b] * vec[k, a + 1 : b + 1])

    for k in range(1, ITERS):
        for a, b in pieces(1 + k, E - 1 - k):
            vec[k, a:b] = applied(k - 1, a, b)

    count = 2 * ITERS - 1
    powers = [0.0] * count
    firsts = [0.0] * ITERS
    steps = [0.0] * (count + 1)
    for a, b in pieces(HALO, HALO + chunk):
        own = slice(a - HALO, b - HALO)
        basis = [vec[k, a:b] for k in range(ITERS)]
        basis.append(applied(ITERS - 1, a, b))
        weight, right = diag[own], source[own]
        gaps = [basis[k] - basis[k + 1] for k in range(ITERS)]
        scaled = [weight * gap for gap in gaps]
        for k in range(count):
            powers[k] = powers[k] + jnp.sum(basis[(k + 1) // 2] * scaled[k // 2], axis=0)
        for k in range(ITERS):
            firsts[k] = firsts[k] + jnp.sum(right * basis[k], axis=0)
        ladder, level = [basis[0], gaps[0]], gaps
        while len(level) > 1:
            level = [level[i] - level[i + 1] for i in range(len(level) - 1)]
            ladder.append(level[0])
        for k in range(2, count + 1):
            steps[k] = steps[k] + jnp.sum(weight * ladder[k // 2] * ladder[(k + 1) // 2], axis=0)
    steps[0], steps[1] = firsts[0], powers[0]
    for k in range(ITERS):
        basis_ref[k] = vec[k, HALO - 1 : HALO + chunk]

    columns = powers + firsts + steps
    rows = [jnp.sum(c, axis=0, keepdims=True) for c in columns]
    high = -(-len(rows) // 8) * 8
    rows = rows + [jnp.zeros((1, L), F32)] * (high - len(rows))
    sums = jnp.sum(jnp.concatenate(rows, axis=0), axis=1, keepdims=True)
    lane = lax.broadcasted_iota(jnp.int32, (high, LANES), 1)
    row = lax.broadcasted_iota(jnp.int32, (high, LANES), 0)
    line = jnp.sum(jnp.where(lane == row, sums, 0.0), axis=0, keepdims=True)
    sums_ref[...] = jnp.broadcast_to(line, sums_ref.shape)


def galerkin(sums):
    n, count = ITERS, 2 * ITERS - 1
    line = jnp.sum(sums, axis=0, keepdims=True)
    lane = lax.broadcasted_iota(jnp.int32, line.shape, 1)

    def pick(k):
        return jnp.sum(jnp.where(lane == k, line, 0.0), axis=1, keepdims=True)

    powers = [pick(k) for k in range(count)]
    firsts = [pick(count + k) for k in range(n)]
    steps = [pick(count + n + k) for k in range(count + 1)]
    matrix = [jnp.concatenate([powers[k], steps[k + 1]], axis=0) for k in range(count)]
    right = [jnp.concatenate([firsts[k], steps[k]], axis=0) for k in range(n)]
    low = [[None] * n for _ in range(n)]
    scale = [None] * n
    quality = None
    for j in range(n):
        pivot = matrix[2 * j]
        for k in range(j):
            pivot = pivot - low[j][k] * low[j][k] * scale[k][0]
        share = pivot / matrix[2 * j]
        fine = share > 1e-7
        quality = jnp.where(fine, share, 0.0) if quality is None else jnp.minimum(quality, jnp.where(fine, share, 0.0))
        inverse = jnp.where(fine, 1.0 / pivot, 0.0)
        scale[j] = (pivot, inverse)
        for r in range(j + 1, n):
            entry = matrix[r + j]
            for k in range(j):
                entry = entry - low[r][k] * low[j][k] * scale[k][0]
            low[r][j] = entry * inverse
    part = list(right)
    for r in range(n):
        for k in range(r):
            part[r] = part[r] - low[r][k] * part[k]
    part = [part[r] * scale[r][1] for r in range(n)]
    for r in reversed(range(n)):
        for k in range(r + 1, n):
            part[r] = part[r] - low[k][r] * part[k]
    first = quality[0:1] >= quality[1:2]
    by_power = [jnp.where(first, p[0:1], 0.0) for p in part]
    by_step = [jnp.where(first, 0.0, p[1:2]) for p in part]
    return by_power, by_step


def render_kernel(
    sums_ref, basis_ref, lower_ref, own_ref, slope_ref, offset_ref, gain_ref, out_ref, press, flat, turned,
    *, ngx, ngz, zl, xl, chunk, step
):
    S, L = ngx * ngz, zl * xl
    yl = S * chunk
    height = out_ref.shape[0] // S
    move = Shifts(ngx, ngz, zl, xl)
    by_power, by_step = galerkin(sums_ref[...])
    by_power = [v.reshape(1, 1, 1) for v in by_power]
    by_step = [v.reshape(1, 1, 1) for v in by_step]
    for a in range(0, chunk + 1, step):
        b = min(a + step, chunk + 1)
        level = [basis_ref[k, a:b] for k in range(ITERS)]
        value = 0.0
        for k in range(ITERS):
            value = value + by_power[k] * level[k]
        value = value + by_step[0] * level[0]
        for k in range(1, ITERS):
            level = [level[i] - level[i + 1] for i in range(len(level) - 1)]
            value = value + by_step[k] * level[0]
        press[a:b] = value
    for a in range(0, chunk, step):
        b = min(a + step, chunk)
        p = press[a + 1 : b + 1]
        fronts = (
            jnp.where(move.z_low, 0.0, move.below_z(p)),
            jnp.where(move.x_low, 0.0, move.below_x(p)),
            press[a:b],
        )
        scalar = None
        for k, front in enumerate(fronts):
            v = jnp.stack([own_ref[pl.ds(c * FIELDS + k + 1, S, stride=chunk * FIELDS), :] for c in range(a, b)])
            corrected = v - lower_ref[k, a:b] * (p - front)
            for c in range(a, b):
                out_ref[pl.ds(k * chunk + c, S, stride=height), :] = corrected[c - a]
            scalar = corrected if scalar is None else scalar + corrected
        for c in range(a, b):
            flat[pl.ds(c, S, stride=chunk), :] = scalar[c - a]
    turned[...] = flat[...].T.reshape(zl, xl, yl)

    group = ngx * chunk
    functions = slope_ref.shape[0] // ngz
    depth = zl * ngz
    lane = lax.broadcasted_iota(jnp.int32, (xl, yl), 1)

    def owned(i, carry):
        images = [jnp.zeros((xl, LANES), F32) for _ in range(ngx)]
        for t in range(functions):
            index = i * functions + t
            rates = [-LOG2E * slope_ref[index, c] for c in range(4)]
            bases = [-LOG2E * offset_ref[index, c] for c in range(4)]
            gain = gain_ref[index] / depth
            through = jnp.ones((xl, yl), F32)
            colors = [jnp.zeros((xl, yl), F32) for _ in range(3)]
            for z in range(zl):
                x = turned[z]
                curves = [1.0 / (1.0 + jnp.exp2(rates[c] * x + bases[c])) for c in range(4)]
                opacity = gain * curves[3]
                weight = through * opacity
                colors = [colors[c] + weight * curves[c] for c in range(3)]
                through = through * (1.0 - opacity)
            planes = list(colors)
            everything = through
            for _ in range(ngz - 1):
                planes = [colors[c] + through * roll(planes[c], -group, 1) for c in range(3)]
                everything = through * roll(everything, -group, 1)
            planes.append(1.0 - everything)
            for c, image in enumerate(planes):
                start = (t * 4 + c) * chunk
                here = (lane >= start) & (lane < start + chunk)
                for k in range(ngx):
                    images[k] = jnp.where(here, roll(image, start - k * chunk, 1), images[k])
        for k in range(ngx):
            place = pl.multiple_of((i * ngx + k) * height + 3 * chunk, 2)
            out_ref[pl.ds(place, xl), :] = images[k]
        return carry

    lax.fori_loop(0, ngz, owned, 0)


def unpack_kernel(in_ref, corrected_ref, images_ref, flat, *, table, chunk):
    zl, xl, yl = corrected_ref.shape[1:]
    functions = images_ref.shape[0]
    pieces = yl // chunk
    for f in range(3):
        for c in range(pieces):
            flat[c * chunk : (c + 1) * chunk, :] = in_ref[owner(table, c), f * chunk : (f + 1) * chunk, :]
        corrected_ref[f] = flat[...].T.reshape(zl, xl, yl)
    lane = lax.broadcasted_iota(jnp.int32, (xl, yl), 1)
    images = [jnp.zeros((xl, yl), F32) for _ in range(functions * 4)]
    for c in range(pieces):
        source = in_ref[owner(table, c), 3 * chunk : 3 * chunk + xl, :]
        here = (lane >= c * chunk) & (lane < (c + 1) * chunk)
        images = [jnp.where(here, roll(source, (c - k) * chunk, 1), image) for k, image in enumerate(images)]
    for k, image in enumerate(images):
        images_ref[k // 4, k % 4] = image


def solution(mesh):
    ngx, ngy, ngz = mesh.shape["gx"], mesh.shape["gy"], mesh.shape["gz"]
    S, devices = ngx * ngz, ngx * ngy * ngz
    table = [z * ngx + x for x, z in snake(ngx, ngz)]

    def local(phase_field, thermal, velocity, transfer_slope, transfer_offset, transfer_gain):
        zl, xl, yl = thermal.shape
        L, chunk = zl * xl, yl // S
        functions = transfer_slope.shape[0] // ngz
        assert yl % S == 0 and L == LANES and yl == LANES and functions * 4 * chunk <= LANES
        hops = -(-HALO // chunk)
        margin = min(chunk, HALO + HALO % 2)
        step = max(1, 4 * 8 // S)

        def call(body, out, scratch=(), **kwargs):
            return pl.pallas_call(
                lambda *refs: body(*refs, **kwargs),
                out_shape=out,
                scratch_shapes=[pltpu.VMEM(s, F32) for s in scratch],
                name=body.__name__,
            )

        def shaped(*shape):
            return jax.ShapeDtypeStruct(shape, F32)

        blocks = call(pack_kernel, shaped(S, chunk * FIELDS, L), table=table, chunk=chunk)(phase_field, thermal, velocity)
        pencils = lax.all_to_all(blocks, ("gz", "gx"), 0, 0, tiled=True)
        first = pencils[:, : margin * FIELDS]
        last = pencils[:, (chunk - margin) * FIELDS :]
        every = ("gx", "gy", "gz")
        pairs = [chain_pairs(ngx, ngy, ngz, hop + 1) for hop in range(hops)]
        lows = [lax.ppermute(last, every, p) for p in pairs]
        highs = [lax.ppermute(first, every, [(b, a) for a, b in p]) for p in pairs]
        own = pencils.reshape(-1, L)
        wide = chunk + 2 * HALO
        basis, lower, sums = call(
            krylov_kernel,
            (shaped(ITERS, chunk + 1, S, L), shaped(3, chunk, S, L), shaped(devices, LANES)),
            ((wide, S, L), (6, wide, S, L), (ITERS, wide, S, L), (chunk, S, L), (chunk, S, L)),
            ngx=ngx, ngz=ngz, zl=zl, xl=xl, chunk=chunk, hops=hops, margin=margin, step=step,
        )(own, *[v.reshape(-1, L) for v in lows + highs])
        sums = lax.all_to_all(sums, every, 0, 0, tiled=True)
        height = 3 * chunk + xl
        height += -height % 8
        smem = pl.BlockSpec(memory_space=pltpu.SMEM)
        vmem = pl.BlockSpec(memory_space=pltpu.VMEM)
        kwargs = dict(ngx=ngx, ngz=ngz, zl=zl, xl=xl, chunk=chunk, step=step)
        packed = pl.pallas_call(
            lambda *refs: render_kernel(*refs, **kwargs),
            out_shape=shaped(S * height, LANES),
            in_specs=[vmem] * 4 + [smem] * 3,
            scratch_shapes=[pltpu.VMEM(s, F32) for s in ((chunk + 1, S, L), (yl, L), (zl, xl, yl))],
            name="render_kernel",
        )(sums, basis, lower, own, transfer_slope, transfer_offset, transfer_gain)
        home = lax.all_to_all(packed.reshape(S, height, LANES), ("gz", "gx"), 0, 0, tiled=True)
        return call(
            unpack_kernel,
            (shaped(3, zl, xl, yl), shaped(functions, 4, xl, yl)),
            ((yl, L),),
            table=table, chunk=chunk,
        )(home)

    return jax.shard_map(
        local,
        mesh=mesh,
        in_specs=(P("gz", "gx", "gy"), P("gz", "gx", "gy"), P(None, "gz", "gx", "gy"), P(), P(), P()),
        out_specs=(P(None, "gz", "gx", "gy"), P("gz", None, "gx", "gy")),
        check_vma=False,
    )
```

```python
import math

import jax
import jax.numpy as jnp
from jax import lax
from jax.experimental import pallas as pl
from jax.experimental.pallas import tpu as pltpu
from jax.sharding import PartitionSpec as P

ITERS = 4
HALO = ITERS + 1
FIELDS = 4
LANES = 128
LOG2E = math.log2(math.e)
F32 = jnp.float32


def snake(ngx, ngz):
    order = []
    for x in range(ngx):
        depths = range(ngz) if x % 2 == 0 else reversed(range(ngz))
        order.extend((x, z) for z in depths)
    return order


def chain_pairs(ngx, ngy, ngz, hop):
    places = []
    order = snake(ngx, ngz)
    for y in range(ngy):
        for x, z in order if y % 2 == 0 else order[::-1]:
            places.append((x * ngy + y) * ngz + z)
    return list(zip(places[:-hop], places[hop:]))


def roll(value, shift, axis):
    size = value.shape[axis]
    shift = shift % size
    return value if shift == 0 else pltpu.roll(value, shift, axis)


def owner(table, c):
    forward = lax.axis_index("gy") % 2 == 0
    return jnp.where(forward, table[c], table[len(table) - 1 - c])


def pack_kernel(phase_ref, thermal_ref, velocity_ref, out_ref, *, table, chunk):
    zl, xl, yl = thermal_ref.shape
    density = (1.0 + 9.0 * phase_ref[...].astype(F32)) * thermal_ref[...]
    for f in range(FIELDS):
        field = density if f == 0 else velocity_ref[f - 1]
        turned = field.reshape(zl * xl, yl).T
        for c in range(yl // chunk):
            rows = turned[c * chunk : (c + 1) * chunk]
            out_ref[owner(table, c), pl.ds(f, chunk, stride=FIELDS), :] = rows


class Shifts:
    def __init__(self, ngx, ngz, zl, xl):
        self.ngx, self.ngz, self.zl, self.xl = ngx, ngz, zl, xl
        shape = (1, ngx * ngz, zl * xl)
        lane = lax.broadcasted_iota(jnp.int32, shape, 2)
        sub = lax.broadcasted_iota(jnp.int32, shape, 1)
        z, x = lane // xl, lane % xl
        gz, gx = sub // ngx, sub % ngx
        self.z_first, self.z_last = z == 0, z == zl - 1
        self.x_first, self.x_last = x == 0, x == xl - 1
        self.z_low = self.z_first & (gz == 0)
        self.z_high = self.z_last & (gz == ngz - 1)
        self.x_low = self.x_first & (gx == 0)
        self.x_high = self.x_last & (gx == ngx - 1)

    def below_z(self, f):
        near = roll(f, self.xl, 2)
        return jnp.where(self.z_first, roll(near, self.ngx, 1), near)

    def above_z(self, f):
        near = roll(f, -self.xl, 2)
        return jnp.where(self.z_last, roll(near, -self.ngx, 1), near)

    def below_x(self, f):
        far = roll(roll(f, 1 - self.xl, 2), 1, 1)
        return jnp.where(self.x_first, far, roll(f, 1, 2))

    def above_x(self, f):
        far = roll(roll(f, self.xl - 1, 2), -1, 1)
        return jnp.where(self.x_last, far, roll(f, -1, 2))


def krylov_kernel(*refs, ngx, ngz, zl, xl, chunk, hops, margin, step):
    own_ref = refs[0]
    low_refs, high_refs = refs[1 : 1 + hops], refs[1 + hops : 1 + 2 * hops]
    basis_ref, lower_ref, sums_ref, dens, coef, vec, diag, source = refs[1 + 2 * hops :]
    S, L = ngx * ngz, zl * xl
    E = chunk + 2 * HALO
    move = Shifts(ngx, ngz, zl, xl)

    def plane(e, f):
        k = e - HALO
        if 0 <= k < chunk:
            return own_ref[pl.ds(k * FIELDS + f, S, stride=chunk * FIELDS), :]
        far = -k - 1 if k < 0 else k - chunk
        hop, at = far // chunk, far % chunk
        ref = low_refs[hop] if k < 0 else high_refs[hop]
        at = margin - 1 - at if k < 0 else at
        return ref[pl.ds(at * FIELDS + f, S, stride=margin * FIELDS), :]

    def planes(a, b, f):
        return jnp.stack([plane(e, f) for e in range(a, b)])

    def pieces(a, b):
        return [(i, min(i + step, b)) for i in range(a, b, step)]

    for e in range(E):
        dens[e] = plane(e, 0)
    for a, b in pieces(1, E - 1):
        d, before, after = dens[a:b], dens[a - 1 : b - 1], dens[a + 1 : b + 1]
        inside = d > 0.0
        d = jnp.where(inside, d, 1.0)

        def face(missing, other):
            return 2.0 / (d + jnp.where(missing, d, other))

        lz, uz = face(move.z_low, move.below_z(d)), face(move.z_high, move.above_z(d))
        lx, ux = face(move.x_low, move.below_x(d)), face(move.x_high, move.above_x(d))
        ly, uy = face(before <= 0.0, before), face(after <= 0.0, after)
        total = lz + uz + lx + ux + ly + uy
        inverse = jnp.where(inside, 1.0 / total, 0.0)
        coef[0, a:b] = jnp.where(move.z_low, 0.0, inverse * lz)
        coef[1, a:b] = jnp.where(move.z_high, 0.0, inverse * uz)
        coef[2, a:b] = jnp.where(move.x_low, 0.0, inverse * lx)
        coef[3, a:b] = jnp.where(move.x_high, 0.0, inverse * ux)
        coef[4, a:b] = inverse * ly
        coef[5, a:b] = inverse * uy
        vz, vx = planes(a, b, 1), planes(a, b, 2)
        rhs = -(jnp.where(move.z_high, 0.0, move.above_z(vz)) - vz)
        rhs = rhs - (jnp.where(move.x_high, 0.0, move.above_x(vx)) - vx)
        rhs = rhs - (planes(a + 1, b + 1, 3) - planes(a, b, 3))
        vec[0, a:b] = inverse * rhs
        for e in range(max(a, HALO), min(b, HALO + chunk)):
            diag[e - HALO] = total[e - a]
            source[e - HALO] = rhs[e - a]
            for k, faces in enumerate((lz, lx, ly)):
                lower_ref[k, e - HALO] = faces[e - a]

    def applied(k, a, b):
        f = vec[k, a:b]
        out = coef[0, a:b] * move.below_z(f) + coef[1, a:b] * move.above_z(f)
        out = out + (coef[2, a:b] * move.below_x(f) + coef[3, a:b] * move.above_x(f))
        return out + (coef[4, a:b] * vec[k, a - 1 : b - 1] + coef[5, a:b] * vec[k, a + 1 : b + 1])

    for k in range(1, ITERS):
        for a, b in pieces(1 + k, E - 1 - k):
            vec[k, a:b] = applied(k - 1, a, b)

    count = 2 * ITERS - 1
    powers = [0.0] * count
    firsts = [0.0] * ITERS
    steps = [0.0] * (count + 1)
    for a, b in pieces(HALO, HALO + chunk):
        own = slice(a - HALO, b - HALO)
        basis = [vec[k, a:b] for k in range(ITERS)]
        basis.append(applied(ITERS - 1, a, b))
        weight, right = diag[own], source[own]
        gaps = [basis[k] - basis[k + 1] for k in range(ITERS)]
        scaled = [weight * gap for gap in gaps]
        for k in range(count):
            powers[k] = powers[k] + jnp.sum(basis[(k + 1) // 2] * scaled[k // 2], axis=0)
        for k in range(ITERS):
            firsts[k] = firsts[k] + jnp.sum(right * basis[k], axis=0)
        ladder, level = [basis[0], gaps[0]], gaps
        while len(level) > 1:
            level = [level[i] - level[i + 1] for i in range(len(level) - 1)]
            ladder.append(level[0])
        for k in range(2, count + 1):
            steps[k] = steps[k] + jnp.sum(weight * ladder[k // 2] * ladder[(k + 1) // 2], axis=0)
    steps[0], steps[1] = firsts[0], powers[0]
    for k in range(ITERS):
        basis_ref[k] = vec[k, HALO - 1 : HALO + chunk]

    columns = powers + firsts + steps
    rows = [jnp.sum(c, axis=0, keepdims=True) for c in columns]
    high = -(-len(rows) // 8) * 8
    rows = rows + [jnp.zeros((1, L), F32)] * (high - len(rows))
    sums = jnp.sum(jnp.concatenate(rows, axis=0), axis=1, keepdims=True)
    lane = lax.broadcasted_iota(jnp.int32, (high, LANES), 1)
    row = lax.broadcasted_iota(jnp.int32, (high, LANES), 0)
    line = jnp.sum(jnp.where(lane == row, sums, 0.0), axis=0, keepdims=True)
    sums_ref[...] = jnp.broadcast_to(line, sums_ref.shape)


def galerkin(sums):
    n, count = ITERS, 2 * ITERS - 1
    line = jnp.sum(sums, axis=0, keepdims=True)
    lane = lax.broadcasted_iota(jnp.int32, line.shape, 1)

    def pick(k):
        return jnp.sum(jnp.where(lane == k, line, 0.0), axis=1, keepdims=True)

    powers = [pick(k) for k in range(count)]
    firsts = [pick(count + k) for k in range(n)]
    steps = [pick(count + n + k) for k in range(count + 1)]
    matrix = [jnp.concatenate([powers[k], steps[k + 1]], axis=0) for k in range(count)]
    right = [jnp.concatenate([firsts[k], steps[k]], axis=0) for k in range(n)]
    low = [[None] * n for _ in range(n)]
    scale = [None] * n
    quality = None
    for j in range(n):
        pivot = matrix[2 * j]
        for k in range(j):
            pivot = pivot - low[j][k] * low[j][k] * scale[k][0]
        share = pivot / matrix[2 * j]
        fine = share > 1e-7
        quality = jnp.where(fine, share, 0.0) if quality is None else jnp.minimum(quality, jnp.where(fine, share, 0.0))
        inverse = jnp.where(fine, 1.0 / pivot, 0.0)
        scale[j] = (pivot, inverse)
        for r in range(j + 1, n):
            entry = matrix[r + j]
            for k in range(j):
                entry = entry - low[r][k] * low[j][k] * scale[k][0]
            low[r][j] = entry * inverse
    part = list(right)
    for r in range(n):
        for k in range(r):
            part[r] = part[r] - low[r][k] * part[k]
    part = [part[r] * scale[r][1] for r in range(n)]
    for r in reversed(range(n)):
        for k in range(r + 1, n):
            part[r] = part[r] - low[k][r] * part[k]
    first = quality[0:1] >= quality[1:2]
    by_power = [jnp.where(first, p[0:1], 0.0) for p in part]
    by_step = [jnp.where(first, 0.0, p[1:2]) for p in part]
    return by_power, by_step


def render_kernel(
    sums_ref, basis_ref, lower_ref, own_ref, slope_ref, offset_ref, gain_ref, out_ref, press, flat, turned,
    *, ngx, ngz, zl, xl, chunk, step
):
    S, L = ngx * ngz, zl * xl
    yl = S * chunk
    height = out_ref.shape[0] // S
    move = Shifts(ngx, ngz, zl, xl)
    by_power, by_step = galerkin(sums_ref[...])
    by_power = [v.reshape(1, 1, 1) for v in by_power]
    by_step = [v.reshape(1, 1, 1) for v in by_step]
    for a in range(0, chunk + 1, step):
        b = min(a + step, chunk + 1)
        level = [basis_ref[k, a:b] for k in range(ITERS)]
        value = 0.0
        for k in range(ITERS):
            value = value + by_power[k] * level[k]
        value = value + by_step[0] * level[0]
        for k in range(1, ITERS):
            level = [level[i] - level[i + 1] for i in range(len(level) - 1)]
            value = value + by_step[k] * level[0]
        press[a:b] = value
    for a in range(0, chunk, step):
        b = min(a + step, chunk)
        p = press[a + 1 : b + 1]
        fronts = (
            jnp.where(move.z_low, 0.0, move.below_z(p)),
            jnp.where(move.x_low, 0.0, move.below_x(p)),
            press[a:b],
        )
        scalar = None
        for k, front in enumerate(fronts):
            v = jnp.stack([own_ref[pl.ds(c * FIELDS + k + 1, S, stride=chunk * FIELDS), :] for c in range(a, b)])
            corrected = v - lower_ref[k, a:b] * (p - front)
            for c in range(a, b):
                out_ref[pl.ds(k * chunk + c, S, stride=height), :] = corrected[c - a]
            scalar = corrected if scalar is None else scalar + corrected
        for c in range(a, b):
            flat[pl.ds(c, S, stride=chunk), :] = scalar[c - a]
    turned[...] = flat[...].T.reshape(zl, xl, yl)

    group = ngx * chunk
    functions = slope_ref.shape[0] // ngz
    depth = zl * ngz
    lane = lax.broadcasted_iota(jnp.int32, (xl, yl), 1)

    def owned(i, carry):
        images = [jnp.zeros((xl, LANES), F32) for _ in range(ngx)]
        for t in range(functions):
            index = i * functions + t
            rates = [-LOG2E * slope_ref[index, c] for c in range(4)]
            bases = [-LOG2E * offset_ref[index, c] for c in range(4)]
            gain = gain_ref[index] / depth
            through = jnp.ones((xl, yl), F32)
            colors = [jnp.zeros((xl, yl), F32) for _ in range(3)]
            for z in range(zl):
                x = turned[z]
                curves = [1.0 / (1.0 + jnp.exp2(rates[c] * x + bases[c])) for c in range(4)]
                opacity = gain * curves[3]
                weight = through * opacity
                colors = [colors[c] + weight * curves[c] for c in range(3)]
                through = through * (1.0 - opacity)
            planes = list(colors)
            everything = through
            for _ in range(ngz - 1):
                planes = [colors[c] + through * roll(planes[c], -group, 1) for c in range(3)]
                everything = through * roll(everything, -group, 1)
            planes.append(1.0 - everything)
            for c, image in enumerate(planes):
                start = (t * 4 + c) * chunk
                here = (lane >= start) & (lane < start + chunk)
                for k in range(ngx):
                    images[k] = jnp.where(here, roll(image, start - k * chunk, 1), images[k])
        for k in range(ngx):
            place = pl.multiple_of((i * ngx + k) * height + 3 * chunk, 2)
            out_ref[pl.ds(place, xl), :] = images[k]
        return carry

    lax.fori_loop(0, ngz, owned, 0)


def unpack_kernel(in_ref, corrected_ref, images_ref, flat, *, table, chunk):
    zl, xl, yl = corrected_ref.shape[1:]
    functions = images_ref.shape[0]
    pieces = yl // chunk
    for f in range(3):
        for c in range(pieces):
            flat[c * chunk : (c + 1) * chunk, :] = in_ref[owner(table, c), f * chunk : (f + 1) * chunk, :]
        corrected_ref[f] = flat[...].T.reshape(zl, xl, yl)
    lane = lax.broadcasted_iota(jnp.int32, (xl, yl), 1)
    images = [jnp.zeros((xl, yl), F32) for _ in range(functions * 4)]
    for c in range(pieces):
        source = in_ref[owner(table, c), 3 * chunk : 3 * chunk + xl, :]
        here = (lane >= c * chunk) & (lane < (c + 1) * chunk)
        images = [jnp.where(here, roll(source, (c - k) * chunk, 1), image) for k, image in enumerate(images)]
    for k, image in enumerate(images):
        images_ref[k // 4, k % 4] = image


def solution(mesh):
    ngx, ngy, ngz = mesh.shape["gx"], mesh.shape["gy"], mesh.shape["gz"]
    S, devices = ngx * ngz, ngx * ngy * ngz
    table = [z * ngx + x for x, z in snake(ngx, ngz)]

    def local(phase_field, thermal, velocity, transfer_slope, transfer_offset, transfer_gain):
        zl, xl, yl = thermal.shape
        L, chunk = zl * xl, yl // S
        functions = transfer_slope.shape[0] // ngz
        assert yl % S == 0 and L == LANES and yl == LANES and functions * 4 * chunk <= LANES
        hops = -(-HALO // chunk)
        margin = min(chunk, HALO + HALO % 2)
        step = max(1, 4 * 8 // S)

        vmem, smem = (pl.BlockSpec(memory_space=space) for space in (pltpu.VMEM, pltpu.SMEM))

        def call(body, specs, out, scratch=(), **kwargs):
            kernel = pl.pallas_call(
                lambda *refs: body(*refs, **kwargs),
                in_specs=specs,
                out_specs=jax.tree.map(lambda _: vmem, out),
                out_shape=out,
                scratch_shapes=[pltpu.VMEM(s, F32) for s in scratch],
                name=body.__name__,
            )

            def run(*args):
                return kernel(*[near(a) if spec is vmem else a for a, spec in zip(args, specs)])

            return run

        def near(array):
            return pltpu.with_memory_space_constraint(array, pltpu.VMEM)

        def shaped(*shape):
            return jax.ShapeDtypeStruct(shape, F32)

        def placed(*shape):
            return pltpu.VMEM(shape, F32)

        free = pl.BlockSpec()
        blocks = call(pack_kernel, [free] * 3, placed(S, chunk * FIELDS, L), table=table, chunk=chunk)(
            phase_field, thermal, velocity
        )
        pencils = lax.all_to_all(blocks, ("gz", "gx"), 0, 0, tiled=True)
        first = pencils[:, : margin * FIELDS]
        last = pencils[:, (chunk - margin) * FIELDS :]
        every = ("gx", "gy", "gz")
        pairs = [chain_pairs(ngx, ngy, ngz, hop + 1) for hop in range(hops)]
        lows = [lax.ppermute(last, every, p) for p in pairs]
        highs = [lax.ppermute(first, every, [(b, a) for a, b in p]) for p in pairs]
        own = pencils.reshape(-1, L)
        wide = chunk + 2 * HALO
        basis, lower, sums = call(
            krylov_kernel,
            [vmem] * (1 + 2 * hops),
            (placed(ITERS, chunk + 1, S, L), placed(3, chunk, S, L), placed(devices, LANES)),
            ((wide, S, L), (6, wide, S, L), (ITERS, wide, S, L), (chunk, S, L), (chunk, S, L)),
            ngx=ngx, ngz=ngz, zl=zl, xl=xl, chunk=chunk, hops=hops, margin=margin, step=step,
        )(own, *[v.reshape(-1, L) for v in lows + highs])
        sums = lax.all_to_all(sums, every, 0, 0, tiled=True)
        height = 3 * chunk + xl
        height += -height % 8
        packed = call(
            render_kernel,
            [vmem] * 4 + [smem] * 3,
            placed(S * height, LANES),
            ((chunk + 1, S, L), (yl, L), (zl, xl, yl)),
            ngx=ngx, ngz=ngz, zl=zl, xl=xl, chunk=chunk, step=step,
        )(sums, basis, lower, own, transfer_slope, transfer_offset, transfer_gain)
        home = lax.all_to_all(packed.reshape(S, height, LANES), ("gz", "gx"), 0, 0, tiled=True)
        return call(
            unpack_kernel,
            [vmem],
            (shaped(3, zl, xl, yl), shaped(functions, 4, xl, yl)),
            ((yl, L),),
            table=table, chunk=chunk,
        )(home)

    return jax.shard_map(
        local,
        mesh=mesh,
        in_specs=(P("gz", "gx", "gy"), P("gz", "gx", "gy"), P(None, "gz", "gx", "gy"), P(), P(), P()),
        out_specs=(P(None, "gz", "gx", "gy"), P("gz", None, "gx", "gy")),
        check_vma=False,
    )
```

```python
import math

import jax
import jax.numpy as jnp
from jax import lax
from jax.experimental import pallas as pl
from jax.experimental.pallas import tpu as pltpu
from jax.sharding import PartitionSpec as P

ITERS = 4
HALO = ITERS + 1
FIELDS = 4
LANES = 128
LOG2E = math.log2(math.e)
F32 = jnp.float32


def snake(ngx, ngz):
    order = []
    for x in range(ngx):
        depths = range(ngz) if x % 2 == 0 else reversed(range(ngz))
        order.extend((x, z) for z in depths)
    return order


def chain_swaps(ngx, ngy, ngz, hop, odd):
    places = []
    order = snake(ngx, ngz)
    for y in range(ngy):
        for x, z in order if y % 2 == 0 else order[::-1]:
            places.append((x * ngy + y) * ngz + z)
    firsts = [i for i in range(len(places) - hop) if i // hop % 2 == odd]
    pairs = [(places[i], places[i + hop]) for i in firsts]
    return pairs + [(b, a) for a, b in pairs]


def chain_place(ngx, ngz):
    x, y, z = lax.axis_index("gx"), lax.axis_index("gy"), lax.axis_index("gz")
    within = x * ngz + jnp.where(x % 2 == 0, z, ngz - 1 - z)
    group = ngx * ngz
    return y * group + jnp.where(y % 2 == 0, within, group - 1 - within)


def roll(value, shift, axis):
    size = value.shape[axis]
    shift = shift % size
    return value if shift == 0 else pltpu.roll(value, shift, axis)


def owner(table, c):
    forward = lax.axis_index("gy") % 2 == 0
    return jnp.where(forward, table[c], table[len(table) - 1 - c])


def pack_kernel(phase_ref, thermal_ref, velocity_ref, out_ref, *, table, chunk):
    zl, xl, yl = thermal_ref.shape
    density = (1.0 + 9.0 * phase_ref[...].astype(F32)) * thermal_ref[...]
    for f in range(FIELDS):
        field = density if f == 0 else velocity_ref[f - 1]
        turned = field.reshape(zl * xl, yl).T
        for c in range(yl // chunk):
            rows = turned[c * chunk : (c + 1) * chunk]
            out_ref[owner(table, c), pl.ds(f, chunk, stride=FIELDS), :] = rows


class Shifts:
    def __init__(self, ngx, ngz, zl, xl):
        self.ngx, self.ngz, self.zl, self.xl = ngx, ngz, zl, xl
        shape = (1, ngx * ngz, zl * xl)
        lane = lax.broadcasted_iota(jnp.int32, shape, 2)
        sub = lax.broadcasted_iota(jnp.int32, shape, 1)
        z, x = lane // xl, lane % xl
        gz, gx = sub // ngx, sub % ngx
        self.z_first, self.z_last = z == 0, z == zl - 1
        self.x_first, self.x_last = x == 0, x == xl - 1
        self.z_low = self.z_first & (gz == 0)
        self.z_high = self.z_last & (gz == ngz - 1)
        self.x_low = self.x_first & (gx == 0)
        self.x_high = self.x_last & (gx == ngx - 1)

    def below_z(self, f):
        near = roll(f, self.xl, 2)
        return jnp.where(self.z_first, roll(near, self.ngx, 1), near)

    def above_z(self, f):
        near = roll(f, -self.xl, 2)
        return jnp.where(self.z_last, roll(near, -self.ngx, 1), near)

    def below_x(self, f):
        far = roll(roll(f, 1 - self.xl, 2), 1, 1)
        return jnp.where(self.x_first, far, roll(f, 1, 2))

    def above_x(self, f):
        far = roll(roll(f, self.xl - 1, 2), -1, 1)
        return jnp.where(self.x_last, far, roll(f, -1, 2))


def krylov_kernel(*refs, ngx, ngz, zl, xl, chunk, hops, margin, step):
    own_ref = refs[0]
    low_refs, high_refs = refs[1 : 1 + hops], refs[1 + hops : 1 + 2 * hops]
    basis_ref, lower_ref, sums_ref, dens, coef, vec, diag, source = refs[1 + 2 * hops :]
    S, L = ngx * ngz, zl * xl
    E = chunk + 2 * HALO
    move = Shifts(ngx, ngz, zl, xl)

    def plane(e, f):
        k = e - HALO
        if 0 <= k < chunk:
            return own_ref[pl.ds(k * FIELDS + f, S, stride=chunk * FIELDS), :]
        far = -k - 1 if k < 0 else k - chunk
        hop, at = far // chunk, far % chunk
        ref = low_refs[hop] if k < 0 else high_refs[hop]
        at = margin - 1 - at if k < 0 else at
        return ref[pl.ds(at * FIELDS + f, S, stride=margin * FIELDS), :]

    def planes(a, b, f):
        return jnp.stack([plane(e, f) for e in range(a, b)])

    def pieces(a, b):
        return [(i, min(i + step, b)) for i in range(a, b, step)]

    for e in range(E):
        dens[e] = plane(e, 0)
    for a, b in pieces(1, E - 1):
        d, before, after = dens[a:b], dens[a - 1 : b - 1], dens[a + 1 : b + 1]
        inside = d > 0.0
        d = jnp.where(inside, d, 1.0)

        def face(missing, other):
            return 2.0 / (d + jnp.where(missing, d, other))

        lz, uz = face(move.z_low, move.below_z(d)), face(move.z_high, move.above_z(d))
        lx, ux = face(move.x_low, move.below_x(d)), face(move.x_high, move.above_x(d))
        ly, uy = face(before <= 0.0, before), face(after <= 0.0, after)
        total = lz + uz + lx + ux + ly + uy
        inverse = jnp.where(inside, 1.0 / total, 0.0)
        coef[0, a:b] = jnp.where(move.z_low, 0.0, inverse * lz)
        coef[1, a:b] = jnp.where(move.z_high, 0.0, inverse * uz)
        coef[2, a:b] = jnp.where(move.x_low, 0.0, inverse * lx)
        coef[3, a:b] = jnp.where(move.x_high, 0.0, inverse * ux)
        coef[4, a:b] = inverse * ly
        coef[5, a:b] = inverse * uy
        vz, vx = planes(a, b, 1), planes(a, b, 2)
        rhs = -(jnp.where(move.z_high, 0.0, move.above_z(vz)) - vz)
        rhs = rhs - (jnp.where(move.x_high, 0.0, move.above_x(vx)) - vx)
        rhs = rhs - (planes(a + 1, b + 1, 3) - planes(a, b, 3))
        vec[0, a:b] = inverse * rhs
        for e in range(max(a, HALO), min(b, HALO + chunk)):
            diag[e - HALO] = total[e - a]
            source[e - HALO] = rhs[e - a]
            for k, faces in enumerate((lz, lx, ly)):
                lower_ref[k, e - HALO] = faces[e - a]

    def applied(k, a, b):
        f = vec[k, a:b]
        out = coef[0, a:b] * move.below_z(f) + coef[1, a:b] * move.above_z(f)
        out = out + (coef[2, a:b] * move.below_x(f) + coef[3, a:b] * move.above_x(f))
        return out + (coef[4, a:b] * vec[k, a - 1 : b - 1] + coef[5, a:b] * vec[k, a + 1 : b + 1])

    for k in range(1, ITERS):
        for a, b in pieces(1 + k, E - 1 - k):
            vec[k, a:b] = applied(k - 1, a, b)

    count = 2 * ITERS - 1
    powers = [0.0] * count
    firsts = [0.0] * ITERS
    steps = [0.0] * (count + 1)
    for a, b in pieces(HALO, HALO + chunk):
        own = slice(a - HALO, b - HALO)
        basis = [vec[k, a:b] for k in range(ITERS)]
        basis.append(applied(ITERS - 1, a, b))
        weight, right = diag[own], source[own]
        gaps = [basis[k] - basis[k + 1] for k in range(ITERS)]
        scaled = [weight * gap for gap in gaps]
        for k in range(count):
            powers[k] = powers[k] + jnp.sum(basis[(k + 1) // 2] * scaled[k // 2], axis=0)
        for k in range(ITERS):
            firsts[k] = firsts[k] + jnp.sum(right * basis[k], axis=0)
        ladder, level = [basis[0], gaps[0]], gaps
        while len(level) > 1:
            level = [level[i] - level[i + 1] for i in range(len(level) - 1)]
            ladder.append(level[0])
        for k in range(2, count + 1):
            steps[k] = steps[k] + jnp.sum(weight * ladder[k // 2] * ladder[(k + 1) // 2], axis=0)
    steps[0], steps[1] = firsts[0], powers[0]
    for k in range(ITERS):
        basis_ref[k] = vec[k, HALO - 1 : HALO + chunk]

    columns = powers + firsts + steps
    rows = [jnp.sum(c, axis=0, keepdims=True) for c in columns]
    high = -(-len(rows) // 8) * 8
    rows = rows + [jnp.zeros((1, L), F32)] * (high - len(rows))
    sums = jnp.sum(jnp.concatenate(rows, axis=0), axis=1, keepdims=True)
    lane = lax.broadcasted_iota(jnp.int32, (high, LANES), 1)
    row = lax.broadcasted_iota(jnp.int32, (high, LANES), 0)
    line = jnp.sum(jnp.where(lane == row, sums, 0.0), axis=0, keepdims=True)
    sums_ref[...] = jnp.broadcast_to(line, sums_ref.shape)


def galerkin(sums):
    n, count = ITERS, 2 * ITERS - 1
    line = jnp.sum(sums, axis=0, keepdims=True)
    lane = lax.broadcasted_iota(jnp.int32, line.shape, 1)

    def pick(k):
        return jnp.sum(jnp.where(lane == k, line, 0.0), axis=1, keepdims=True)

    powers = [pick(k) for k in range(count)]
    firsts = [pick(count + k) for k in range(n)]
    steps = [pick(count + n + k) for k in range(count + 1)]
    matrix = [jnp.concatenate([powers[k], steps[k + 1]], axis=0) for k in range(count)]
    right = [jnp.concatenate([firsts[k], steps[k]], axis=0) for k in range(n)]
    low = [[None] * n for _ in range(n)]
    scale = [None] * n
    quality = None
    for j in range(n):
        pivot = matrix[2 * j]
        for k in range(j):
            pivot = pivot - low[j][k] * low[j][k] * scale[k][0]
        share = pivot / matrix[2 * j]
        fine = share > 1e-7
        quality = jnp.where(fine, share, 0.0) if quality is None else jnp.minimum(quality, jnp.where(fine, share, 0.0))
        inverse = jnp.where(fine, 1.0 / pivot, 0.0)
        scale[j] = (pivot, inverse)
        for r in range(j + 1, n):
            entry = matrix[r + j]
            for k in range(j):
                entry = entry - low[r][k] * low[j][k] * scale[k][0]
            low[r][j] = entry * inverse
    part = list(right)
    for r in range(n):
        for k in range(r):
            part[r] = part[r] - low[r][k] * part[k]
    part = [part[r] * scale[r][1] for r in range(n)]
    for r in reversed(range(n)):
        for k in range(r + 1, n):
            part[r] = part[r] - low[k][r] * part[k]
    first = quality[0:1] >= quality[1:2]
    by_power = [jnp.where(first, p[0:1], 0.0) for p in part]
    by_step = [jnp.where(first, 0.0, p[1:2]) for p in part]
    return by_power, by_step


def render_kernel(
    sums_ref, basis_ref, lower_ref, own_ref, slope_ref, offset_ref, gain_ref, out_ref, press, flat, turned,
    *, ngx, ngz, zl, xl, chunk, step
):
    S, L = ngx * ngz, zl * xl
    yl = S * chunk
    height = out_ref.shape[0] // S
    move = Shifts(ngx, ngz, zl, xl)
    by_power, by_step = galerkin(sums_ref[...])
    by_power = [v.reshape(1, 1, 1) for v in by_power]
    by_step = [v.reshape(1, 1, 1) for v in by_step]
    for a in range(0, chunk + 1, step):
        b = min(a + step, chunk + 1)
        level = [basis_ref[k, a:b] for k in range(ITERS)]
        value = 0.0
        for k in range(ITERS):
            value = value + by_power[k] * level[k]
        value = value + by_step[0] * level[0]
        for k in range(1, ITERS):
            level = [level[i] - level[i + 1] for i in range(len(level) - 1)]
            value = value + by_step[k] * level[0]
        press[a:b] = value
    for a in range(0, chunk, step):
        b = min(a + step, chunk)
        p = press[a + 1 : b + 1]
        fronts = (
            jnp.where(move.z_low, 0.0, move.below_z(p)),
            jnp.where(move.x_low, 0.0, move.below_x(p)),
            press[a:b],
        )
        scalar = None
        for k, front in enumerate(fronts):
            v = jnp.stack([own_ref[pl.ds(c * FIELDS + k + 1, S, stride=chunk * FIELDS), :] for c in range(a, b)])
            corrected = v - lower_ref[k, a:b] * (p - front)
            for c in range(a, b):
                out_ref[pl.ds(k * chunk + c, S, stride=height), :] = corrected[c - a]
            scalar = corrected if scalar is None else scalar + corrected
        for c in range(a, b):
            flat[pl.ds(c, S, stride=chunk), :] = scalar[c - a]
    turned[...] = flat[...].T.reshape(zl, xl, yl)

    group = ngx * chunk
    functions = slope_ref.shape[1] // ngz
    depth = zl * ngz
    lane = lax.broadcasted_iota(jnp.int32, (xl, yl), 1)

    def owned(i, carry):
        images = [jnp.zeros((xl, LANES), F32) for _ in range(ngx)]
        for t in range(functions):
            index = i * functions + t
            rates = [-LOG2E * slope_ref[c, index] for c in range(4)]
            bases = [-LOG2E * offset_ref[c, index] for c in range(4)]
            gain = gain_ref[index] / depth
            through = jnp.ones((xl, yl), F32)
            colors = [jnp.zeros((xl, yl), F32) for _ in range(3)]
            for z in range(zl):
                x = turned[z]
                curves = [1.0 / (1.0 + jnp.exp2(rates[c] * x + bases[c])) for c in range(4)]
                opacity = gain * curves[3]
                weight = through * opacity
                colors = [colors[c] + weight * curves[c] for c in range(3)]
                through = through * (1.0 - opacity)
            planes = list(colors)
            everything = through
            for _ in range(ngz - 1):
                planes = [colors[c] + through * roll(planes[c], -group, 1) for c in range(3)]
                everything = through * roll(everything, -group, 1)
            planes.append(1.0 - everything)
            for c, image in enumerate(planes):
                start = (t * 4 + c) * chunk
                here = (lane >= start) & (lane < start + chunk)
                for k in range(ngx):
                    images[k] = jnp.where(here, roll(image, start - k * chunk, 1), images[k])
        for k in range(ngx):
            place = pl.multiple_of((i * ngx + k) * height + 3 * chunk, 2)
            out_ref[pl.ds(place, xl), :] = images[k]
        return carry

    lax.fori_loop(0, ngz, owned, 0)


def unpack_kernel(in_ref, corrected_ref, images_ref, flat, *, table, chunk):
    zl, xl, yl = corrected_ref.shape[1:]
    functions = images_ref.shape[0]
    pieces = yl // chunk
    for f in range(3):
        for c in range(pieces):
            flat[c * chunk : (c + 1) * chunk, :] = in_ref[owner(table, c), f * chunk : (f + 1) * chunk, :]
        corrected_ref[f] = flat[...].T.reshape(zl, xl, yl)
    lane = lax.broadcasted_iota(jnp.int32, (xl, yl), 1)
    images = [jnp.zeros((xl, yl), F32) for _ in range(functions * 4)]
    for c in range(pieces):
        source = in_ref[owner(table, c), 3 * chunk : 3 * chunk + xl, :]
        here = (lane >= c * chunk) & (lane < (c + 1) * chunk)
        images = [jnp.where(here, roll(source, (c - k) * chunk, 1), image) for k, image in enumerate(images)]
    for k, image in enumerate(images):
        images_ref[k // 4, k % 4] = image


def solution(mesh):
    ngx, ngy, ngz = mesh.shape["gx"], mesh.shape["gy"], mesh.shape["gz"]
    S, devices = ngx * ngz, ngx * ngy * ngz
    table = [z * ngx + x for x, z in snake(ngx, ngz)]

    def local(phase_field, thermal, velocity, transfer_slope, transfer_offset, transfer_gain):
        zl, xl, yl = thermal.shape
        L, chunk = zl * xl, yl // S
        functions = transfer_slope.shape[0] // ngz
        assert yl % S == 0 and L == LANES and yl == LANES and functions * 4 * chunk <= LANES
        hops = -(-HALO // chunk)
        margin = min(chunk, HALO + HALO % 2)
        step = max(1, 4 * 8 // S)

        vmem, smem = (pl.BlockSpec(memory_space=space) for space in (pltpu.VMEM, pltpu.SMEM))

        def call(body, specs, out, scratch=(), **kwargs):
            kernel = pl.pallas_call(
                lambda *refs: body(*refs, **kwargs),
                in_specs=specs,
                out_specs=jax.tree.map(lambda _: vmem, out),
                out_shape=out,
                scratch_shapes=[pltpu.VMEM(s, F32) for s in scratch],
                name=body.__name__,
            )

            def run(*args):
                return kernel(*[near(a) if spec is vmem else a for a, spec in zip(args, specs)])

            return run

        def near(array):
            return pltpu.with_memory_space_constraint(array, pltpu.VMEM)

        def shaped(*shape):
            return jax.ShapeDtypeStruct(shape, F32)

        def placed(*shape):
            return pltpu.VMEM(shape, F32)

        free = pl.BlockSpec()
        blocks = call(pack_kernel, [free] * 3, placed(S, chunk * FIELDS, L), table=table, chunk=chunk)(
            phase_field, thermal, velocity
        )
        pencils = lax.all_to_all(blocks, ("gz", "gx"), 0, 0, tiled=True)
        first = pencils[:, : margin * FIELDS]
        last = pencils[:, (chunk - margin) * FIELDS :]
        every = ("gx", "gy", "gz")
        place = chain_place(ngx, ngz)
        lows, highs = [], []
        for hop in range(1, hops + 1):
            even = place // hop % 2 == 0
            ahead = lax.ppermute(jnp.where(even, last, first), every, chain_swaps(ngx, ngy, ngz, hop, 0))
            behind = lax.ppermute(jnp.where(even, first, last), every, chain_swaps(ngx, ngy, ngz, hop, 1))
            lows.append(jnp.where(even, behind, ahead))
            highs.append(jnp.where(even, ahead, behind))
        own = pencils.reshape(-1, L)
        wide = chunk + 2 * HALO
        basis, lower, sums = call(
            krylov_kernel,
            [vmem] * (1 + 2 * hops),
            (placed(ITERS, chunk + 1, S, L), placed(3, chunk, S, L), placed(devices, LANES)),
            ((wide, S, L), (6, wide, S, L), (ITERS, wide, S, L), (chunk, S, L), (chunk, S, L)),
            ngx=ngx, ngz=ngz, zl=zl, xl=xl, chunk=chunk, hops=hops, margin=margin, step=step,
        )(own, *[v.reshape(-1, L) for v in lows + highs])
        sums = lax.all_to_all(sums, every, 0, 0, tiled=True)
        height = 3 * chunk + xl
        height += -height % 8
        packed = call(
            render_kernel,
            [vmem] * 4 + [smem] * 3,
            placed(S * height, LANES),
            ((chunk + 1, S, L), (yl, L), (zl, xl, yl)),
            ngx=ngx, ngz=ngz, zl=zl, xl=xl, chunk=chunk, step=step,
        )(sums, basis, lower, own, transfer_slope.T, transfer_offset.T, transfer_gain)
        home = lax.all_to_all(packed.reshape(S, height, LANES), ("gz", "gx"), 0, 0, tiled=True)
        return call(
            unpack_kernel,
            [vmem],
            (shaped(3, zl, xl, yl), shaped(functions, 4, xl, yl)),
            ((yl, L),),
            table=table, chunk=chunk,
        )(home)

    return jax.shard_map(
        local,
        mesh=mesh,
        in_specs=(P("gz", "gx", "gy"), P("gz", "gx", "gy"), P(None, "gz", "gx", "gy"), P(), P(), P()),
        out_specs=(P(None, "gz", "gx", "gy"), P("gz", None, "gx", "gy")),
        check_vma=False,
    )
```

```python
import math

import jax
import jax.numpy as jnp
from jax import lax
from jax.experimental import pallas as pl
from jax.experimental.pallas import tpu as pltpu
from jax.sharding import PartitionSpec as P

ITERS = 4
HALO = ITERS + 1
FIELDS = 4
LANES = 128
LOG2E = math.log2(math.e)
F32 = jnp.float32


def snake(ngx, ngz):
    order = []
    for x in range(ngx):
        depths = range(ngz) if x % 2 == 0 else reversed(range(ngz))
        order.extend((x, z) for z in depths)
    return order


def chain_swaps(ngx, ngy, ngz, hop, odd):
    places = []
    order = snake(ngx, ngz)
    for y in range(ngy):
        for x, z in order if y % 2 == 0 else order[::-1]:
            places.append((x * ngy + y) * ngz + z)
    firsts = [i for i in range(len(places) - hop) if i // hop % 2 == odd]
    pairs = [(places[i], places[i + hop]) for i in firsts]
    return pairs + [(b, a) for a, b in pairs]


def chain_place(ngx, ngz):
    x, y, z = lax.axis_index("gx"), lax.axis_index("gy"), lax.axis_index("gz")
    within = x * ngz + jnp.where(x % 2 == 0, z, ngz - 1 - z)
    group = ngx * ngz
    return y * group + jnp.where(y % 2 == 0, within, group - 1 - within)


def roll(value, shift, axis):
    size = value.shape[axis]
    shift = shift % size
    return value if shift == 0 else pltpu.roll(value, shift, axis)


def owner(table, c):
    forward = lax.axis_index("gy") % 2 == 0
    return jnp.where(forward, table[c], table[len(table) - 1 - c])


def pack_kernel(phase_ref, thermal_ref, velocity_ref, slope_ref, offset_ref, gain_ref, out_ref, curves_ref, *, table, chunk, depth):
    zl, xl, yl = thermal_ref.shape
    density = (1.0 + 9.0 * phase_ref[...].astype(F32)) * thermal_ref[...]
    for f in range(FIELDS):
        field = density if f == 0 else velocity_ref[f - 1]
        turned = field.reshape(zl * xl, yl).T
        for c in range(yl // chunk):
            rows = turned[c * chunk : (c + 1) * chunk]
            out_ref[owner(table, c), pl.ds(f, chunk, stride=FIELDS), :] = rows
    for t in range(curves_ref.shape[0]):
        curves_ref[t, 0:4, :] = jnp.broadcast_to(-LOG2E * slope_ref[:, t : t + 1], (4, LANES))
        curves_ref[t, 4:8, :] = jnp.broadcast_to(-LOG2E * offset_ref[:, t : t + 1], (4, LANES))
        curves_ref[t, 8:9, :] = jnp.broadcast_to(gain_ref[:, t : t + 1] / depth, (1, LANES))


def even_place(ngx, ngz, hop):
    return chain_place(ngx, ngz) // hop % 2 == 0


def edges_kernel(own_ref, *out_refs, ngx, ngz, rows):
    for h in range(len(out_refs) // 2):
        high = own_ref.shape[1] - rows
        even = even_place(ngx, ngz, h + 1)
        for ref, start in zip(out_refs[2 * h : 2 * h + 2], (jnp.where(even, high, 0), jnp.where(even, 0, high))):
            ref[...] = own_ref[:, pl.ds(pl.multiple_of(start, 8), rows), :]


class Shifts:
    def __init__(self, ngx, ngz, zl, xl):
        self.ngx, self.ngz, self.zl, self.xl = ngx, ngz, zl, xl
        shape = (1, ngx * ngz, zl * xl)
        lane = lax.broadcasted_iota(jnp.int32, shape, 2)
        sub = lax.broadcasted_iota(jnp.int32, shape, 1)
        z, x = lane // xl, lane % xl
        gz, gx = sub // ngx, sub % ngx
        self.z_first, self.z_last = z == 0, z == zl - 1
        self.x_first, self.x_last = x == 0, x == xl - 1
        self.z_low = self.z_first & (gz == 0)
        self.z_high = self.z_last & (gz == ngz - 1)
        self.x_low = self.x_first & (gx == 0)
        self.x_high = self.x_last & (gx == ngx - 1)

    def below_z(self, f):
        near = roll(f, self.xl, 2)
        return jnp.where(self.z_first, roll(near, self.ngx, 1), near)

    def above_z(self, f):
        near = roll(f, -self.xl, 2)
        return jnp.where(self.z_last, roll(near, -self.ngx, 1), near)

    def below_x(self, f):
        far = roll(roll(f, 1 - self.xl, 2), 1, 1)
        return jnp.where(self.x_first, far, roll(f, 1, 2))

    def above_x(self, f):
        far = roll(roll(f, self.xl - 1, 2), -1, 1)
        return jnp.where(self.x_last, far, roll(f, -1, 2))


def krylov_kernel(*refs, ngx, ngz, zl, xl, chunk, hops, margin, step):
    own_ref, swapped = refs[0], refs[1 : 1 + 2 * hops]
    basis_ref, lower_ref, sums_ref, lows, highs, dens, coef, vec, diag, source = refs[1 + 2 * hops :]
    for h in range(hops):
        ahead_ref, behind_ref = swapped[2 * h : 2 * h + 2]
        even = even_place(ngx, ngz, h + 1)

        @pl.when(even)
        def _():
            lows[h], highs[h] = behind_ref[...], ahead_ref[...]

        @pl.when(jnp.logical_not(even))
        def _():
            lows[h], highs[h] = ahead_ref[...], behind_ref[...]

    S, L = ngx * ngz, zl * xl
    E = chunk + 2 * HALO
    move = Shifts(ngx, ngz, zl, xl)

    def plane(e, f):
        k = e - HALO
        if 0 <= k < chunk:
            return own_ref[pl.ds(k * FIELDS + f, S, stride=chunk * FIELDS), :]
        far = -k - 1 if k < 0 else k - chunk
        hop, at = far // chunk, far % chunk
        ref = lows if k < 0 else highs
        at = margin - 1 - at if k < 0 else at
        return ref[hop, pl.ds(at * FIELDS + f, S, stride=margin * FIELDS), :]

    def planes(a, b, f):
        return jnp.stack([plane(e, f) for e in range(a, b)])

    def pieces(a, b):
        return [(i, min(i + step, b)) for i in range(a, b, step)]

    for e in range(E):
        dens[e] = plane(e, 0)
    for a, b in pieces(1, E - 1):
        d, before, after = dens[a:b], dens[a - 1 : b - 1], dens[a + 1 : b + 1]
        inside = d > 0.0
        d = jnp.where(inside, d, 1.0)

        def face(missing, other):
            return 2.0 / (d + jnp.where(missing, d, other))

        lz, uz = face(move.z_low, move.below_z(d)), face(move.z_high, move.above_z(d))
        lx, ux = face(move.x_low, move.below_x(d)), face(move.x_high, move.above_x(d))
        ly, uy = face(before <= 0.0, before), face(after <= 0.0, after)
        total = lz + uz + lx + ux + ly + uy
        inverse = jnp.where(inside, 1.0 / total, 0.0)
        coef[0, a:b] = jnp.where(move.z_low, 0.0, inverse * lz)
        coef[1, a:b] = jnp.where(move.z_high, 0.0, inverse * uz)
        coef[2, a:b] = jnp.where(move.x_low, 0.0, inverse * lx)
        coef[3, a:b] = jnp.where(move.x_high, 0.0, inverse * ux)
        coef[4, a:b] = inverse * ly
        coef[5, a:b] = inverse * uy
        vz, vx = planes(a, b, 1), planes(a, b, 2)
        rhs = -(jnp.where(move.z_high, 0.0, move.above_z(vz)) - vz)
        rhs = rhs - (jnp.where(move.x_high, 0.0, move.above_x(vx)) - vx)
        rhs = rhs - (planes(a + 1, b + 1, 3) - planes(a, b, 3))
        vec[0, a:b] = inverse * rhs
        for e in range(max(a, HALO), min(b, HALO + chunk)):
            diag[e - HALO] = total[e - a]
            source[e - HALO] = rhs[e - a]
            for k, faces in enumerate((lz, lx, ly)):
                lower_ref[k, e - HALO] = faces[e - a]

    def applied(k, a, b):
        f = vec[k, a:b]
        out = coef[0, a:b] * move.below_z(f) + coef[1, a:b] * move.above_z(f)
        out = out + (coef[2, a:b] * move.below_x(f) + coef[3, a:b] * move.above_x(f))
        return out + (coef[4, a:b] * vec[k, a - 1 : b - 1] + coef[5, a:b] * vec[k, a + 1 : b + 1])

    for k in range(1, ITERS):
        for a, b in pieces(1 + k, E - 1 - k):
            vec[k, a:b] = applied(k - 1, a, b)

    count = 2 * ITERS - 1
    powers = [0.0] * count
    firsts = [0.0] * ITERS
    steps = [0.0] * (count + 1)
    for a, b in pieces(HALO, HALO + chunk):
        own = slice(a - HALO, b - HALO)
        basis = [vec[k, a:b] for k in range(ITERS)]
        basis.append(applied(ITERS - 1, a, b))
        weight, right = diag[own], source[own]
        gaps = [basis[k] - basis[k + 1] for k in range(ITERS)]
        scaled = [weight * gap for gap in gaps]
        for k in range(count):
            powers[k] = powers[k] + jnp.sum(basis[(k + 1) // 2] * scaled[k // 2], axis=0)
        for k in range(ITERS):
            firsts[k] = firsts[k] + jnp.sum(right * basis[k], axis=0)
        ladder, level = [basis[0], gaps[0]], gaps
        while len(level) > 1:
            level = [level[i] - level[i + 1] for i in range(len(level) - 1)]
            ladder.append(level[0])
        for k in range(2, count + 1):
            steps[k] = steps[k] + jnp.sum(weight * ladder[k // 2] * ladder[(k + 1) // 2], axis=0)
    steps[0], steps[1] = firsts[0], powers[0]
    for k in range(ITERS):
        basis_ref[k] = vec[k, HALO - 1 : HALO + chunk]

    columns = powers + firsts + steps
    rows = [jnp.sum(c, axis=0, keepdims=True) for c in columns]
    high = -(-len(rows) // 8) * 8
    rows = rows + [jnp.zeros((1, L), F32)] * (high - len(rows))
    sums = jnp.sum(jnp.concatenate(rows, axis=0), axis=1, keepdims=True)
    lane = lax.broadcasted_iota(jnp.int32, (high, LANES), 1)
    row = lax.broadcasted_iota(jnp.int32, (high, LANES), 0)
    line = jnp.sum(jnp.where(lane == row, sums, 0.0), axis=0, keepdims=True)
    sums_ref[...] = jnp.broadcast_to(line, sums_ref.shape)


def galerkin(sums):
    n, count = ITERS, 2 * ITERS - 1
    line = jnp.sum(sums, axis=0, keepdims=True)
    lane = lax.broadcasted_iota(jnp.int32, line.shape, 1)

    def pick(k):
        return jnp.sum(jnp.where(lane == k, line, 0.0), axis=1, keepdims=True)

    powers = [pick(k) for k in range(count)]
    firsts = [pick(count + k) for k in range(n)]
    steps = [pick(count + n + k) for k in range(count + 1)]
    matrix = [jnp.concatenate([powers[k], steps[k + 1]], axis=0) for k in range(count)]
    right = [jnp.concatenate([firsts[k], steps[k]], axis=0) for k in range(n)]
    low = [[None] * n for _ in range(n)]
    scale = [None] * n
    quality = None
    for j in range(n):
        pivot = matrix[2 * j]
        for k in range(j):
            pivot = pivot - low[j][k] * low[j][k] * scale[k][0]
        share = pivot / matrix[2 * j]
        fine = share > 1e-7
        quality = jnp.where(fine, share, 0.0) if quality is None else jnp.minimum(quality, jnp.where(fine, share, 0.0))
        inverse = jnp.where(fine, 1.0 / pivot, 0.0)
        scale[j] = (pivot, inverse)
        for r in range(j + 1, n):
            entry = matrix[r + j]
            for k in range(j):
                entry = entry - low[r][k] * low[j][k] * scale[k][0]
            low[r][j] = entry * inverse
    part = list(right)
    for r in range(n):
        for k in range(r):
            part[r] = part[r] - low[r][k] * part[k]
    part = [part[r] * scale[r][1] for r in range(n)]
    for r in reversed(range(n)):
        for k in range(r + 1, n):
            part[r] = part[r] - low[k][r] * part[k]
    first = quality[0:1] >= quality[1:2]
    by_power = [jnp.where(first, p[0:1], 0.0) for p in part]
    by_step = [jnp.where(first, 0.0, p[1:2]) for p in part]
    return by_power, by_step


def render_kernel(
    sums_ref, basis_ref, lower_ref, own_ref, table_ref, out_ref, press, flat, turned,
    *, ngx, ngz, zl, xl, chunk, step
):
    S, L = ngx * ngz, zl * xl
    yl = S * chunk
    height = out_ref.shape[0] // S
    move = Shifts(ngx, ngz, zl, xl)
    by_power, by_step = galerkin(sums_ref[...])
    by_power = [v.reshape(1, 1, 1) for v in by_power]
    by_step = [v.reshape(1, 1, 1) for v in by_step]
    for a in range(0, chunk + 1, step):
        b = min(a + step, chunk + 1)
        level = [basis_ref[k, a:b] for k in range(ITERS)]
        value = 0.0
        for k in range(ITERS):
            value = value + by_power[k] * level[k]
        value = value + by_step[0] * level[0]
        for k in range(1, ITERS):
            level = [level[i] - level[i + 1] for i in range(len(level) - 1)]
            value = value + by_step[k] * level[0]
        press[a:b] = value
    for a in range(0, chunk, step):
        b = min(a + step, chunk)
        p = press[a + 1 : b + 1]
        fronts = (
            jnp.where(move.z_low, 0.0, move.below_z(p)),
            jnp.where(move.x_low, 0.0, move.below_x(p)),
            press[a:b],
        )
        scalar = None
        for k, front in enumerate(fronts):
            v = jnp.stack([own_ref[pl.ds(c * FIELDS + k + 1, S, stride=chunk * FIELDS), :] for c in range(a, b)])
            corrected = v - lower_ref[k, a:b] * (p - front)
            for c in range(a, b):
                out_ref[pl.ds(k * chunk + c, S, stride=height), :] = corrected[c - a]
            scalar = corrected if scalar is None else scalar + corrected
        for c in range(a, b):
            flat[pl.ds(c, S, stride=chunk), :] = scalar[c - a]
    turned[...] = flat[...].T.reshape(zl, xl, yl)

    group = ngx * chunk
    functions = table_ref.shape[0] // ngz
    lane = lax.broadcasted_iota(jnp.int32, (xl, yl), 1)

    def owned(i, carry):
        images = [jnp.zeros((xl, LANES), F32) for _ in range(ngx)]
        for t in range(functions):
            index = i * functions + t
            rows = [jnp.broadcast_to(table_ref[index, r : r + 1, :], (xl, yl)) for r in range(9)]
            rates, bases, gain = rows[:4], rows[4:8], rows[8]
            through = jnp.ones((xl, yl), F32)
            colors = [jnp.zeros((xl, yl), F32) for _ in range(3)]
            for z in range(zl):
                x = turned[z]
                curves = [1.0 / (1.0 + jnp.exp2(rates[c] * x + bases[c])) for c in range(4)]
                opacity = gain * curves[3]
                weight = through * opacity
                colors = [colors[c] + weight * curves[c] for c in range(3)]
                through = through * (1.0 - opacity)
            planes = list(colors)
            everything = through
            for _ in range(ngz - 1):
                planes = [colors[c] + through * roll(planes[c], -group, 1) for c in range(3)]
                everything = through * roll(everything, -group, 1)
            planes.append(1.0 - everything)
            for c, image in enumerate(planes):
                start = (t * 4 + c) * chunk
                here = (lane >= start) & (lane < start + chunk)
                for k in range(ngx):
                    images[k] = jnp.where(here, roll(image, start - k * chunk, 1), images[k])
        for k in range(ngx):
            place = pl.multiple_of((i * ngx + k) * height + 3 * chunk, 2)
            out_ref[pl.ds(place, xl), :] = images[k]
        return carry

    lax.fori_loop(0, ngz, owned, 0)


def unpack_kernel(in_ref, corrected_ref, images_ref, flat, *, table, chunk):
    zl, xl, yl = corrected_ref.shape[1:]
    functions = images_ref.shape[0]
    pieces = yl // chunk
    for f in range(3):
        for c in range(pieces):
            flat[c * chunk : (c + 1) * chunk, :] = in_ref[owner(table, c), f * chunk : (f + 1) * chunk, :]
        corrected_ref[f] = flat[...].T.reshape(zl, xl, yl)
    lane = lax.broadcasted_iota(jnp.int32, (xl, yl), 1)
    images = [jnp.zeros((xl, yl), F32) for _ in range(functions * 4)]
    for c in range(pieces):
        source = in_ref[owner(table, c), 3 * chunk : 3 * chunk + xl, :]
        here = (lane >= c * chunk) & (lane < (c + 1) * chunk)
        images = [jnp.where(here, roll(source, (c - k) * chunk, 1), image) for k, image in enumerate(images)]
    for k, image in enumerate(images):
        images_ref[k // 4, k % 4] = image


def solution(mesh):
    ngx, ngy, ngz = mesh.shape["gx"], mesh.shape["gy"], mesh.shape["gz"]
    S, devices = ngx * ngz, ngx * ngy * ngz
    table = [z * ngx + x for x, z in snake(ngx, ngz)]

    def local(phase_field, thermal, velocity, transfer_slope, transfer_offset, transfer_gain):
        zl, xl, yl = thermal.shape
        L, chunk = zl * xl, yl // S
        functions = transfer_slope.shape[0] // ngz
        assert yl % S == 0 and L == LANES and yl == LANES and functions * 4 * chunk <= LANES
        hops = -(-HALO // chunk)
        margin = min(chunk, HALO + HALO % 2)
        step = max(1, 4 * 8 // S)

        vmem = pl.BlockSpec(memory_space=pltpu.VMEM)

        def call(body, specs, out, scratch=(), **kwargs):
            kernel = pl.pallas_call(
                lambda *refs: body(*refs, **kwargs),
                in_specs=specs,
                out_specs=jax.tree.map(lambda _: vmem, out),
                out_shape=out,
                scratch_shapes=[pltpu.VMEM(s, F32) for s in scratch],
                name=body.__name__,
            )

            def run(*args):
                return kernel(*[near(a) if spec is vmem else a for a, spec in zip(args, specs)])

            return run

        def near(array):
            return pltpu.with_memory_space_constraint(array, pltpu.VMEM)

        def shaped(*shape):
            return jax.ShapeDtypeStruct(shape, F32)

        def placed(*shape):
            return pltpu.VMEM(shape, F32)

        free = pl.BlockSpec()
        tables = (transfer_slope.T, transfer_offset.T, transfer_gain[None, :])
        blocks, curves = call(
            pack_kernel,
            [free] * 6,
            (placed(S, chunk * FIELDS, L), placed(transfer_gain.shape[0], 16, LANES)),
            table=table, chunk=chunk, depth=zl * ngz,
        )(phase_field, thermal, velocity, *tables)
        pencils = lax.all_to_all(blocks, ("gz", "gx"), 0, 0, tiled=True)
        every = ("gx", "gy", "gz")
        messages = call(
            edges_kernel,
            [vmem],
            [placed(S, margin * FIELDS, L)] * (2 * hops),
            ngx=ngx, ngz=ngz, rows=margin * FIELDS,
        )(pencils)
        swapped = [
            lax.ppermute(message, every, chain_swaps(ngx, ngy, ngz, i // 2 + 1, i % 2)).reshape(-1, L)
            for i, message in enumerate(messages)
        ]
        own = pencils.reshape(-1, L)
        wide = chunk + 2 * HALO
        basis, lower, sums = call(
            krylov_kernel,
            [vmem] * (1 + 2 * hops),
            (placed(ITERS, chunk + 1, S, L), placed(3, chunk, S, L), placed(devices, LANES)),
            ((hops, S * margin * FIELDS, L),) * 2 + ((wide, S, L), (6, wide, S, L), (ITERS, wide, S, L), (chunk, S, L), (chunk, S, L)),
            ngx=ngx, ngz=ngz, zl=zl, xl=xl, chunk=chunk, hops=hops, margin=margin, step=step,
        )(own, *swapped)
        sums = lax.all_to_all(sums, every, 0, 0, tiled=True)
        height = 3 * chunk + xl
        height += -height % 8
        packed = call(
            render_kernel,
            [vmem] * 5,
            placed(S * height, LANES),
            ((chunk + 1, S, L), (yl, L), (zl, xl, yl)),
            ngx=ngx, ngz=ngz, zl=zl, xl=xl, chunk=chunk, step=step,
        )(sums, basis, lower, own, curves)
        home = lax.all_to_all(packed.reshape(S, height, LANES), ("gz", "gx"), 0, 0, tiled=True)
        return call(
            unpack_kernel,
            [vmem],
            (shaped(3, zl, xl, yl), shaped(functions, 4, xl, yl)),
            ((yl, L),),
            table=table, chunk=chunk,
        )(home)

    return jax.shard_map(
        local,
        mesh=mesh,
        in_specs=(P("gz", "gx", "gy"), P("gz", "gx", "gy"), P(None, "gz", "gx", "gy"), P(), P(), P()),
        out_specs=(P(None, "gz", "gx", "gy"), P("gz", None, "gx", "gy")),
        check_vma=False,
    )
```

```python
import math

import jax
import jax.numpy as jnp
from jax import lax
from jax.experimental import pallas as pl
from jax.experimental.pallas import tpu as pltpu
from jax.sharding import PartitionSpec as P

ITERS = 4
HALO = ITERS + 1
FIELDS = 4
LANES = 128
LOG2E = math.log2(math.e)
F32 = jnp.float32


def snake(ngx, ngz):
    order = []
    for x in range(ngx):
        depths = range(ngz) if x % 2 == 0 else reversed(range(ngz))
        order.extend((x, z) for z in depths)
    return order


def chain(ngx, ngy, ngz):
    places = []
    order = snake(ngx, ngz)
    for y in range(ngy):
        for x, z in order if y % 2 == 0 else order[::-1]:
            places.append((x * ngy + y) * ngz + z)
    return places


def both_ways(places, pairs):
    pairs = [(places[a], places[b]) for a, b in pairs]
    return pairs + [(b, a) for a, b in pairs]


def hop_swaps(places, hop, odd):
    return both_ways(places, [(i, i + hop) for i in range(len(places) - hop) if i // hop % 2 == odd])


def run_swaps(places, run, start):
    pairs, rest = [], list(range(start))
    while start + run <= len(places):
        pairs.append((start, start + run - 1))
        pairs.extend((i, i + 1) for i in range(start + 1, start + run - 1, 2))
        start += run
    rest.extend(range(start, len(places)))
    pairs.extend((i, i + 1) for i in rest if i % 2 == 0)
    return both_ways(places, pairs)


def chain_place(ngx, ngz):
    x, y, z = lax.axis_index("gx"), lax.axis_index("gy"), lax.axis_index("gz")
    within = x * ngz + jnp.where(x % 2 == 0, z, ngz - 1 - z)
    group = ngx * ngz
    return y * group + jnp.where(y % 2 == 0, within, group - 1 - within)


def roll(value, shift, axis):
    size = value.shape[axis]
    shift = shift % size
    return value if shift == 0 else pltpu.roll(value, shift, axis)


def owner(table, c):
    forward = lax.axis_index("gy") % 2 == 0
    return jnp.where(forward, table[c], table[len(table) - 1 - c])


def pack_kernel(phase_ref, thermal_ref, velocity_ref, slope_ref, offset_ref, gain_ref, out_ref, curves_ref, *, table, chunk, depth):
    zl, xl, yl = thermal_ref.shape
    density = (1.0 + 9.0 * phase_ref[...].astype(F32)) * thermal_ref[...]
    for f in range(FIELDS):
        field = density if f == 0 else velocity_ref[f - 1]
        turned = field.reshape(zl * xl, yl).T
        for c in range(yl // chunk):
            rows = turned[c * chunk : (c + 1) * chunk]
            out_ref[owner(table, c), pl.ds(f, chunk, stride=FIELDS), :] = rows
    for t in range(curves_ref.shape[0]):
        curves_ref[t, 0:4, :] = jnp.broadcast_to(-LOG2E * slope_ref[:, t : t + 1], (4, LANES))
        curves_ref[t, 4:8, :] = jnp.broadcast_to(-LOG2E * offset_ref[:, t : t + 1], (4, LANES))
        curves_ref[t, 8:9, :] = jnp.broadcast_to(gain_ref[:, t : t + 1] / depth, (1, LANES))


def even_place(ngx, ngz, hop):
    return chain_place(ngx, ngz) // hop % 2 == 0


class Shifts:
    def __init__(self, ngx, ngz, zl, xl):
        self.ngx, self.ngz, self.zl, self.xl = ngx, ngz, zl, xl
        shape = (1, ngx * ngz, zl * xl)
        lane = lax.broadcasted_iota(jnp.int32, shape, 2)
        sub = lax.broadcasted_iota(jnp.int32, shape, 1)
        z, x = lane // xl, lane % xl
        gz, gx = sub // ngx, sub % ngx
        self.z_first, self.z_last = z == 0, z == zl - 1
        self.x_first, self.x_last = x == 0, x == xl - 1
        self.z_low = self.z_first & (gz == 0)
        self.z_high = self.z_last & (gz == ngz - 1)
        self.x_low = self.x_first & (gx == 0)
        self.x_high = self.x_last & (gx == ngx - 1)

    def below_z(self, f):
        near = roll(f, self.xl, 2)
        return jnp.where(self.z_first, roll(near, self.ngx, 1), near)

    def above_z(self, f):
        near = roll(f, -self.xl, 2)
        return jnp.where(self.z_last, roll(near, -self.ngx, 1), near)

    def below_x(self, f):
        far = roll(roll(f, 1 - self.xl, 2), 1, 1)
        return jnp.where(self.x_first, far, roll(f, 1, 2))

    def above_x(self, f):
        far = roll(roll(f, self.xl - 1, 2), -1, 1)
        return jnp.where(self.x_last, far, roll(f, -1, 2))


def divergence(move, velocity, after):
    vz, vx, vy = velocity
    out = -(jnp.where(move.z_high, 0.0, move.above_z(vz)) - vz)
    out = out - (jnp.where(move.x_high, 0.0, move.above_x(vx)) - vx)
    return out + vy if after is None else out - (after - vy)


def column_reader(own_ref, S, chunk):
    def read(k, f):
        return own_ref[pl.ds(k * FIELDS + f, S, stride=chunk * FIELDS), :][None]

    return read


def column(move, read, k, chunk):
    velocity = [read(k, f) for f in (1, 2, 3)]
    return velocity, divergence(move, velocity, read(k + 1, 3) if k + 1 < chunk else None)


def edges_kernel(own_ref, *out_refs, ngx, ngz, zl, xl, chunk, margin):
    move = Shifts(ngx, ngz, zl, xl)
    read = column_reader(own_ref, ngx * ngz, chunk)
    messages = []
    for start in (0, chunk - margin):
        planes = [read(k, 0) for k in range(start, start + margin)]
        planes += [column(move, read, k, chunk)[1] for k in range(start, start + margin)]
        messages.append(jnp.concatenate(planes + [read(0, 3)], axis=0))
    first, last = messages
    for h in range(len(out_refs) // 2):
        ahead_ref, behind_ref = out_refs[2 * h : 2 * h + 2]
        even = even_place(ngx, ngz, h + 1)

        @pl.when(even)
        def _():
            ahead_ref[...], behind_ref[...] = last, first

        @pl.when(jnp.logical_not(even))
        def _():
            ahead_ref[...], behind_ref[...] = first, last


def shared_faces(move, d):
    def face(missing, other):
        return 2.0 / (d + jnp.where(missing, d, other))

    return (
        face(move.z_low, move.below_z(d)),
        face(move.z_high, move.above_z(d)),
        face(move.x_low, move.below_x(d)),
        face(move.x_high, move.above_x(d)),
    )


def own_kernel(own_ref, density_ref, source_ref, velocity_ref, faces_ref, *, ngx, ngz, zl, xl, chunk, step):
    move = Shifts(ngx, ngz, zl, xl)
    read = column_reader(own_ref, ngx * ngz, chunk)
    for k in range(chunk):
        d = read(k, 0)
        velocity, source = column(move, read, k, chunk)
        density_ref[k : k + 1], source_ref[k : k + 1] = d, source
        for f, v in enumerate(velocity):
            velocity_ref[f, k : k + 1] = v
        for f, v in enumerate(shared_faces(move, d)):
            faces_ref[f, k : k + 1] = v


def krylov_kernel(*refs, ngx, ngz, zl, xl, chunk, hops, margin, step, places, runs):
    density_ref, source_ref, velocity_ref, faces_ref = refs[:4]
    count = 2 * hops + runs
    swapped = refs[4 : 4 + count]
    basis_ref, lower_ref, sums_ref, sides, dens, coef, vec, diag, source = refs[4 + count :]
    S, L = ngx * ngz, zl * xl
    E = chunk + 2 * HALO
    move = Shifts(ngx, ngz, zl, xl)

    place = chain_place(ngx, ngz)
    for h in range(hops):
        even = even_place(ngx, ngz, h + 1)
        sides[jnp.where(even, 1, 0), h] = swapped[2 * h][...]
        other = jnp.where(even, 0, 1)
        if not runs:
            sides[other, h] = swapped[2 * h + 1][...]
            continue
        within = place % (2 * S)
        border = (within == 0) | (within == 2 * S - 1)
        end = (place == 0) | (place == places - 1)

        @pl.when(jnp.logical_not(border))
        def _():
            sides[other, h] = swapped[1][...]

        @pl.when(border & jnp.logical_not(end))
        def _():
            sides[other, h] = swapped[2][...]

        @pl.when(end)
        def _():
            sides[other, h] = jnp.zeros(sides.shape[2:], F32)

    def pieces(a, b):
        return [(i, min(i + step, b)) for i in range(a, b, step)]

    def outer(j, up):
        hop, at = j // chunk, j % chunk
        index = at if up else margin - 1 - at
        rhs = sides[up, hop, margin + index]
        if not up and at == 0:
            rhs = rhs - (velocity_ref[2, 0] if hop == 0 else sides[0, hop - 1, 2 * margin])
        if up and at == chunk - 1 and hop + 1 < hops:
            rhs = rhs - sides[1, hop + 1, 2 * margin]
        return sides[up, hop, index], rhs

    for j in range(HALO):
        dens[HALO - 1 - j], low_rhs = outer(j, 0)
        dens[HALO + chunk + j], high_rhs = outer(j, 1)
        source[HALO - 1 - j], source[HALO + chunk + j] = low_rhs, high_rhs
    for a, b in pieces(0, chunk):
        dens[HALO + a : HALO + b] = density_ref[a:b]
        source[HALO + a : HALO + b] = source_ref[a:b]
    top = HALO + chunk - 1
    source[top] = source[top] - sides[1, 0, 2 * margin]

    spans = pieces(1, HALO) + pieces(HALO, HALO + chunk) + pieces(HALO + chunk, E - 1)
    for a, b in spans:
        d, before, after = dens[a:b], dens[a - 1 : b - 1], dens[a + 1 : b + 1]
        owned = a >= HALO and b <= HALO + chunk
        inside = d > 0.0
        if owned:
            lz, uz, lx, ux = (faces_ref[f, a - HALO : b - HALO] for f in range(4))
        else:
            d = jnp.where(inside, d, 1.0)
            lz, uz, lx, ux = shared_faces(move, d)
        ly = 2.0 / (d + jnp.where(before > 0.0, before, d))
        uy = 2.0 / (d + jnp.where(after > 0.0, after, d))
        total = lz + uz + lx + ux + ly + uy
        inverse = 1.0 / total
        if owned:
            diag[a - HALO : b - HALO] = total
            lower_ref[a - HALO : b - HALO] = ly
        else:
            inverse = jnp.where(inside, inverse, 0.0)
        coef[0, a:b] = jnp.where(move.z_low, 0.0, inverse * lz)
        coef[1, a:b] = jnp.where(move.z_high, 0.0, inverse * uz)
        coef[2, a:b] = jnp.where(move.x_low, 0.0, inverse * lx)
        coef[3, a:b] = jnp.where(move.x_high, 0.0, inverse * ux)
        coef[4, a:b] = inverse * ly
        coef[5, a:b] = inverse * uy
        vec[0, a:b] = inverse * source[a:b]

    def applied(k, a, b):
        f = vec[k, a:b]
        out = coef[0, a:b] * move.below_z(f) + coef[1, a:b] * move.above_z(f)
        out = out + (coef[2, a:b] * move.below_x(f) + coef[3, a:b] * move.above_x(f))
        return out + (coef[4, a:b] * vec[k, a - 1 : b - 1] + coef[5, a:b] * vec[k, a + 1 : b + 1])

    for k in range(1, ITERS):
        for a, b in pieces(1 + k, E - 1 - k):
            vec[k, a:b] = applied(k - 1, a, b)

    count = 2 * ITERS - 1
    powers = [0.0] * count
    firsts = [0.0] * ITERS
    steps = [0.0] * (count + 1)
    for a, b in pieces(HALO, HALO + chunk):
        own = slice(a - HALO, b - HALO)
        basis = [vec[k, a:b] for k in range(ITERS)]
        basis.append(applied(ITERS - 1, a, b))
        weight, right = diag[own], source[a:b]
        gaps = [basis[k] - basis[k + 1] for k in range(ITERS)]
        scaled = [weight * gap for gap in gaps]
        for k in range(count):
            powers[k] = powers[k] + jnp.sum(basis[(k + 1) // 2] * scaled[k // 2], axis=0)
        for k in range(ITERS):
            firsts[k] = firsts[k] + jnp.sum(right * basis[k], axis=0)
        ladder, level = [basis[0], gaps[0]], gaps
        while len(level) > 1:
            level = [level[i] - level[i + 1] for i in range(len(level) - 1)]
            ladder.append(level[0])
        for k in range(2, count + 1):
            steps[k] = steps[k] + jnp.sum(weight * ladder[k // 2] * ladder[(k + 1) // 2], axis=0)
    steps[0], steps[1] = firsts[0], powers[0]
    for k in range(ITERS):
        basis_ref[k] = vec[k, HALO - 1 : HALO + chunk]

    columns = powers + firsts + steps
    rows = [jnp.sum(c, axis=0, keepdims=True) for c in columns]
    high = -(-len(rows) // 8) * 8
    rows = rows + [jnp.zeros((1, L), F32)] * (high - len(rows))
    sums = jnp.sum(jnp.concatenate(rows, axis=0), axis=1, keepdims=True)
    lane = lax.broadcasted_iota(jnp.int32, (high, LANES), 1)
    row = lax.broadcasted_iota(jnp.int32, (high, LANES), 0)
    line = jnp.sum(jnp.where(lane == row, sums, 0.0), axis=0, keepdims=True)
    sums_ref[...] = jnp.broadcast_to(line, sums_ref.shape)


def galerkin(sums):
    n, count = ITERS, 2 * ITERS - 1
    line = jnp.sum(sums, axis=0, keepdims=True)
    lane = lax.broadcasted_iota(jnp.int32, line.shape, 1)

    def pick(k):
        return jnp.sum(jnp.where(lane == k, line, 0.0), axis=1, keepdims=True)

    powers = [pick(k) for k in range(count)]
    firsts = [pick(count + k) for k in range(n)]
    steps = [pick(count + n + k) for k in range(count + 1)]
    matrix = [jnp.concatenate([powers[k], steps[k + 1]], axis=0) for k in range(count)]
    right = [jnp.concatenate([firsts[k], steps[k]], axis=0) for k in range(n)]
    low = [[None] * n for _ in range(n)]
    scale = [None] * n
    quality = None
    for j in range(n):
        pivot = matrix[2 * j]
        for k in range(j):
            pivot = pivot - low[j][k] * low[j][k] * scale[k][0]
        share = pivot / matrix[2 * j]
        fine = share > 1e-7
        quality = jnp.where(fine, share, 0.0) if quality is None else jnp.minimum(quality, jnp.where(fine, share, 0.0))
        inverse = jnp.where(fine, 1.0 / pivot, 0.0)
        scale[j] = (pivot, inverse)
        for r in range(j + 1, n):
            entry = matrix[r + j]
            for k in range(j):
                entry = entry - low[r][k] * low[j][k] * scale[k][0]
            low[r][j] = entry * inverse
    part = list(right)
    for r in range(n):
        for k in range(r):
            part[r] = part[r] - low[r][k] * part[k]
    part = [part[r] * scale[r][1] for r in range(n)]
    for r in reversed(range(n)):
        for k in range(r + 1, n):
            part[r] = part[r] - low[k][r] * part[k]
    first = quality[0:1] >= quality[1:2]
    by_power = [jnp.where(first, p[0:1], 0.0) for p in part]
    by_step = [jnp.where(first, 0.0, p[1:2]) for p in part]
    return by_power, by_step


def render_kernel(
    sums_ref, basis_ref, faces_ref, lower_ref, velocity_ref, table_ref, out_ref, press, flat, turned, parts,
    *, ngx, ngz, zl, xl, chunk, step
):
    S, L = ngx * ngz, zl * xl
    yl = S * chunk
    height = out_ref.shape[0] // S
    move = Shifts(ngx, ngz, zl, xl)
    by_power, by_step = galerkin(sums_ref[...])
    by_power = [v.reshape(1, 1, 1) for v in by_power]
    by_step = [v.reshape(1, 1, 1) for v in by_step]
    for a in range(0, chunk + 1, step):
        b = min(a + step, chunk + 1)
        level = [basis_ref[k, a:b] for k in range(ITERS)]
        value = 0.0
        for k in range(ITERS):
            value = value + by_power[k] * level[k]
        value = value + by_step[0] * level[0]
        for k in range(1, ITERS):
            level = [level[i] - level[i + 1] for i in range(len(level) - 1)]
            value = value + by_step[k] * level[0]
        press[a:b] = value
    for a in range(0, chunk, step):
        b = min(a + step, chunk)
        p = press[a + 1 : b + 1]
        fronts = (
            jnp.where(move.z_low, 0.0, move.below_z(p)),
            jnp.where(move.x_low, 0.0, move.below_x(p)),
            press[a:b],
        )
        scalar = None
        for k, front in enumerate(fronts):
            lower = lower_ref[a:b] if k == 2 else faces_ref[2 * k, a:b]
            corrected = velocity_ref[k, a:b] - lower * (p - front)
            for c in range(a, b):
                out_ref[pl.ds(k * chunk + c, S, stride=height), :] = corrected[c - a]
            scalar = corrected if scalar is None else scalar + corrected
        for c in range(a, b):
            flat[pl.ds(c, S, stride=chunk), :] = scalar[c - a]
    turned[...] = flat[...].T.reshape(zl, xl, yl)

    group = ngx * chunk
    functions = table_ref.shape[0] // ngz
    lane = lax.broadcasted_iota(jnp.int32, (xl, yl), 1)

    def curve_sums(index, carry):
        rows = [jnp.broadcast_to(table_ref[index, r : r + 1, :], (xl, yl)) for r in range(9)]
        rates, bases, gain = rows[:4], rows[4:8], rows[8]
        through = jnp.ones((xl, yl), F32)
        colors = [jnp.zeros((xl, yl), F32) for _ in range(3)]
        for z in range(zl):
            x = turned[z]
            curves = [1.0 / (1.0 + jnp.exp2(rates[c] * x + bases[c])) for c in range(4)]
            opacity = gain * curves[3]
            weight = through * opacity
            colors = [colors[c] + weight * curves[c] for c in range(3)]
            through = through * (1.0 - opacity)
        for c, value in enumerate(colors + [through]):
            parts[index, c] = value
        return carry

    lax.fori_loop(0, table_ref.shape[0], curve_sums, 0)
    for i in range(ngz):
        images = [jnp.zeros((xl, LANES), F32) for _ in range(ngx)]
        for t in range(functions):
            colors = [parts[i * functions + t, c] for c in range(3)]
            through = parts[i * functions + t, 3]
            planes = list(colors)
            everything = through
            for _ in range(ngz - 1):
                planes = [colors[c] + through * roll(planes[c], -group, 1) for c in range(3)]
                everything = through * roll(everything, -group, 1)
            planes.append(1.0 - everything)
            for c, image in enumerate(planes):
                start = (t * 4 + c) * chunk
                here = (lane >= start) & (lane < start + chunk)
                for k in range(ngx):
                    images[k] = jnp.where(here, roll(image, start - k * chunk, 1), images[k])
        for k in range(ngx):
            place = (i * ngx + k) * height + 3 * chunk
            out_ref[place : place + xl, :] = images[k]


def unpack_kernel(in_ref, corrected_ref, images_ref, flat, *, table, chunk):
    zl, xl, yl = corrected_ref.shape[1:]
    functions = images_ref.shape[0]
    pieces = yl // chunk
    for f in range(3):
        for c in range(pieces):
            flat[c * chunk : (c + 1) * chunk, :] = in_ref[owner(table, c), f * chunk : (f + 1) * chunk, :]
        corrected_ref[f] = flat[...].T.reshape(zl, xl, yl)
    lane = lax.broadcasted_iota(jnp.int32, (xl, yl), 1)
    images = [jnp.zeros((xl, yl), F32) for _ in range(functions * 4)]
    for c in range(pieces):
        source = in_ref[owner(table, c), 3 * chunk : 3 * chunk + xl, :]
        here = (lane >= c * chunk) & (lane < (c + 1) * chunk)
        images = [jnp.where(here, roll(source, (c - k) * chunk, 1), image) for k, image in enumerate(images)]
    for k, image in enumerate(images):
        images_ref[k // 4, k % 4] = image


def solution(mesh):
    ngx, ngy, ngz = mesh.shape["gx"], mesh.shape["gy"], mesh.shape["gz"]
    S, devices = ngx * ngz, ngx * ngy * ngz
    table = [z * ngx + x for x, z in snake(ngx, ngz)]
    places = chain(ngx, ngy, ngz)

    def local(phase_field, thermal, velocity, transfer_slope, transfer_offset, transfer_gain):
        zl, xl, yl = thermal.shape
        L, chunk = zl * xl, yl // S
        functions = transfer_slope.shape[0] // ngz
        assert yl % S == 0 and L == LANES and yl == LANES and functions * 4 * chunk <= LANES
        hops = -(-HALO // chunk)
        margin = min(chunk, HALO)
        step = max(1, 4 * 8 // S)

        vmem = pl.BlockSpec(memory_space=pltpu.VMEM)

        def call(body, specs, out, scratch=(), **kwargs):
            kernel = pl.pallas_call(
                lambda *refs: body(*refs, **kwargs),
                in_specs=specs,
                out_specs=jax.tree.map(lambda _: vmem, out),
                out_shape=out,
                scratch_shapes=[pltpu.VMEM(s, F32) for s in scratch],
                name=body.__name__,
            )

            def run(*args):
                return kernel(*[near(a) if spec is vmem else a for a, spec in zip(args, specs)])

            return run

        def near(array):
            return pltpu.with_memory_space_constraint(array, pltpu.VMEM)

        def shaped(*shape):
            return jax.ShapeDtypeStruct(shape, F32)

        def placed(*shape):
            return pltpu.VMEM(shape, F32)

        free = pl.BlockSpec()
        tables = (transfer_slope.T, transfer_offset.T, transfer_gain[None, :])
        blocks, curves = call(
            pack_kernel,
            [free] * 6,
            (placed(S, chunk * FIELDS, L), placed(transfer_gain.shape[0], 16, LANES)),
            table=table, chunk=chunk, depth=zl * ngz,
        )(phase_field, thermal, velocity, *tables)
        pencils = lax.all_to_all(blocks, ("gz", "gx"), 0, 0, tiled=True)
        every = ("gx", "gy", "gz")
        own = pencils.reshape(-1, L)
        sizes = dict(ngx=ngx, ngz=ngz, zl=zl, xl=xl, chunk=chunk)
        message = (2 * margin + 1, S, L)
        messages = call(edges_kernel, [vmem], [placed(*message)] * (2 * hops), margin=margin, **sizes)(own)
        swaps = [(messages[i], hop_swaps(places, i // 2 + 1, i % 2)) for i in range(2 * hops)]
        runs = hops == 1 and ngy % 2 == 0 and S % 2 == 0
        if runs:
            swaps = [swaps[0]] + [(messages[1], run_swaps(places, 2 * S, start)) for start in (0, S)]
        swapped = [lax.ppermute(value, every, pairs) for value, pairs in swaps[::-1]][::-1]
        density, source, velocities, faces = call(
            own_kernel,
            [vmem],
            (placed(chunk, S, L), placed(chunk, S, L), placed(3, chunk, S, L), placed(4, chunk, S, L)),
            step=step, **sizes,
        )(own)
        wide = chunk + 2 * HALO
        basis, lower, sums = call(
            krylov_kernel,
            [vmem] * (4 + len(swapped)),
            (placed(ITERS, chunk + 1, S, L), placed(chunk, S, L), placed(devices, LANES)),
            ((2, hops) + message, (wide, S, L), (6, wide, S, L), (ITERS, wide, S, L), (chunk, S, L), (wide, S, L)),
            hops=hops, margin=margin, step=step, places=devices, runs=int(runs), **sizes,
        )(density, source, velocities, faces, *swapped)
        sums = lax.all_to_all(sums, every, 0, 0, tiled=True)
        height = 3 * chunk + xl
        height += -height % 8
        packed = call(
            render_kernel,
            [vmem] * 6,
            placed(S * height, LANES),
            ((chunk + 1, S, L), (yl, L), (zl, xl, yl), (curves.shape[0], 4, xl, yl)),
            step=step, **sizes,
        )(sums, basis, faces, lower, velocities, curves)
        home = lax.all_to_all(packed.reshape(S, height, LANES), ("gz", "gx"), 0, 0, tiled=True)
        return call(
            unpack_kernel,
            [vmem],
            (shaped(3, zl, xl, yl), shaped(functions, 4, xl, yl)),
            ((yl, L),),
            table=table, chunk=chunk,
        )(home)

    return jax.shard_map(
        local,
        mesh=mesh,
        in_specs=(P("gz", "gx", "gy"), P("gz", "gx", "gy"), P(None, "gz", "gx", "gy"), P(), P(), P()),
        out_specs=(P(None, "gz", "gx", "gy"), P("gz", None, "gx", "gy")),
        check_vma=False,
    )
```

```python
import math

import jax
import jax.numpy as jnp
from jax import lax
from jax.experimental import pallas as pl
from jax.experimental.pallas import tpu as pltpu
from jax.sharding import PartitionSpec as P

ITERS = 4
HALO = ITERS + 1
FIELDS = 4
LANES = 128
LOG2E = math.log2(math.e)
F32 = jnp.float32


def snake(ngx, ngz):
    order = []
    for x in range(ngx):
        depths = range(ngz) if x % 2 == 0 else reversed(range(ngz))
        order.extend((x, z) for z in depths)
    return order


def chain(ngx, ngy, ngz):
    places = []
    order = snake(ngx, ngz)
    for y in range(ngy):
        for x, z in order if y % 2 == 0 else order[::-1]:
            places.append((x * ngy + y) * ngz + z)
    return places


def both_ways(places, pairs):
    pairs = [(places[a], places[b]) for a, b in pairs]
    return pairs + [(b, a) for a, b in pairs]


def hop_swaps(places, hop, odd):
    return both_ways(places, [(i, i + hop) for i in range(len(places) - hop) if i // hop % 2 == odd])


def run_swaps(places, run, start):
    pairs, rest = [], list(range(start))
    while start + run <= len(places):
        pairs.append((start, start + run - 1))
        pairs.extend((i, i + 1) for i in range(start + 1, start + run - 1, 2))
        start += run
    rest.extend(range(start, len(places)))
    pairs.extend((i, i + 1) for i in rest if i % 2 == 0)
    return both_ways(places, pairs)


def chain_place(ngx, ngz):
    x, y, z = lax.axis_index("gx"), lax.axis_index("gy"), lax.axis_index("gz")
    within = x * ngz + jnp.where(x % 2 == 0, z, ngz - 1 - z)
    group = ngx * ngz
    return y * group + jnp.where(y % 2 == 0, within, group - 1 - within)


def roll(value, shift, axis):
    size = value.shape[axis]
    shift = shift % size
    return value if shift == 0 else pltpu.roll(value, shift, axis)


def owner(table, c):
    forward = lax.axis_index("gy") % 2 == 0
    return jnp.where(forward, table[c], table[len(table) - 1 - c])


def pack_kernel(phase_ref, thermal_ref, velocity_ref, slope_ref, offset_ref, gain_ref, *outs, table, chunk, depth):
    out_ref, curves_ref, density_ref, kept_ref = outs
    zl, xl, yl = thermal_ref.shape
    density = (1.0 + 9.0 * phase_ref[...].astype(F32)) * thermal_ref[...]
    density_ref[...] = density
    kept_ref[...] = velocity_ref[...]
    for f in range(FIELDS):
        field = density if f == 0 else velocity_ref[f - 1]
        turned = field.reshape(zl * xl, yl).T
        for c in range(yl // chunk):
            rows = turned[c * chunk : (c + 1) * chunk]
            out_ref[owner(table, c), pl.ds(f, chunk, stride=FIELDS), :] = rows
    for t in range(curves_ref.shape[0]):
        curves_ref[t, 0:4, :] = jnp.broadcast_to(-LOG2E * slope_ref[:, t : t + 1], (4, LANES))
        curves_ref[t, 4:8, :] = jnp.broadcast_to(-LOG2E * offset_ref[:, t : t + 1], (4, LANES))
        curves_ref[t, 8:9, :] = jnp.broadcast_to(gain_ref[:, t : t + 1] / depth, (1, LANES))


class Slot:
    def __init__(self, zl, xl, chunk):
        self.width = 1
        while self.width < zl + xl:
            self.width *= 2
        groups = LANES // self.width
        self.faces = chunk
        self.deep = -(-chunk // groups)
        self.side = chunk + self.deep
        self.images = -(-(self.side + 1) // 8) * 8
        self.height = -(-(self.images + xl) // 8) * 8


def even_place(ngx, ngz, hop):
    return chain_place(ngx, ngz) // hop % 2 == 0


class Shifts:
    def __init__(self, ngx, ngz, zl, xl):
        self.ngx, self.ngz, self.zl, self.xl = ngx, ngz, zl, xl
        shape = (1, ngx * ngz, zl * xl)
        lane = lax.broadcasted_iota(jnp.int32, shape, 2)
        sub = lax.broadcasted_iota(jnp.int32, shape, 1)
        z, x = lane // xl, lane % xl
        gz, gx = sub // ngx, sub % ngx
        self.z_first, self.z_last = z == 0, z == zl - 1
        self.x_first, self.x_last = x == 0, x == xl - 1
        self.z_low = self.z_first & (gz == 0)
        self.z_high = self.z_last & (gz == ngz - 1)
        self.x_low = self.x_first & (gx == 0)
        self.x_high = self.x_last & (gx == ngx - 1)

    def below_z(self, f):
        near = roll(f, self.xl, 2)
        return jnp.where(self.z_first, roll(near, self.ngx, 1), near)

    def above_z(self, f):
        near = roll(f, -self.xl, 2)
        return jnp.where(self.z_last, roll(near, -self.ngx, 1), near)

    def below_x(self, f):
        far = roll(roll(f, 1 - self.xl, 2), 1, 1)
        return jnp.where(self.x_first, far, roll(f, 1, 2))

    def above_x(self, f):
        far = roll(roll(f, self.xl - 1, 2), -1, 1)
        return jnp.where(self.x_last, far, roll(f, -1, 2))


def divergence(move, velocity, after):
    vz, vx, vy = velocity
    out = -(jnp.where(move.z_high, 0.0, move.above_z(vz)) - vz)
    out = out - (jnp.where(move.x_high, 0.0, move.above_x(vx)) - vx)
    return out + vy if after is None else out - (after - vy)


def column_reader(own_ref, S, chunk):
    def read(k, f):
        return own_ref[pl.ds(k * FIELDS + f, S, stride=chunk * FIELDS), :][None]

    return read


def column(move, read, k, chunk):
    velocity = [read(k, f) for f in (1, 2, 3)]
    return velocity, divergence(move, velocity, read(k + 1, 3) if k + 1 < chunk else None)


def edges_kernel(own_ref, *out_refs, ngx, ngz, zl, xl, chunk, margin):
    move = Shifts(ngx, ngz, zl, xl)
    read = column_reader(own_ref, ngx * ngz, chunk)
    messages = []
    for start in (0, chunk - margin):
        planes = [read(k, 0) for k in range(start, start + margin)]
        planes += [column(move, read, k, chunk)[1] for k in range(start, start + margin)]
        messages.append(jnp.concatenate(planes + [read(0, 3)], axis=0))
    first, last = messages
    for h in range(len(out_refs) // 2):
        ahead_ref, behind_ref = out_refs[2 * h : 2 * h + 2]
        even = even_place(ngx, ngz, h + 1)

        @pl.when(even)
        def _():
            ahead_ref[...], behind_ref[...] = last, first

        @pl.when(jnp.logical_not(even))
        def _():
            ahead_ref[...], behind_ref[...] = first, last


def shared_faces(move, d):
    def face(missing, other):
        return 2.0 / (d + jnp.where(missing, d, other))

    return (
        face(move.z_low, move.below_z(d)),
        face(move.z_high, move.above_z(d)),
        face(move.x_low, move.below_x(d)),
        face(move.x_high, move.above_x(d)),
    )


def own_kernel(own_ref, home_ref, density_ref, source_ref, velocity_ref, faces_ref, lower_ref, *, ngx, ngz, zl, xl, chunk):
    d = home_ref[...]
    lower_ref[0] = 2.0 / (d + jnp.concatenate([d[:1], d[:-1]], axis=0))
    lower_ref[1] = 2.0 / (d + roll(d, 1, 1))
    lower_ref[2] = 2.0 / (d + roll(d, 1, 2))
    move = Shifts(ngx, ngz, zl, xl)
    read = column_reader(own_ref, ngx * ngz, chunk)
    for k in range(chunk):
        d = read(k, 0)
        velocity, source = column(move, read, k, chunk)
        density_ref[k : k + 1], source_ref[k : k + 1] = d, source
        for f, v in enumerate(velocity):
            velocity_ref[f, k : k + 1] = v
        for f, v in enumerate(shared_faces(move, d)):
            faces_ref[f, k : k + 1] = v


def krylov_kernel(*refs, ngx, ngz, zl, xl, chunk, hops, margin, step, places, runs):
    density_ref, source_ref, velocity_ref, faces_ref = refs[:4]
    count = 2 * hops + runs
    swapped = refs[4 : 4 + count]
    basis_ref, lower_ref, sums_ref, sides, dens, coef, vec, diag, source = refs[4 + count :]
    S, L = ngx * ngz, zl * xl
    E = chunk + 2 * HALO
    move = Shifts(ngx, ngz, zl, xl)

    place = chain_place(ngx, ngz)
    for h in range(hops):
        even = even_place(ngx, ngz, h + 1)
        sides[jnp.where(even, 1, 0), h] = swapped[2 * h][...]
        other = jnp.where(even, 0, 1)
        if not runs:
            sides[other, h] = swapped[2 * h + 1][...]
            continue
        within = place % (2 * S)
        border = (within == 0) | (within == 2 * S - 1)
        end = (place == 0) | (place == places - 1)

        @pl.when(jnp.logical_not(border))
        def _():
            sides[other, h] = swapped[1][...]

        @pl.when(border & jnp.logical_not(end))
        def _():
            sides[other, h] = swapped[2][...]

        @pl.when(end)
        def _():
            sides[other, h] = jnp.zeros(sides.shape[2:], F32)

    def pieces(a, b):
        return [(i, min(i + step, b)) for i in range(a, b, step)]

    def outer(j, up):
        hop, at = j // chunk, j % chunk
        index = at if up else margin - 1 - at
        rhs = sides[up, hop, margin + index]
        if not up and at == 0:
            rhs = rhs - (velocity_ref[2, 0] if hop == 0 else sides[0, hop - 1, 2 * margin])
        if up and at == chunk - 1 and hop + 1 < hops:
            rhs = rhs - sides[1, hop + 1, 2 * margin]
        return sides[up, hop, index], rhs

    for j in range(HALO):
        dens[HALO - 1 - j], low_rhs = outer(j, 0)
        dens[HALO + chunk + j], high_rhs = outer(j, 1)
        source[HALO - 1 - j], source[HALO + chunk + j] = low_rhs, high_rhs
    for a, b in pieces(0, chunk):
        dens[HALO + a : HALO + b] = density_ref[a:b]
        source[HALO + a : HALO + b] = source_ref[a:b]
    top = HALO + chunk - 1
    source[top] = source[top] - sides[1, 0, 2 * margin]

    spans = pieces(1, HALO) + pieces(HALO, HALO + chunk) + pieces(HALO + chunk, E - 1)
    for a, b in spans:
        d, before, after = dens[a:b], dens[a - 1 : b - 1], dens[a + 1 : b + 1]
        owned = a >= HALO and b <= HALO + chunk
        inside = d > 0.0
        if owned:
            lz, uz, lx, ux = (faces_ref[f, a - HALO : b - HALO] for f in range(4))
        else:
            d = jnp.where(inside, d, 1.0)
            lz, uz, lx, ux = shared_faces(move, d)
        ly = 2.0 / (d + jnp.where(before > 0.0, before, d))
        uy = 2.0 / (d + jnp.where(after > 0.0, after, d))
        total = lz + uz + lx + ux + ly + uy
        inverse = 1.0 / total
        if owned:
            diag[a - HALO : b - HALO] = total
            lower_ref[a - HALO : b - HALO] = ly
        else:
            inverse = jnp.where(inside, inverse, 0.0)
        coef[0, a:b] = jnp.where(move.z_low, 0.0, inverse * lz)
        coef[1, a:b] = jnp.where(move.z_high, 0.0, inverse * uz)
        coef[2, a:b] = jnp.where(move.x_low, 0.0, inverse * lx)
        coef[3, a:b] = jnp.where(move.x_high, 0.0, inverse * ux)
        coef[4, a:b] = inverse * ly
        coef[5, a:b] = inverse * uy
        vec[0, a:b] = inverse * source[a:b]

    def applied(k, a, b):
        f = vec[k, a:b]
        out = coef[0, a:b] * move.below_z(f) + coef[1, a:b] * move.above_z(f)
        out = out + (coef[2, a:b] * move.below_x(f) + coef[3, a:b] * move.above_x(f))
        return out + (coef[4, a:b] * vec[k, a - 1 : b - 1] + coef[5, a:b] * vec[k, a + 1 : b + 1])

    for k in range(1, ITERS):
        for a, b in pieces(1 + k, E - 1 - k):
            vec[k, a:b] = applied(k - 1, a, b)

    count = 2 * ITERS - 1
    powers = [0.0] * count
    firsts = [0.0] * ITERS
    steps = [0.0] * (count + 1)
    for a, b in pieces(HALO, HALO + chunk):
        own = slice(a - HALO, b - HALO)
        basis = [vec[k, a:b] for k in range(ITERS)]
        basis.append(applied(ITERS - 1, a, b))
        weight, right = diag[own], source[a:b]
        gaps = [basis[k] - basis[k + 1] for k in range(ITERS)]
        scaled = [weight * gap for gap in gaps]
        for k in range(count):
            powers[k] = powers[k] + jnp.sum(basis[(k + 1) // 2] * scaled[k // 2], axis=0)
        for k in range(ITERS):
            firsts[k] = firsts[k] + jnp.sum(right * basis[k], axis=0)
        ladder, level = [basis[0], gaps[0]], gaps
        while len(level) > 1:
            level = [level[i] - level[i + 1] for i in range(len(level) - 1)]
            ladder.append(level[0])
        for k in range(2, count + 1):
            steps[k] = steps[k] + jnp.sum(weight * ladder[k // 2] * ladder[(k + 1) // 2], axis=0)
    steps[0], steps[1] = firsts[0], powers[0]
    for k in range(ITERS):
        basis_ref[k] = vec[k, HALO - 1 : HALO + chunk]

    columns = powers + firsts + steps
    rows = [jnp.sum(c, axis=0, keepdims=True) for c in columns]
    high = -(-len(rows) // 8) * 8
    rows = rows + [jnp.zeros((1, L), F32)] * (high - len(rows))
    sums = jnp.sum(jnp.concatenate(rows, axis=0), axis=1, keepdims=True)
    lane = lax.broadcasted_iota(jnp.int32, (high, LANES), 1)
    row = lax.broadcasted_iota(jnp.int32, (high, LANES), 0)
    line = jnp.sum(jnp.where(lane == row, sums, 0.0), axis=0, keepdims=True)
    sums_ref[...] = jnp.broadcast_to(line, sums_ref.shape)


def galerkin(sums):
    n, count = ITERS, 2 * ITERS - 1
    line = jnp.sum(sums, axis=0, keepdims=True)
    lane = lax.broadcasted_iota(jnp.int32, line.shape, 1)

    def pick(k):
        return jnp.sum(jnp.where(lane == k, line, 0.0), axis=1, keepdims=True)

    powers = [pick(k) for k in range(count)]
    firsts = [pick(count + k) for k in range(n)]
    steps = [pick(count + n + k) for k in range(count + 1)]
    matrix = [jnp.concatenate([powers[k], steps[k + 1]], axis=0) for k in range(count)]
    right = [jnp.concatenate([firsts[k], steps[k]], axis=0) for k in range(n)]
    low = [[None] * n for _ in range(n)]
    scale = [None] * n
    quality = None
    for j in range(n):
        pivot = matrix[2 * j]
        for k in range(j):
            pivot = pivot - low[j][k] * low[j][k] * scale[k][0]
        share = pivot / matrix[2 * j]
        fine = share > 1e-7
        quality = jnp.where(fine, share, 0.0) if quality is None else jnp.minimum(quality, jnp.where(fine, share, 0.0))
        inverse = jnp.where(fine, 1.0 / pivot, 0.0)
        scale[j] = (pivot, inverse)
        for r in range(j + 1, n):
            entry = matrix[r + j]
            for k in range(j):
                entry = entry - low[r][k] * low[j][k] * scale[k][0]
            low[r][j] = entry * inverse
    part = list(right)
    for r in range(n):
        for k in range(r):
            part[r] = part[r] - low[r][k] * part[k]
    part = [part[r] * scale[r][1] for r in range(n)]
    for r in reversed(range(n)):
        for k in range(r + 1, n):
            part[r] = part[r] - low[k][r] * part[k]
    first = quality[0:1] >= quality[1:2]
    by_power = [jnp.where(first, p[0:1], 0.0) for p in part]
    by_step = [jnp.where(first, 0.0, p[1:2]) for p in part]
    return by_power, by_step


def render_kernel(
    sums_ref, basis_ref, faces_ref, lower_ref, velocity_ref, table_ref, out_ref, press, flat, turned, parts,
    *, ngx, ngz, zl, xl, chunk, step
):
    S, L = ngx * ngz, zl * xl
    yl = S * chunk
    slot = Slot(zl, xl, chunk)
    height = slot.height
    move = Shifts(ngx, ngz, zl, xl)
    by_power, by_step = galerkin(sums_ref[...])
    by_power = [v.reshape(1, 1, 1) for v in by_power]
    by_step = [v.reshape(1, 1, 1) for v in by_step]
    for a in range(0, chunk + 1, step):
        b = min(a + step, chunk + 1)
        level = [basis_ref[k, a:b] for k in range(ITERS)]
        value = 0.0
        for k in range(ITERS):
            value = value + by_power[k] * level[k]
        value = value + by_step[0] * level[0]
        for k in range(1, ITERS):
            level = [level[i] - level[i + 1] for i in range(len(level) - 1)]
            value = value + by_step[k] * level[0]
        press[a:b] = value
    spot = lax.broadcasted_iota(jnp.int32, (S, L), 1)
    sides = [jnp.zeros((S, L), F32) for _ in range(slot.deep)]
    for a in range(0, chunk, step):
        b = min(a + step, chunk)
        p = press[a + 1 : b + 1]
        fronts = (
            jnp.where(move.z_low, 0.0, move.below_z(p)),
            jnp.where(move.x_low, 0.0, move.below_x(p)),
            press[a:b],
        )
        pieces = []
        for k, front in enumerate(fronts):
            lower = lower_ref[a:b] if k == 2 else faces_ref[2 * k, a:b]
            pieces.append(velocity_ref[k, a:b] - lower * (p - front))
        scalar = pieces[0] + pieces[1] + pieces[2]
        if a == 0:
            out_ref[pl.ds(slot.side, S, stride=height), :] = pieces[2][0]
        for c in range(a, b):
            out_ref[pl.ds(c, S, stride=height), :] = p[c - a]
            flat[pl.ds(c, S, stride=chunk), :] = scalar[c - a]
            base = c // slot.deep * slot.width
            deep = roll(pieces[0][c - a], base, 1)
            where = (spot - (base + xl)) * xl
            wide = jnp.take_along_axis(pieces[1][c - a], jnp.clip(where, 0, L - 1), axis=1, mode="promise_in_bounds")
            r = c % slot.deep
            sides[r] = jnp.where(spot >= base, jnp.where(spot >= base + xl, wide, deep), sides[r])
    for r, side in enumerate(sides):
        out_ref[pl.ds(slot.faces + r, S, stride=height), :] = side
    turned[...] = flat[...].T.reshape(zl, xl, yl)

    group = ngx * chunk
    band = LANES // 4
    functions = table_ref.shape[0] // ngz
    lane = lax.broadcasted_iota(jnp.int32, (xl, yl), 1)

    def curve_sums(index, carry):
        rows = [jnp.broadcast_to(table_ref[index, r : r + 1, :], (xl, yl)) for r in range(9)]
        rates, bases, gain = rows[:4], rows[4:8], rows[8]
        through = jnp.ones((xl, yl), F32)
        colors = [jnp.zeros((xl, yl), F32) for _ in range(3)]
        for z in range(zl):
            x = turned[z]
            curves = [1.0 / (1.0 + jnp.exp2(rates[c] * x + bases[c])) for c in range(4)]
            opacity = gain * curves[3]
            weight = through * opacity
            colors = [colors[c] + weight * curves[c] for c in range(3)]
            through = through * (1.0 - opacity)
        for c, value in enumerate(colors + [through]):
            parts[index, c] = value
        return carry

    lax.fori_loop(0, table_ref.shape[0], curve_sums, 0)
    for i in range(ngz):
        images = [jnp.zeros((xl, LANES), F32) for _ in range(ngx)]
        for t in range(functions):
            planes = [parts[i * functions + t, c] for c in range(4)]
            span = 1
            while span < ngz:
                behind = [roll(plane, -span * group, 1) for plane in planes]
                planes = [planes[c] + planes[3] * behind[c] for c in range(3)] + [planes[3] * behind[3]]
                span *= 2
            planes[3] = 1.0 - planes[3]
            merged = planes[0]
            for c in range(1, 4):
                merged = jnp.where(lane >= c * band, roll(planes[c], c * band, 1), merged)
            for k in range(ngx):
                here = (lane % band) // chunk == t
                images[k] = jnp.where(here, roll(merged, (t - k) * chunk, 1), images[k])
        for k in range(ngx):
            place = (i * ngx + k) * height + slot.images
            out_ref[place : place + xl, :] = images[k]


def unpack_kernel(in_ref, lower_ref, velocity_ref, corrected_ref, images_ref, flat, sides, *, table, chunk):
    zl, xl, yl = corrected_ref.shape[1:]
    slot = Slot(zl, xl, chunk)
    functions = images_ref.shape[0]
    band = LANES // 4
    lane = lax.broadcasted_iota(jnp.int32, (xl, yl), 1)
    images = [jnp.zeros((xl, yl), F32) for _ in range(functions * 4)]
    for c in range(yl // chunk):
        place = owner(table, c)
        flat[c * chunk : (c + 1) * chunk, :] = in_ref[place, :chunk, :]
        faces = in_ref[place, slot.faces : slot.faces + 8, :]
        for g in range(-(-chunk // slot.deep)):
            rows = min(slot.deep, chunk - g * slot.deep)
            start = c * chunk + g * slot.deep
            sides[start : start + rows, :] = roll(faces, -g * slot.width, 1)[:rows]
        source = in_ref[place, slot.images : slot.images + xl, :]
        here = (lane >= c * chunk) & (lane < (c + 1) * chunk)
        for k in range(functions * 4):
            shift = c * chunk - (k % 4 * band + k // 4 * chunk)
            images[k] = jnp.where(here, roll(source, shift, 1), images[k])
    for k, image in enumerate(images):
        images_ref[k // 4, k % 4] = image
    p = flat[...].T.reshape(zl, xl, yl)
    faces = sides[...].T
    deep, wide = faces[:xl], faces[xl : xl + zl]
    front = in_ref[owner(table, 0), slot.side : slot.side + 1, :]
    high = jnp.broadcast_to(front, (yl, zl * xl)).T.reshape(zl, xl, yl)
    x = lax.broadcasted_iota(jnp.int32, (zl, xl, yl), 1)
    y = lax.broadcasted_iota(jnp.int32, (zl, xl, yl), 2)
    inner = velocity_ref[0, 1:] - lower_ref[0, 1:] * (p[1:] - p[:-1])
    corrected_ref[0, 0], corrected_ref[0, 1:] = deep, inner
    inner = velocity_ref[1] - lower_ref[1] * (p - roll(p, 1, 1))
    corrected_ref[1] = jnp.where(x == 0, wide[:, None, :], inner)
    inner = velocity_ref[2] - lower_ref[2] * (p - roll(p, 1, 2))
    corrected_ref[2] = jnp.where(y == 0, high, inner)


def solution(mesh):
    ngx, ngy, ngz = mesh.shape["gx"], mesh.shape["gy"], mesh.shape["gz"]
    S, devices = ngx * ngz, ngx * ngy * ngz
    table = [z * ngx + x for x, z in snake(ngx, ngz)]
    places = chain(ngx, ngy, ngz)

    def local(phase_field, thermal, velocity, transfer_slope, transfer_offset, transfer_gain):
        zl, xl, yl = thermal.shape
        L, chunk = zl * xl, yl // S
        functions = transfer_slope.shape[0] // ngz
        assert yl % S == 0 and L == LANES and yl == LANES and max(ngx, functions) * 4 * chunk <= LANES
        assert ngz & (ngz - 1) == 0
        hops = -(-HALO // chunk)
        margin = min(chunk, HALO)
        step = max(1, 4 * 8 // S)

        vmem = pl.BlockSpec(memory_space=pltpu.VMEM)

        def call(body, specs, out, scratch=(), **kwargs):
            kernel = pl.pallas_call(
                lambda *refs: body(*refs, **kwargs),
                in_specs=specs,
                out_specs=jax.tree.map(lambda _: vmem, out),
                out_shape=out,
                scratch_shapes=[pltpu.VMEM(s, F32) for s in scratch],
                name=body.__name__,
            )

            def run(*args):
                return kernel(*[near(a) if spec is vmem else a for a, spec in zip(args, specs)])

            return run

        def near(array):
            return pltpu.with_memory_space_constraint(array, pltpu.VMEM)

        def shaped(*shape):
            return jax.ShapeDtypeStruct(shape, F32)

        def placed(*shape):
            return pltpu.VMEM(shape, F32)

        free = pl.BlockSpec()
        tables = (transfer_slope.T, transfer_offset.T, transfer_gain[None, :])
        block = (zl, xl, yl)
        blocks, curves, home_density, kept = call(
            pack_kernel,
            [free] * 6,
            (placed(S, chunk * FIELDS, L), placed(transfer_gain.shape[0], 16, LANES), placed(*block), placed(3, *block)),
            table=table, chunk=chunk, depth=zl * ngz,
        )(phase_field, thermal, velocity, *tables)
        pencils = lax.all_to_all(blocks, ("gz", "gx"), 0, 0, tiled=True)
        every = ("gx", "gy", "gz")
        own = pencils.reshape(-1, L)
        sizes = dict(ngx=ngx, ngz=ngz, zl=zl, xl=xl, chunk=chunk)
        message = (2 * margin + 1, S, L)
        messages = call(edges_kernel, [vmem], [placed(*message)] * (2 * hops), margin=margin, **sizes)(own)
        swaps = [(messages[i], hop_swaps(places, i // 2 + 1, i % 2)) for i in range(2 * hops)]
        runs = hops == 1 and ngy % 2 == 0 and S % 2 == 0
        if runs:
            swaps = [swaps[0]] + [(messages[1], run_swaps(places, 2 * S, start)) for start in (0, S)]
        swapped = [lax.ppermute(value, every, pairs) for value, pairs in swaps[::-1]][::-1]
        density, source, velocities, faces, home_lower = call(
            own_kernel,
            [vmem] * 2,
            (placed(chunk, S, L), placed(chunk, S, L), placed(3, chunk, S, L), placed(4, chunk, S, L), placed(3, *block)),
            **sizes,
        )(own, home_density)
        wide = chunk + 2 * HALO
        basis, lower, sums = call(
            krylov_kernel,
            [vmem] * (4 + len(swapped)),
            (placed(ITERS, chunk + 1, S, L), placed(chunk, S, L), placed(devices, LANES)),
            ((2, hops) + message, (wide, S, L), (6, wide, S, L), (ITERS, wide, S, L), (chunk, S, L), (wide, S, L)),
            hops=hops, margin=margin, step=step, places=devices, runs=int(runs), **sizes,
        )(density, source, velocities, faces, *swapped)
        sums = lax.all_to_all(sums, every, 0, 0, tiled=True)
        height = Slot(zl, xl, chunk).height
        packed = call(
            render_kernel,
            [vmem] * 6,
            placed(S * height, LANES),
            ((chunk + 1, S, L), (yl, L), (zl, xl, yl), (curves.shape[0], 4, xl, yl)),
            step=step, **sizes,
        )(sums, basis, faces, lower, velocities, curves)
        home = lax.all_to_all(packed.reshape(S, height, LANES), ("gz", "gx"), 0, 0, tiled=True)
        return call(
            unpack_kernel,
            [vmem] * 3,
            (shaped(3, *block), shaped(functions, 4, xl, yl)),
            ((yl, L), (yl, LANES)),
            table=table, chunk=chunk,
        )(home, home_lower, kept)

    return jax.shard_map(
        local,
        mesh=mesh,
        in_specs=(P("gz", "gx", "gy"), P("gz", "gx", "gy"), P(None, "gz", "gx", "gy"), P(), P(), P()),
        out_specs=(P(None, "gz", "gx", "gy"), P("gz", None, "gx", "gy")),
        check_vma=False,
    )
```

```python
import math

import jax
import jax.numpy as jnp
from jax import lax
from jax.experimental import pallas as pl
from jax.experimental.pallas import tpu as pltpu
from jax.sharding import PartitionSpec as P

ITERS = 4
HALO = ITERS + 1
FIELDS = 4
LANES = 128
VMEM_LIMIT = 24 << 20
LOG2E = math.log2(math.e)
F32 = jnp.float32


def snake(ngx, ngz):
    order = []
    for x in range(ngx):
        depths = range(ngz) if x % 2 == 0 else reversed(range(ngz))
        order.extend((x, z) for z in depths)
    return order


def chain(ngx, ngy, ngz):
    places = []
    order = snake(ngx, ngz)
    for y in range(ngy):
        for x, z in order if y % 2 == 0 else order[::-1]:
            places.append((x * ngy + y) * ngz + z)
    return places


def both_ways(places, pairs):
    pairs = [(places[a], places[b]) for a, b in pairs]
    return pairs + [(b, a) for a, b in pairs]


def hop_swaps(places, hop, odd):
    return both_ways(places, [(i, i + hop) for i in range(len(places) - hop) if i // hop % 2 == odd])


def run_swaps(places, run, start):
    pairs, rest = [], list(range(start))
    while start + run <= len(places):
        pairs.append((start, start + run - 1))
        pairs.extend((i, i + 1) for i in range(start + 1, start + run - 1, 2))
        start += run
    rest.extend(range(start, len(places)))
    pairs.extend((i, i + 1) for i in rest if i % 2 == 0)
    return both_ways(places, pairs)


def chain_place(ngx, ngz):
    x, y, z = lax.axis_index("gx"), lax.axis_index("gy"), lax.axis_index("gz")
    within = x * ngz + jnp.where(x % 2 == 0, z, ngz - 1 - z)
    group = ngx * ngz
    return y * group + jnp.where(y % 2 == 0, within, group - 1 - within)


def roll(value, shift, axis):
    size = value.shape[axis]
    shift = shift % size
    return value if shift == 0 else pltpu.roll(value, shift, axis)


def owner(table, c):
    forward = lax.axis_index("gy") % 2 == 0
    return jnp.where(forward, table[c], table[len(table) - 1 - c])


def pack_kernel(phase_ref, thermal_ref, velocity_ref, slope_ref, offset_ref, gain_ref, *outs, table, chunk, depth):
    out_ref, curves_ref, density_ref, kept_ref = outs
    zl, xl, yl = thermal_ref.shape
    density = (1.0 + 9.0 * phase_ref[...].astype(F32)) * thermal_ref[...]
    density_ref[...] = density
    kept_ref[...] = velocity_ref[...]
    for f in range(FIELDS):
        field = density if f == 0 else velocity_ref[f - 1]
        turned = field.reshape(zl * xl, yl).T
        for c in range(yl // chunk):
            rows = turned[c * chunk : (c + 1) * chunk]
            out_ref[owner(table, c), pl.ds(f, chunk, stride=FIELDS), :] = rows
    for t in range(curves_ref.shape[0]):
        curves_ref[t, 0:4, :] = jnp.broadcast_to(-LOG2E * slope_ref[:, t : t + 1], (4, LANES))
        curves_ref[t, 4:8, :] = jnp.broadcast_to(-LOG2E * offset_ref[:, t : t + 1], (4, LANES))
        curves_ref[t, 8:9, :] = jnp.broadcast_to(gain_ref[:, t : t + 1] / depth, (1, LANES))


class Slot:
    def __init__(self, zl, xl, chunk):
        self.width = 1
        while self.width < zl + xl:
            self.width *= 2
        groups = LANES // self.width
        self.faces = chunk
        self.deep = -(-chunk // groups)
        self.side = chunk + self.deep
        self.images = -(-(self.side + 1) // 8) * 8
        self.height = -(-(self.images + xl) // 8) * 8


def even_place(ngx, ngz, hop):
    return chain_place(ngx, ngz) // hop % 2 == 0


class Shifts:
    def __init__(self, ngx, ngz, zl, xl):
        self.ngx, self.ngz, self.zl, self.xl = ngx, ngz, zl, xl
        shape = (1, ngx * ngz, zl * xl)
        lane = lax.broadcasted_iota(jnp.int32, shape, 2)
        sub = lax.broadcasted_iota(jnp.int32, shape, 1)
        z, x = lane // xl, lane % xl
        gz, gx = sub // ngx, sub % ngx
        self.z_first, self.z_last = z == 0, z == zl - 1
        self.x_first, self.x_last = x == 0, x == xl - 1
        self.z_low = self.z_first & (gz == 0)
        self.z_high = self.z_last & (gz == ngz - 1)
        self.x_low = self.x_first & (gx == 0)
        self.x_high = self.x_last & (gx == ngx - 1)

    def below_z(self, f):
        near = roll(f, self.xl, 2)
        return jnp.where(self.z_first, roll(near, self.ngx, 1), near)

    def above_z(self, f):
        near = roll(f, -self.xl, 2)
        return jnp.where(self.z_last, roll(near, -self.ngx, 1), near)

    def below_x(self, f):
        far = roll(roll(f, 1 - self.xl, 2), 1, 1)
        return jnp.where(self.x_first, far, roll(f, 1, 2))

    def above_x(self, f):
        far = roll(roll(f, self.xl - 1, 2), -1, 1)
        return jnp.where(self.x_last, far, roll(f, -1, 2))


def divergence(move, velocity, after):
    vz, vx, vy = velocity
    out = -(jnp.where(move.z_high, 0.0, move.above_z(vz)) - vz)
    out = out - (jnp.where(move.x_high, 0.0, move.above_x(vx)) - vx)
    return out + vy if after is None else out - (after - vy)


def column_reader(own_ref, S, chunk):
    def read(k, f):
        return own_ref[pl.ds(k * FIELDS + f, S, stride=chunk * FIELDS), :][None]

    return read


def column(move, read, k, chunk):
    velocity = [read(k, f) for f in (1, 2, 3)]
    return velocity, divergence(move, velocity, read(k + 1, 3) if k + 1 < chunk else None)


def edges_kernel(own_ref, *out_refs, ngx, ngz, zl, xl, chunk, margin):
    move = Shifts(ngx, ngz, zl, xl)
    read = column_reader(own_ref, ngx * ngz, chunk)
    messages = []
    for start in (0, chunk - margin):
        planes = [read(k, 0) for k in range(start, start + margin)]
        planes += [column(move, read, k, chunk)[1] for k in range(start, start + margin)]
        messages.append(jnp.concatenate(planes + [read(0, 3)], axis=0))
    first, last = messages
    for h in range(len(out_refs) // 2):
        ahead_ref, behind_ref = out_refs[2 * h : 2 * h + 2]
        even = even_place(ngx, ngz, h + 1)

        @pl.when(even)
        def _():
            ahead_ref[...], behind_ref[...] = last, first

        @pl.when(jnp.logical_not(even))
        def _():
            ahead_ref[...], behind_ref[...] = first, last


def shared_faces(move, d):
    def face(missing, other):
        return 2.0 / (d + jnp.where(missing, d, other))

    return (
        face(move.z_low, move.below_z(d)),
        face(move.z_high, move.above_z(d)),
        face(move.x_low, move.below_x(d)),
        face(move.x_high, move.above_x(d)),
    )


class Operator:
    def __init__(self, move, coef, vec):
        self.move, self.coef, self.vec = move, coef, vec

    def set(self, a, b, faces, d, before, after, source, inside=None):
        move = self.move
        lz, uz, lx, ux = faces
        ly = 2.0 / (d + jnp.where(before > 0.0, before, d))
        uy = 2.0 / (d + jnp.where(after > 0.0, after, d))
        total = lz + uz + lx + ux + ly + uy
        inverse = 1.0 / total
        if inside is not None:
            inverse = jnp.where(inside, inverse, 0.0)
        self.coef[0, a:b] = jnp.where(move.z_low, 0.0, inverse * lz)
        self.coef[1, a:b] = jnp.where(move.z_high, 0.0, inverse * uz)
        self.coef[2, a:b] = jnp.where(move.x_low, 0.0, inverse * lx)
        self.coef[3, a:b] = jnp.where(move.x_high, 0.0, inverse * ux)
        self.coef[4, a:b] = inverse * ly
        self.coef[5, a:b] = inverse * uy
        self.vec[0, a:b] = inverse * source
        return total, ly

    def apply(self, k, a, b):
        move, coef, vec = self.move, self.coef, self.vec
        f = vec[k, a:b]
        out = coef[0, a:b] * move.below_z(f) + coef[1, a:b] * move.above_z(f)
        out = out + (coef[2, a:b] * move.below_x(f) + coef[3, a:b] * move.above_x(f))
        return out + (coef[4, a:b] * vec[k, a - 1 : b - 1] + coef[5, a:b] * vec[k, a + 1 : b + 1])

    def add_sums(self, sums, a, b, weight, right):
        basis = [self.vec[k, a:b] for k in range(ITERS)]
        basis.append(self.apply(ITERS - 1, a, b))
        gaps = [basis[k] - basis[k + 1] for k in range(ITERS)]
        scaled = [weight * gap for gap in gaps]
        terms = [basis[(k + 1) // 2] * scaled[k // 2] for k in range(2 * ITERS - 1)]
        terms += [right * basis[k] for k in range(ITERS)]
        ladder, level = [basis[0], gaps[0]], gaps
        while len(level) > 1:
            level = [level[i] - level[i + 1] for i in range(len(level) - 1)]
            ladder.append(level[0])
        terms += [weight * ladder[k // 2] * ladder[(k + 1) // 2] for k in range(2, 2 * ITERS)]
        return [total + jnp.sum(term, axis=0) for total, term in zip(sums, terms)]


SUMS = 2 * ITERS - 1 + ITERS + 2 * ITERS - 2


def pieces(a, b, step):
    return [(i, min(i + step, b)) for i in range(a, b, step)]


def inner(k, chunk):
    return (k + 1, chunk - 1 - k) if chunk - 1 - k > k + 1 else (0, 0)


def own_kernel(
    own_ref, home_ref, density_ref, source_ref, velocity_ref, faces_ref, coef_ref, vec_ref, diag_ref, side_ref, sums_ref, lower_ref,
    *, ngx, ngz, zl, xl, chunk, step
):
    move = Shifts(ngx, ngz, zl, xl)
    read = column_reader(own_ref, ngx * ngz, chunk)
    for k in range(chunk):
        d = read(k, 0)
        velocity, source = column(move, read, k, chunk)
        density_ref[k : k + 1], source_ref[k : k + 1] = d, source
        for f, v in enumerate(velocity):
            velocity_ref[f, k : k + 1] = v
        for f, v in enumerate(shared_faces(move, d)):
            faces_ref[f, k : k + 1] = v
    operator = Operator(move, coef_ref, vec_ref)
    for a, b in pieces(*inner(0, chunk), step):
        faces = [faces_ref[f, a:b] for f in range(4)]
        d, before, after = density_ref[a:b], density_ref[a - 1 : b - 1], density_ref[a + 1 : b + 1]
        diag_ref[a:b], side_ref[a:b] = operator.set(a, b, faces, d, before, after, source_ref[a:b])
    for k in range(1, ITERS):
        for a, b in pieces(*inner(k, chunk), step):
            vec_ref[k, a:b] = operator.apply(k - 1, a, b)
    sums = [jnp.zeros(sums_ref.shape[1:], F32)] * SUMS
    for a, b in pieces(*inner(ITERS, chunk), step):
        sums = operator.add_sums(sums, a, b, diag_ref[a:b], source_ref[a:b])
    for k, value in enumerate(sums):
        sums_ref[k] = value
    d = home_ref[...]
    lower_ref[0] = 2.0 / (d + jnp.concatenate([d[:1], d[:-1]], axis=0))
    lower_ref[1] = 2.0 / (d + roll(d, 1, 1))
    lower_ref[2] = 2.0 / (d + roll(d, 1, 2))


def krylov_kernel(*refs, ngx, ngz, zl, xl, chunk, hops, margin, step, places, runs):
    density_ref, source_ref, velocity_ref, faces_ref, own_coef, own_vec, own_diag, own_side, own_sums = refs[:9]
    count = 2 * hops + runs
    swapped = refs[9 : 9 + count]
    vec, lower_ref, sums_ref, sides, dens, coef, diag, source = refs[9 + count :]
    S, L = ngx * ngz, zl * xl
    E = chunk + 2 * HALO
    move = Shifts(ngx, ngz, zl, xl)

    place = chain_place(ngx, ngz)
    for h in range(hops):
        even = even_place(ngx, ngz, h + 1)
        sides[jnp.where(even, 1, 0), h] = swapped[2 * h][...]
        other = jnp.where(even, 0, 1)
        if not runs:
            sides[other, h] = swapped[2 * h + 1][...]
            continue
        within = place % (2 * S)
        border = (within == 0) | (within == 2 * S - 1)
        end = (place == 0) | (place == places - 1)

        @pl.when(jnp.logical_not(border))
        def _():
            sides[other, h] = swapped[1][...]

        @pl.when(border & jnp.logical_not(end))
        def _():
            sides[other, h] = swapped[2][...]

        @pl.when(end)
        def _():
            sides[other, h] = jnp.zeros(sides.shape[2:], F32)

    def ring(k):
        low, high = inner(k, chunk)
        if low == high:
            return pieces(1 + k, E - 1 - k, step)
        low, high = HALO + low, HALO + high
        return pieces(1 + k, low, step) + pieces(high, E - 1 - k, step)

    def outer(j, up):
        hop, at = j // chunk, j % chunk
        index = at if up else margin - 1 - at
        rhs = sides[up, hop, margin + index]
        if not up and at == 0:
            rhs = rhs - (velocity_ref[2, 0] if hop == 0 else sides[0, hop - 1, 2 * margin])
        if up and at == chunk - 1 and hop + 1 < hops:
            rhs = rhs - sides[1, hop + 1, 2 * margin]
        return sides[up, hop, index], rhs

    for j in range(HALO):
        dens[HALO - 1 - j], low_rhs = outer(j, 0)
        dens[HALO + chunk + j], high_rhs = outer(j, 1)
        source[HALO - 1 - j], source[HALO + chunk + j] = low_rhs, high_rhs
    dens[HALO : HALO + chunk] = density_ref[...]
    source[HALO : HALO + chunk] = source_ref[...]
    top = HALO + chunk - 1
    source[top] = source[top] - sides[1, 0, 2 * margin]
    for k in range(ITERS):
        a, b = inner(k, chunk)
        if a < b:
            vec[k, HALO + a : HALO + b] = own_vec[k, a:b]
    a, b = inner(0, chunk)
    if a < b:
        coef[:, HALO + a : HALO + b] = own_coef[:, a:b]
        lower_ref[a:b], diag[a:b] = own_side[a:b], own_diag[a:b]

    operator = Operator(move, coef, vec)
    for start, stop in ring(0):
        edges = sorted({start, stop, *(e for e in (HALO, HALO + chunk) if start < e < stop)})
        for a, b in zip(edges[:-1], edges[1:]):
            d, before, after = dens[a:b], dens[a - 1 : b - 1], dens[a + 1 : b + 1]
            if HALO <= a < HALO + chunk:
                own = slice(a - HALO, b - HALO)
                faces = [faces_ref[f, own] for f in range(4)]
                diag[own], lower_ref[own] = operator.set(a, b, faces, d, before, after, source[a:b])
            else:
                inside = d > 0.0
                d = jnp.where(inside, d, 1.0)
                operator.set(a, b, shared_faces(move, d), d, before, after, source[a:b], inside)
    for k in range(1, ITERS):
        for a, b in ring(k):
            vec[k, a:b] = operator.apply(k - 1, a, b)
    sums = [own_sums[k] for k in range(SUMS)]
    for a, b in ring(ITERS):
        sums = operator.add_sums(sums, a, b, diag[a - HALO : b - HALO], source[a:b])
    powers, firsts = sums[: 2 * ITERS - 1], sums[2 * ITERS - 1 : 3 * ITERS - 1]
    steps = [firsts[0], powers[0]] + sums[3 * ITERS - 1 :]

    columns = powers + firsts + steps
    rows = [jnp.sum(c, axis=0, keepdims=True) for c in columns]
    high = -(-len(rows) // 8) * 8
    rows = rows + [jnp.zeros((1, L), F32)] * (high - len(rows))
    sums = jnp.sum(jnp.concatenate(rows, axis=0), axis=1, keepdims=True)
    lane = lax.broadcasted_iota(jnp.int32, (high, LANES), 1)
    row = lax.broadcasted_iota(jnp.int32, (high, LANES), 0)
    line = jnp.sum(jnp.where(lane == row, sums, 0.0), axis=0, keepdims=True)
    sums_ref[...] = jnp.broadcast_to(line, sums_ref.shape)


def galerkin(sums):
    n, count = ITERS, 2 * ITERS - 1
    line = jnp.sum(sums, axis=0, keepdims=True)
    lane = lax.broadcasted_iota(jnp.int32, line.shape, 1)

    def pick(k):
        return jnp.sum(jnp.where(lane == k, line, 0.0), axis=1, keepdims=True)

    powers = [pick(k) for k in range(count)]
    firsts = [pick(count + k) for k in range(n)]
    steps = [pick(count + n + k) for k in range(count + 1)]
    matrix = [jnp.concatenate([powers[k], steps[k + 1]], axis=0) for k in range(count)]
    right = [jnp.concatenate([firsts[k], steps[k]], axis=0) for k in range(n)]
    low = [[None] * n for _ in range(n)]
    scale = [None] * n
    quality = None
    for j in range(n):
        pivot = matrix[2 * j]
        for k in range(j):
            pivot = pivot - low[j][k] * low[j][k] * scale[k][0]
        share = pivot / matrix[2 * j]
        fine = share > 1e-7
        quality = jnp.where(fine, share, 0.0) if quality is None else jnp.minimum(quality, jnp.where(fine, share, 0.0))
        inverse = jnp.where(fine, 1.0 / pivot, 0.0)
        scale[j] = (pivot, inverse)
        for r in range(j + 1, n):
            entry = matrix[r + j]
            for k in range(j):
                entry = entry - low[r][k] * low[j][k] * scale[k][0]
            low[r][j] = entry * inverse
    part = list(right)
    for r in range(n):
        for k in range(r):
            part[r] = part[r] - low[r][k] * part[k]
    part = [part[r] * scale[r][1] for r in range(n)]
    for r in reversed(range(n)):
        for k in range(r + 1, n):
            part[r] = part[r] - low[k][r] * part[k]
    first = quality[0:1] >= quality[1:2]
    by_power = [jnp.where(first, p[0:1], 0.0) for p in part]
    by_step = [jnp.where(first, 0.0, p[1:2]) for p in part]
    return by_power, by_step


def render_kernel(
    sums_ref, basis_ref, faces_ref, lower_ref, velocity_ref, table_ref, out_ref, press, flat, turned, parts,
    *, ngx, ngz, zl, xl, chunk, step
):
    S, L = ngx * ngz, zl * xl
    yl = S * chunk
    slot = Slot(zl, xl, chunk)
    height = slot.height
    move = Shifts(ngx, ngz, zl, xl)
    by_power, by_step = galerkin(sums_ref[...])
    by_power = [v.reshape(1, 1, 1) for v in by_power]
    by_step = [v.reshape(1, 1, 1) for v in by_step]
    for a in range(0, chunk + 1, step):
        b = min(a + step, chunk + 1)
        level = [basis_ref[k, HALO - 1 + a : HALO - 1 + b] for k in range(ITERS)]
        value = 0.0
        for k in range(ITERS):
            value = value + by_power[k] * level[k]
        value = value + by_step[0] * level[0]
        for k in range(1, ITERS):
            level = [level[i] - level[i + 1] for i in range(len(level) - 1)]
            value = value + by_step[k] * level[0]
        press[a:b] = value
    spot = lax.broadcasted_iota(jnp.int32, (S, L), 1)
    sides = [jnp.zeros((S, L), F32) for _ in range(slot.deep)]
    for a in range(0, chunk, step):
        b = min(a + step, chunk)
        p = press[a + 1 : b + 1]
        fronts = (
            jnp.where(move.z_low, 0.0, move.below_z(p)),
            jnp.where(move.x_low, 0.0, move.below_x(p)),
            press[a:b],
        )
        pieces = []
        for k, front in enumerate(fronts):
            lower = lower_ref[a:b] if k == 2 else faces_ref[2 * k, a:b]
            pieces.append(velocity_ref[k, a:b] - lower * (p - front))
        scalar = pieces[0] + pieces[1] + pieces[2]
        if a == 0:
            out_ref[pl.ds(slot.side, S, stride=height), :] = pieces[2][0]
        for c in range(a, b):
            out_ref[pl.ds(c, S, stride=height), :] = p[c - a]
            flat[pl.ds(c, S, stride=chunk), :] = scalar[c - a]
            base = c // slot.deep * slot.width
            deep = roll(pieces[0][c - a], base, 1)
            where = (spot - (base + xl)) * xl
            wide = jnp.take_along_axis(pieces[1][c - a], jnp.clip(where, 0, L - 1), axis=1, mode="promise_in_bounds")
            r = c % slot.deep
            sides[r] = jnp.where(spot >= base, jnp.where(spot >= base + xl, wide, deep), sides[r])
    for r, side in enumerate(sides):
        out_ref[pl.ds(slot.faces + r, S, stride=height), :] = side
    turned[...] = flat[...].T.reshape(zl, xl, yl)

    group = ngx * chunk
    band = LANES // 4
    functions = table_ref.shape[0] // ngz
    lane = lax.broadcasted_iota(jnp.int32, (xl, yl), 1)

    def curve_sums(index, carry):
        rows = [jnp.broadcast_to(table_ref[index, r : r + 1, :], (xl, yl)) for r in range(9)]
        rates, bases, gain = rows[:4], rows[4:8], rows[8]
        through = jnp.ones((xl, yl), F32)
        colors = [jnp.zeros((xl, yl), F32) for _ in range(3)]
        for z in range(zl):
            x = turned[z]
            curves = [1.0 / (1.0 + jnp.exp2(rates[c] * x + bases[c])) for c in range(4)]
            opacity = gain * curves[3]
            weight = through * opacity
            colors = [colors[c] + weight * curves[c] for c in range(3)]
            through = through * (1.0 - opacity)
        for c, value in enumerate(colors + [through]):
            parts[index, c] = value
        return carry

    lax.fori_loop(0, table_ref.shape[0], curve_sums, 0)
    for i in range(ngz):
        images = [jnp.zeros((xl, LANES), F32) for _ in range(ngx)]
        for t in range(functions):
            planes = [parts[i * functions + t, c] for c in range(4)]
            span = 1
            while span < ngz:
                behind = [roll(plane, -span * group, 1) for plane in planes]
                planes = [planes[c] + planes[3] * behind[c] for c in range(3)] + [planes[3] * behind[3]]
                span *= 2
            planes[3] = 1.0 - planes[3]
            merged = planes[0]
            for c in range(1, 4):
                merged = jnp.where(lane >= c * band, roll(planes[c], c * band, 1), merged)
            for k in range(ngx):
                here = (lane % band) // chunk == t
                images[k] = jnp.where(here, roll(merged, (t - k) * chunk, 1), images[k])
        for k in range(ngx):
            place = (i * ngx + k) * height + slot.images
            out_ref[place : place + xl, :] = images[k]


def unpack_kernel(in_ref, lower_ref, velocity_ref, corrected_ref, images_ref, flat, sides, *, table, chunk):
    zl, xl, yl = corrected_ref.shape[1:]
    slot = Slot(zl, xl, chunk)
    functions = images_ref.shape[0]
    band = LANES // 4
    lane = lax.broadcasted_iota(jnp.int32, (xl, yl), 1)
    images = [jnp.zeros((xl, yl), F32) for _ in range(functions * 4)]
    for c in range(yl // chunk):
        place = owner(table, c)
        flat[c * chunk : (c + 1) * chunk, :] = in_ref[place, :chunk, :]
        faces = in_ref[place, slot.faces : slot.faces + 8, :]
        for g in range(-(-chunk // slot.deep)):
            rows = min(slot.deep, chunk - g * slot.deep)
            start = c * chunk + g * slot.deep
            sides[start : start + rows, :] = roll(faces, -g * slot.width, 1)[:rows]
        source = in_ref[place, slot.images : slot.images + xl, :]
        here = (lane >= c * chunk) & (lane < (c + 1) * chunk)
        for k in range(functions * 4):
            shift = c * chunk - (k % 4 * band + k // 4 * chunk)
            images[k] = jnp.where(here, roll(source, shift, 1), images[k])
    for k, image in enumerate(images):
        images_ref[k // 4, k % 4] = image
    p = flat[...].T.reshape(zl, xl, yl)
    faces = sides[...].T
    deep, wide = faces[:xl], faces[xl : xl + zl]
    front = in_ref[owner(table, 0), slot.side : slot.side + 1, :]
    high = jnp.broadcast_to(front, (yl, zl * xl)).T.reshape(zl, xl, yl)
    x = lax.broadcasted_iota(jnp.int32, (zl, xl, yl), 1)
    y = lax.broadcasted_iota(jnp.int32, (zl, xl, yl), 2)
    inner = velocity_ref[0, 1:] - lower_ref[0, 1:] * (p[1:] - p[:-1])
    corrected_ref[0, 0], corrected_ref[0, 1:] = deep, inner
    inner = velocity_ref[1] - lower_ref[1] * (p - roll(p, 1, 1))
    corrected_ref[1] = jnp.where(x == 0, wide[:, None, :], inner)
    inner = velocity_ref[2] - lower_ref[2] * (p - roll(p, 1, 2))
    corrected_ref[2] = jnp.where(y == 0, high, inner)


def solution(mesh):
    ngx, ngy, ngz = mesh.shape["gx"], mesh.shape["gy"], mesh.shape["gz"]
    S, devices = ngx * ngz, ngx * ngy * ngz
    table = [z * ngx + x for x, z in snake(ngx, ngz)]
    places = chain(ngx, ngy, ngz)

    def local(phase_field, thermal, velocity, transfer_slope, transfer_offset, transfer_gain):
        zl, xl, yl = thermal.shape
        L, chunk = zl * xl, yl // S
        functions = transfer_slope.shape[0] // ngz
        assert yl % S == 0 and L == LANES and yl == LANES and max(ngx, functions) * 4 * chunk <= LANES
        assert ngz & (ngz - 1) == 0
        hops = -(-HALO // chunk)
        margin = min(chunk, HALO)
        step = max(1, 4 * 8 // S)

        vmem = pl.BlockSpec(memory_space=pltpu.VMEM)

        def call(body, specs, out, scratch=(), limit=None, **kwargs):
            kernel = pl.pallas_call(
                lambda *refs: body(*refs, **kwargs),
                in_specs=specs,
                out_specs=jax.tree.map(lambda _: vmem, out),
                out_shape=out,
                scratch_shapes=[pltpu.VMEM(s, F32) for s in scratch],
                compiler_params=pltpu.CompilerParams(vmem_limit_bytes=limit),
                name=body.__name__,
            )

            def run(*args):
                return kernel(*[near(a) if spec is vmem else a for a, spec in zip(args, specs)])

            return run

        def near(array):
            return pltpu.with_memory_space_constraint(array, pltpu.VMEM)

        def shaped(*shape):
            return jax.ShapeDtypeStruct(shape, F32)

        def placed(*shape):
            return pltpu.VMEM(shape, F32)

        free = pl.BlockSpec()
        tables = (transfer_slope.T, transfer_offset.T, transfer_gain[None, :])
        block = (zl, xl, yl)
        blocks, curves, home_density, kept = call(
            pack_kernel,
            [free] * 6,
            (placed(S, chunk * FIELDS, L), placed(transfer_gain.shape[0], 16, LANES), placed(*block), placed(3, *block)),
            table=table, chunk=chunk, depth=zl * ngz,
        )(phase_field, thermal, velocity, *tables)
        pencils = lax.all_to_all(blocks, ("gz", "gx"), 0, 0, tiled=True)
        every = ("gx", "gy", "gz")
        own = pencils.reshape(-1, L)
        sizes = dict(ngx=ngx, ngz=ngz, zl=zl, xl=xl, chunk=chunk)
        message = (2 * margin + 1, S, L)
        messages = call(edges_kernel, [vmem], [placed(*message)] * (2 * hops), margin=margin, **sizes)(own)
        swaps = [(messages[i], hop_swaps(places, i // 2 + 1, i % 2)) for i in range(2 * hops)]
        runs = hops == 1 and ngy % 2 == 0 and S % 2 == 0
        if runs:
            swaps = [swaps[0]] + [(messages[1], run_swaps(places, 2 * S, start)) for start in (0, S)]
        swapped = [lax.ppermute(value, every, pairs) for value, pairs in swaps[::-1]][::-1]
        *own_values, home_lower = call(
            own_kernel,
            [vmem] * 2,
            (
                *[placed(*lead, chunk, S, L) for lead in ((), (), (3,), (4,), (6,), (ITERS,), (), ())],
                placed(SUMS, S, L),
                placed(3, *block),
            ),
            limit=VMEM_LIMIT, step=step, **sizes,
        )(own, home_density)
        velocities, faces = own_values[2:4]
        wide = chunk + 2 * HALO
        basis, lower, sums = call(
            krylov_kernel,
            [vmem] * (9 + len(swapped)),
            (placed(ITERS, wide, S, L), placed(chunk, S, L), placed(devices, LANES)),
            ((2, hops) + message, (wide, S, L), (6, wide, S, L), (chunk, S, L), (wide, S, L)),
            limit=VMEM_LIMIT, hops=hops, margin=margin, step=step, places=devices, runs=int(runs), **sizes,
        )(*own_values, *swapped)
        sums = lax.all_to_all(sums, every, 0, 0, tiled=True)
        height = Slot(zl, xl, chunk).height
        packed = call(
            render_kernel,
            [vmem] * 6,
            placed(S * height, LANES),
            ((chunk + 1, S, L), (yl, L), (zl, xl, yl), (curves.shape[0], 4, xl, yl)),
            step=step, **sizes,
        )(sums, basis, faces, lower, velocities, curves)
        home = lax.all_to_all(packed.reshape(S, height, LANES), ("gz", "gx"), 0, 0, tiled=True)
        return call(
            unpack_kernel,
            [vmem] * 3,
            (shaped(3, *block), shaped(functions, 4, xl, yl)),
            ((yl, L), (yl, LANES)),
            table=table, chunk=chunk,
        )(home, home_lower, kept)

    return jax.shard_map(
        local,
        mesh=mesh,
        in_specs=(P("gz", "gx", "gy"), P("gz", "gx", "gy"), P(None, "gz", "gx", "gy"), P(), P(), P()),
        out_specs=(P(None, "gz", "gx", "gy"), P("gz", None, "gx", "gy")),
        check_vma=False,
    )
```

```python
import math

import jax
import jax.numpy as jnp
from jax import lax
from jax.experimental import pallas as pl
from jax.experimental.pallas import tpu as pltpu
from jax.sharding import PartitionSpec as P

ITERS = 4
HALO = ITERS + 1
FIELDS = 4
LANES = 128
VMEM_LIMIT = 24 << 20
LOG2E = math.log2(math.e)
F32 = jnp.float32


def snake(ngx, ngz):
    order = []
    for x in range(ngx):
        depths = range(ngz) if x % 2 == 0 else reversed(range(ngz))
        order.extend((x, z) for z in depths)
    return order


def chain(ngx, ngy, ngz):
    places = []
    order = snake(ngx, ngz)
    for y in range(ngy):
        for x, z in order if y % 2 == 0 else order[::-1]:
            places.append((x * ngy + y) * ngz + z)
    return places


def both_ways(places, pairs):
    pairs = [(places[a], places[b]) for a, b in pairs]
    return pairs + [(b, a) for a, b in pairs]


def hop_swaps(places, hop, odd):
    return both_ways(places, [(i, i + hop) for i in range(len(places) - hop) if i // hop % 2 == odd])


def run_swaps(places, run, start):
    pairs, rest = [], list(range(start))
    while start + run <= len(places):
        pairs.append((start, start + run - 1))
        pairs.extend((i, i + 1) for i in range(start + 1, start + run - 1, 2))
        start += run
    rest.extend(range(start, len(places)))
    pairs.extend((i, i + 1) for i in rest if i % 2 == 0)
    return both_ways(places, pairs)


def chain_place(ngx, ngz):
    x, y, z = lax.axis_index("gx"), lax.axis_index("gy"), lax.axis_index("gz")
    within = x * ngz + jnp.where(x % 2 == 0, z, ngz - 1 - z)
    group = ngx * ngz
    return y * group + jnp.where(y % 2 == 0, within, group - 1 - within)


def roll(value, shift, axis):
    size = value.shape[axis]
    shift = shift % size
    return value if shift == 0 else pltpu.roll(value, shift, axis)


def owner(table, c):
    forward = lax.axis_index("gy") % 2 == 0
    return jnp.where(forward, table[c], table[len(table) - 1 - c])


def pack_kernel(phase_ref, thermal_ref, velocity_ref, slope_ref, offset_ref, gain_ref, *outs, table, chunk, depth):
    out_ref, curves_ref, density_ref, kept_ref = outs
    zl, xl, yl = thermal_ref.shape
    density = (1.0 + 9.0 * phase_ref[...].astype(F32)) * thermal_ref[...]
    density_ref[...] = density
    kept_ref[...] = velocity_ref[...]
    for f in range(FIELDS):
        field = density if f == 0 else velocity_ref[f - 1]
        turned = field.reshape(zl * xl, yl).T
        for c in range(yl // chunk):
            rows = turned[c * chunk : (c + 1) * chunk]
            out_ref[owner(table, c), pl.ds(f, chunk, stride=FIELDS), :] = rows
    for t in range(curves_ref.shape[0]):
        curves_ref[t, 0:4, :] = jnp.broadcast_to(-LOG2E * slope_ref[:, t : t + 1], (4, LANES))
        curves_ref[t, 4:8, :] = jnp.broadcast_to(-LOG2E * offset_ref[:, t : t + 1], (4, LANES))
        curves_ref[t, 8:9, :] = jnp.broadcast_to(gain_ref[:, t : t + 1] / depth, (1, LANES))


class Slot:
    def __init__(self, zl, xl, chunk):
        self.width = 1
        while self.width < zl + xl:
            self.width *= 2
        groups = LANES // self.width
        self.faces = chunk
        self.deep = -(-chunk // groups)
        self.side = chunk + self.deep
        self.images = -(-(self.side + 1) // 8) * 8
        self.height = -(-(self.images + xl) // 8) * 8


def even_place(ngx, ngz, hop):
    return chain_place(ngx, ngz) // hop % 2 == 0


class Shifts:
    def __init__(self, ngx, ngz, zl, xl):
        self.ngx, self.ngz, self.zl, self.xl = ngx, ngz, zl, xl
        shape = (1, ngx * ngz, zl * xl)
        lane = lax.broadcasted_iota(jnp.int32, shape, 2)
        sub = lax.broadcasted_iota(jnp.int32, shape, 1)
        z, x = lane // xl, lane % xl
        gz, gx = sub // ngx, sub % ngx
        self.z_first, self.z_last = z == 0, z == zl - 1
        self.x_first, self.x_last = x == 0, x == xl - 1
        self.z_low = self.z_first & (gz == 0)
        self.z_high = self.z_last & (gz == ngz - 1)
        self.x_low = self.x_first & (gx == 0)
        self.x_high = self.x_last & (gx == ngx - 1)

    def below_z(self, f):
        near = roll(f, self.xl, 2)
        return jnp.where(self.z_first, roll(near, self.ngx, 1), near)

    def above_z(self, f):
        near = roll(f, -self.xl, 2)
        return jnp.where(self.z_last, roll(near, -self.ngx, 1), near)

    def below_x(self, f):
        far = roll(roll(f, 1 - self.xl, 2), 1, 1)
        return jnp.where(self.x_first, far, roll(f, 1, 2))

    def above_x(self, f):
        far = roll(roll(f, self.xl - 1, 2), -1, 1)
        return jnp.where(self.x_last, far, roll(f, -1, 2))


def divergence(move, velocity, after):
    vz, vx, vy = velocity
    out = -(jnp.where(move.z_high, 0.0, move.above_z(vz)) - vz)
    out = out - (jnp.where(move.x_high, 0.0, move.above_x(vx)) - vx)
    return out + vy if after is None else out - (after - vy)


def column_reader(own_ref, S, chunk):
    def read(k, f):
        return own_ref[pl.ds(k * FIELDS + f, S, stride=chunk * FIELDS), :][None]

    return read


def column(move, read, k, chunk):
    velocity = [read(k, f) for f in (1, 2, 3)]
    return velocity, divergence(move, velocity, read(k + 1, 3) if k + 1 < chunk else None)


def edges_kernel(own_ref, *out_refs, ngx, ngz, zl, xl, chunk, margin):
    move = Shifts(ngx, ngz, zl, xl)
    read = column_reader(own_ref, ngx * ngz, chunk)
    messages = []
    for start in (0, chunk - margin):
        planes = [read(k, 0) for k in range(start, start + margin)]
        planes += [column(move, read, k, chunk)[1] for k in range(start, start + margin)]
        messages.append(jnp.concatenate(planes + [read(0, 3)], axis=0))
    first, last = messages
    for h in range(len(out_refs) // 2):
        ahead_ref, behind_ref = out_refs[2 * h : 2 * h + 2]
        even = even_place(ngx, ngz, h + 1)

        @pl.when(even)
        def _():
            ahead_ref[...], behind_ref[...] = last, first

        @pl.when(jnp.logical_not(even))
        def _():
            ahead_ref[...], behind_ref[...] = first, last


def shared_faces(move, d):
    def face(missing, other):
        return 2.0 / (d + jnp.where(missing, d, other))

    return (
        face(move.z_low, move.below_z(d)),
        face(move.z_high, move.above_z(d)),
        face(move.x_low, move.below_x(d)),
        face(move.x_high, move.above_x(d)),
    )


def differences(levels):
    basis, gaps = [], []
    while len(levels) > 1:
        basis.append(levels[0])
        gaps.append(levels[1])
        levels = [levels[i] - levels[i + 1] for i in range(len(levels) - 1)]
    return basis + levels, gaps


class Operator:
    def __init__(self, move, coef, vec):
        self.move, self.coef, self.vec = move, coef, vec

    def set(self, a, b, faces, d, before, after, source, inside=None):
        move = self.move
        lz, uz, lx, ux = faces
        ly = 2.0 / (d + jnp.where(before > 0.0, before, d))
        uy = 2.0 / (d + jnp.where(after > 0.0, after, d))
        total = lz + uz + lx + ux + ly + uy
        inverse = 1.0 / total
        if inside is not None:
            inverse = jnp.where(inside, inverse, 0.0)
        self.coef[0, a:b] = jnp.where(move.z_low, 0.0, inverse * lz)
        self.coef[1, a:b] = jnp.where(move.z_high, 0.0, inverse * uz)
        self.coef[2, a:b] = jnp.where(move.x_low, 0.0, inverse * lx)
        self.coef[3, a:b] = jnp.where(move.x_high, 0.0, inverse * ux)
        self.coef[4, a:b] = inverse * ly
        self.coef[5, a:b] = inverse * uy
        rim = jnp.where(move.z_low, lz, 0.0) + jnp.where(move.z_high, uz, 0.0)
        rim = rim + (jnp.where(move.x_low, lx, 0.0) + jnp.where(move.x_high, ux, 0.0))
        self.coef[6, a:b] = inverse * rim
        self.vec[0, a:b] = inverse * source
        return total, ly

    def apply(self, k, a, b):
        move, coef, vec = self.move, self.coef, self.vec
        f = vec[k, a:b]
        out = coef[0, a:b] * (f - move.below_z(f)) + coef[1, a:b] * (f - move.above_z(f))
        out = out + (coef[2, a:b] * (f - move.below_x(f)) + coef[3, a:b] * (f - move.above_x(f)))
        out = out + (coef[4, a:b] * (f - vec[k, a - 1 : b - 1]) + coef[5, a:b] * (f - vec[k, a + 1 : b + 1]))
        return out + coef[6, a:b] * f

    def add_sums(self, sums, a, b, weight, right):
        levels = [self.vec[k, a:b] for k in range(ITERS)]
        levels.append(self.apply(ITERS - 1, a, b))
        basis, gaps = differences(levels)
        scaled = [weight * gap for gap in gaps]
        terms = [basis[(k + 1) // 2] * scaled[k // 2] for k in range(2 * ITERS - 1)]
        terms += [right * basis[k] for k in range(ITERS)]
        terms += [weight * levels[k // 2] * levels[(k + 1) // 2] for k in range(2, 2 * ITERS)]
        return [total + jnp.sum(term, axis=0) for total, term in zip(sums, terms)]


SUMS = 2 * ITERS - 1 + ITERS + 2 * ITERS - 2


def pieces(a, b, step):
    return [(i, min(i + step, b)) for i in range(a, b, step)]


def inner(k, chunk):
    return (k + 1, chunk - 1 - k) if chunk - 1 - k > k + 1 else (0, 0)


def own_kernel(
    own_ref, home_ref, density_ref, source_ref, velocity_ref, faces_ref, coef_ref, vec_ref, diag_ref, side_ref, sums_ref, lower_ref,
    *, ngx, ngz, zl, xl, chunk, step
):
    move = Shifts(ngx, ngz, zl, xl)
    read = column_reader(own_ref, ngx * ngz, chunk)
    for k in range(chunk):
        d = read(k, 0)
        velocity, source = column(move, read, k, chunk)
        density_ref[k : k + 1], source_ref[k : k + 1] = d, source
        for f, v in enumerate(velocity):
            velocity_ref[f, k : k + 1] = v
        for f, v in enumerate(shared_faces(move, d)):
            faces_ref[f, k : k + 1] = v
    operator = Operator(move, coef_ref, vec_ref)
    for a, b in pieces(*inner(0, chunk), step):
        faces = [faces_ref[f, a:b] for f in range(4)]
        d, before, after = density_ref[a:b], density_ref[a - 1 : b - 1], density_ref[a + 1 : b + 1]
        diag_ref[a:b], side_ref[a:b] = operator.set(a, b, faces, d, before, after, source_ref[a:b])
    for k in range(1, ITERS):
        for a, b in pieces(*inner(k, chunk), step):
            vec_ref[k, a:b] = operator.apply(k - 1, a, b)
    sums = [jnp.zeros(sums_ref.shape[1:], F32)] * SUMS
    for a, b in pieces(*inner(ITERS, chunk), step):
        sums = operator.add_sums(sums, a, b, diag_ref[a:b], source_ref[a:b])
    for k, value in enumerate(sums):
        sums_ref[k] = value
    d = home_ref[...]
    lower_ref[0] = 2.0 / (d + jnp.concatenate([d[:1], d[:-1]], axis=0))
    lower_ref[1] = 2.0 / (d + roll(d, 1, 1))
    lower_ref[2] = 2.0 / (d + roll(d, 1, 2))


def krylov_kernel(*refs, ngx, ngz, zl, xl, chunk, hops, margin, step, places, runs):
    density_ref, source_ref, velocity_ref, faces_ref, own_coef, own_vec, own_diag, own_side, own_sums = refs[:9]
    count = 2 * hops + runs
    swapped = refs[9 : 9 + count]
    vec, lower_ref, sums_ref, sides, dens, coef, diag, source = refs[9 + count :]
    S, L = ngx * ngz, zl * xl
    E = chunk + 2 * HALO
    move = Shifts(ngx, ngz, zl, xl)

    place = chain_place(ngx, ngz)
    for h in range(hops):
        even = even_place(ngx, ngz, h + 1)
        sides[jnp.where(even, 1, 0), h] = swapped[2 * h][...]
        other = jnp.where(even, 0, 1)
        if not runs:
            sides[other, h] = swapped[2 * h + 1][...]
            continue
        within = place % (2 * S)
        border = (within == 0) | (within == 2 * S - 1)
        end = (place == 0) | (place == places - 1)

        @pl.when(jnp.logical_not(border))
        def _():
            sides[other, h] = swapped[1][...]

        @pl.when(border & jnp.logical_not(end))
        def _():
            sides[other, h] = swapped[2][...]

        @pl.when(end)
        def _():
            sides[other, h] = jnp.zeros(sides.shape[2:], F32)

    def ring(k):
        low, high = inner(k, chunk)
        if low == high:
            return pieces(1 + k, E - 1 - k, step)
        low, high = HALO + low, HALO + high
        return pieces(1 + k, low, step) + pieces(high, E - 1 - k, step)

    def outer(j, up):
        hop, at = j // chunk, j % chunk
        index = at if up else margin - 1 - at
        rhs = sides[up, hop, margin + index]
        if not up and at == 0:
            rhs = rhs - (velocity_ref[2, 0] if hop == 0 else sides[0, hop - 1, 2 * margin])
        if up and at == chunk - 1 and hop + 1 < hops:
            rhs = rhs - sides[1, hop + 1, 2 * margin]
        return sides[up, hop, index], rhs

    for j in range(HALO):
        dens[HALO - 1 - j], low_rhs = outer(j, 0)
        dens[HALO + chunk + j], high_rhs = outer(j, 1)
        source[HALO - 1 - j], source[HALO + chunk + j] = low_rhs, high_rhs
    dens[HALO : HALO + chunk] = density_ref[...]
    source[HALO : HALO + chunk] = source_ref[...]
    top = HALO + chunk - 1
    source[top] = source[top] - sides[1, 0, 2 * margin]
    for k in range(ITERS):
        a, b = inner(k, chunk)
        if a < b:
            vec[k, HALO + a : HALO + b] = own_vec[k, a:b]
    a, b = inner(0, chunk)
    if a < b:
        coef[:, HALO + a : HALO + b] = own_coef[:, a:b]
        lower_ref[a:b], diag[a:b] = own_side[a:b], own_diag[a:b]

    operator = Operator(move, coef, vec)
    for start, stop in ring(0):
        edges = sorted({start, stop, *(e for e in (HALO, HALO + chunk) if start < e < stop)})
        for a, b in zip(edges[:-1], edges[1:]):
            d, before, after = dens[a:b], dens[a - 1 : b - 1], dens[a + 1 : b + 1]
            if HALO <= a < HALO + chunk:
                own = slice(a - HALO, b - HALO)
                faces = [faces_ref[f, own] for f in range(4)]
                diag[own], lower_ref[own] = operator.set(a, b, faces, d, before, after, source[a:b])
            else:
                inside = d > 0.0
                d = jnp.where(inside, d, 1.0)
                operator.set(a, b, shared_faces(move, d), d, before, after, source[a:b], inside)
    for k in range(1, ITERS):
        for a, b in ring(k):
            vec[k, a:b] = operator.apply(k - 1, a, b)
    sums = [own_sums[k] for k in range(SUMS)]
    for a, b in ring(ITERS):
        sums = operator.add_sums(sums, a, b, diag[a - HALO : b - HALO], source[a:b])
    powers, firsts = sums[: 2 * ITERS - 1], sums[2 * ITERS - 1 : 3 * ITERS - 1]
    steps = [firsts[0], powers[0]] + sums[3 * ITERS - 1 :]

    columns = powers + firsts + steps
    rows = [jnp.sum(c, axis=0, keepdims=True) for c in columns]
    high = -(-len(rows) // 8) * 8
    rows = rows + [jnp.zeros((1, L), F32)] * (high - len(rows))
    sums = jnp.sum(jnp.concatenate(rows, axis=0), axis=1, keepdims=True)
    lane = lax.broadcasted_iota(jnp.int32, (high, LANES), 1)
    row = lax.broadcasted_iota(jnp.int32, (high, LANES), 0)
    line = jnp.sum(jnp.where(lane == row, sums, 0.0), axis=0, keepdims=True)
    sums_ref[...] = jnp.broadcast_to(line, sums_ref.shape)


def galerkin(sums):
    n, count = ITERS, 2 * ITERS - 1
    line = jnp.sum(sums, axis=0, keepdims=True)
    lane = lax.broadcasted_iota(jnp.int32, line.shape, 1)

    def pick(k):
        return jnp.sum(jnp.where(lane == k, line, 0.0), axis=1, keepdims=True)

    powers = [pick(k) for k in range(count)]
    firsts = [pick(count + k) for k in range(n)]
    steps = [pick(count + n + k) for k in range(count + 1)]
    matrix = [jnp.concatenate([powers[k], steps[k + 1]], axis=0) for k in range(count)]
    right = [jnp.concatenate([firsts[k], steps[k]], axis=0) for k in range(n)]
    low = [[None] * n for _ in range(n)]
    scale = [None] * n
    quality = None
    for j in range(n):
        pivot = matrix[2 * j]
        for k in range(j):
            pivot = pivot - low[j][k] * low[j][k] * scale[k][0]
        share = pivot / matrix[2 * j]
        fine = share > 1e-7
        quality = jnp.where(fine, share, 0.0) if quality is None else jnp.minimum(quality, jnp.where(fine, share, 0.0))
        inverse = jnp.where(fine, 1.0 / pivot, 0.0)
        scale[j] = (pivot, inverse)
        for r in range(j + 1, n):
            entry = matrix[r + j]
            for k in range(j):
                entry = entry - low[r][k] * low[j][k] * scale[k][0]
            low[r][j] = entry * inverse
    part = list(right)
    for r in range(n):
        for k in range(r):
            part[r] = part[r] - low[r][k] * part[k]
    part = [part[r] * scale[r][1] for r in range(n)]
    for r in reversed(range(n)):
        for k in range(r + 1, n):
            part[r] = part[r] - low[k][r] * part[k]
    first = quality[0:1] >= quality[1:2]
    by_power = [jnp.where(first, p[0:1], 0.0) for p in part]
    by_step = [jnp.where(first, 0.0, p[1:2]) for p in part]
    return by_power, by_step


def render_kernel(
    sums_ref, vec_ref, faces_ref, lower_ref, velocity_ref, table_ref, out_ref, press, flat, turned,
    *, ngx, ngz, zl, xl, chunk, step
):
    S, L = ngx * ngz, zl * xl
    yl = S * chunk
    slot = Slot(zl, xl, chunk)
    height = slot.height
    move = Shifts(ngx, ngz, zl, xl)
    by_power, by_step = galerkin(sums_ref[...])
    by_power = [v.reshape(1, 1, 1) for v in by_power]
    by_step = [v.reshape(1, 1, 1) for v in by_step]
    for a in range(0, chunk + 1, step):
        b = min(a + step, chunk + 1)
        levels = [vec_ref[k, HALO - 1 + a : HALO - 1 + b] for k in range(ITERS)]
        basis = differences(levels)[0]
        value = 0.0
        for k in range(ITERS):
            value = value + by_power[k] * basis[k] + by_step[k] * levels[k]
        press[a:b] = value
    spot = lax.broadcasted_iota(jnp.int32, (S, L), 1)
    sides = [jnp.zeros((S, L), F32) for _ in range(slot.deep)]
    for a in range(0, chunk, step):
        b = min(a + step, chunk)
        p = press[a + 1 : b + 1]
        fronts = (
            jnp.where(move.z_low, 0.0, move.below_z(p)),
            jnp.where(move.x_low, 0.0, move.below_x(p)),
            press[a:b],
        )
        pieces = []
        for k, front in enumerate(fronts):
            lower = lower_ref[a:b] if k == 2 else faces_ref[2 * k, a:b]
            pieces.append(velocity_ref[k, a:b] - lower * (p - front))
        scalar = pieces[0] + pieces[1] + pieces[2]
        if a == 0:
            out_ref[pl.ds(slot.side, S, stride=height), :] = pieces[2][0]
        for c in range(a, b):
            out_ref[pl.ds(c, S, stride=height), :] = p[c - a]
            flat[pl.ds(c, S, stride=chunk), :] = scalar[c - a]
            base = c // slot.deep * slot.width
            deep = roll(pieces[0][c - a], base, 1)
            where = (spot - (base + xl)) * xl
            wide = jnp.take_along_axis(pieces[1][c - a], jnp.clip(where, 0, L - 1), axis=1, mode="promise_in_bounds")
            r = c % slot.deep
            sides[r] = jnp.where(spot >= base, jnp.where(spot >= base + xl, wide, deep), sides[r])
    for r, side in enumerate(sides):
        out_ref[pl.ds(slot.faces + r, S, stride=height), :] = side
    turned[...] = flat[...].T.reshape(zl, xl, yl)

    group = ngx * chunk
    band = LANES // 4
    functions = table_ref.shape[0] // ngz
    lane = lax.broadcasted_iota(jnp.int32, (xl, yl), 1)

    def curve_sums(index):
        rows = [jnp.broadcast_to(table_ref[index, r : r + 1, :], (xl, yl)) for r in range(9)]
        rates, bases, gain = rows[:4], rows[4:8], rows[8]
        through = jnp.ones((xl, yl), F32)
        colors = [jnp.zeros((xl, yl), F32) for _ in range(3)]
        for z in range(zl):
            x = turned[z]
            curves = [1.0 / (1.0 + jnp.exp2(rates[c] * x + bases[c])) for c in range(4)]
            opacity = gain * curves[3]
            weight = through * opacity
            colors = [colors[c] + weight * curves[c] for c in range(3)]
            through = through * (1.0 - opacity)
        return colors + [through]

    for i in range(ngz):
        images = [jnp.zeros((xl, LANES), F32) for _ in range(ngx)]
        for t in range(functions):
            planes = curve_sums(i * functions + t)
            span = 1
            while span < ngz:
                behind = [roll(plane, -span * group, 1) for plane in planes]
                planes = [planes[c] + planes[3] * behind[c] for c in range(3)] + [planes[3] * behind[3]]
                span *= 2
            planes[3] = 1.0 - planes[3]
            merged = planes[0]
            for c in range(1, 4):
                merged = jnp.where(lane >= c * band, roll(planes[c], c * band, 1), merged)
            for k in range(ngx):
                here = (lane % band) // chunk == t
                images[k] = jnp.where(here, roll(merged, (t - k) * chunk, 1), images[k])
        for k in range(ngx):
            place = (i * ngx + k) * height + slot.images
            out_ref[place : place + xl, :] = images[k]


def unpack_kernel(in_ref, lower_ref, velocity_ref, corrected_ref, images_ref, flat, sides, *, table, chunk):
    zl, xl, yl = corrected_ref.shape[1:]
    slot = Slot(zl, xl, chunk)
    functions = images_ref.shape[0]
    band = LANES // 4
    lane = lax.broadcasted_iota(jnp.int32, (xl, yl), 1)
    images = [jnp.zeros((xl, yl), F32) for _ in range(functions * 4)]
    for c in range(yl // chunk):
        place = owner(table, c)
        flat[c * chunk : (c + 1) * chunk, :] = in_ref[place, :chunk, :]
        faces = in_ref[place, slot.faces : slot.faces + 8, :]
        for g in range(-(-chunk // slot.deep)):
            rows = min(slot.deep, chunk - g * slot.deep)
            start = c * chunk + g * slot.deep
            sides[start : start + rows, :] = roll(faces, -g * slot.width, 1)[:rows]
        source = in_ref[place, slot.images : slot.images + xl, :]
        here = (lane >= c * chunk) & (lane < (c + 1) * chunk)
        for k in range(functions * 4):
            shift = c * chunk - (k % 4 * band + k // 4 * chunk)
            images[k] = jnp.where(here, roll(source, shift, 1), images[k])
    for k, image in enumerate(images):
        images_ref[k // 4, k % 4] = image
    p = flat[...].T.reshape(zl, xl, yl)
    faces = sides[...].T
    deep, wide = faces[:xl], faces[xl : xl + zl]
    front = in_ref[owner(table, 0), slot.side : slot.side + 1, :]
    high = jnp.broadcast_to(front, (yl, zl * xl)).T.reshape(zl, xl, yl)
    x = lax.broadcasted_iota(jnp.int32, (zl, xl, yl), 1)
    y = lax.broadcasted_iota(jnp.int32, (zl, xl, yl), 2)
    inner = velocity_ref[0, 1:] - lower_ref[0, 1:] * (p[1:] - p[:-1])
    corrected_ref[0, 0], corrected_ref[0, 1:] = deep, inner
    inner = velocity_ref[1] - lower_ref[1] * (p - roll(p, 1, 1))
    corrected_ref[1] = jnp.where(x == 0, wide[:, None, :], inner)
    inner = velocity_ref[2] - lower_ref[2] * (p - roll(p, 1, 2))
    corrected_ref[2] = jnp.where(y == 0, high, inner)


def solution(mesh):
    ngx, ngy, ngz = mesh.shape["gx"], mesh.shape["gy"], mesh.shape["gz"]
    S, devices = ngx * ngz, ngx * ngy * ngz
    table = [z * ngx + x for x, z in snake(ngx, ngz)]
    places = chain(ngx, ngy, ngz)

    def local(phase_field, thermal, velocity, transfer_slope, transfer_offset, transfer_gain):
        zl, xl, yl = thermal.shape
        L, chunk = zl * xl, yl // S
        functions = transfer_slope.shape[0] // ngz
        assert yl % S == 0 and L == LANES and yl == LANES and max(ngx, functions) * 4 * chunk <= LANES
        assert ngz & (ngz - 1) == 0
        hops = -(-HALO // chunk)
        margin = min(chunk, HALO)
        step = max(1, 4 * 8 // S)

        vmem = pl.BlockSpec(memory_space=pltpu.VMEM)

        def call(body, specs, out, scratch=(), limit=None, **kwargs):
            kernel = pl.pallas_call(
                lambda *refs: body(*refs, **kwargs),
                in_specs=specs,
                out_specs=jax.tree.map(lambda _: vmem, out),
                out_shape=out,
                scratch_shapes=[pltpu.VMEM(s, F32) for s in scratch],
                compiler_params=pltpu.CompilerParams(vmem_limit_bytes=limit),
                name=body.__name__,
            )

            def run(*args):
                return kernel(*[near(a) if spec is vmem else a for a, spec in zip(args, specs)])

            return run

        def near(array):
            return pltpu.with_memory_space_constraint(array, pltpu.VMEM)

        def shaped(*shape):
            return jax.ShapeDtypeStruct(shape, F32)

        def placed(*shape):
            return pltpu.VMEM(shape, F32)

        free = pl.BlockSpec()
        tables = (transfer_slope.T, transfer_offset.T, transfer_gain[None, :])
        block = (zl, xl, yl)
        blocks, curves, home_density, kept = call(
            pack_kernel,
            [free] * 6,
            (placed(S, chunk * FIELDS, L), placed(transfer_gain.shape[0], 16, LANES), placed(*block), placed(3, *block)),
            table=table, chunk=chunk, depth=zl * ngz,
        )(phase_field, thermal, velocity, *tables)
        pencils = lax.all_to_all(blocks, ("gz", "gx"), 0, 0, tiled=True)
        every = ("gx", "gy", "gz")
        own = pencils.reshape(-1, L)
        sizes = dict(ngx=ngx, ngz=ngz, zl=zl, xl=xl, chunk=chunk)
        message = (2 * margin + 1, S, L)
        messages = call(edges_kernel, [vmem], [placed(*message)] * (2 * hops), margin=margin, **sizes)(own)
        swaps = [(messages[i], hop_swaps(places, i // 2 + 1, i % 2)) for i in range(2 * hops)]
        runs = hops == 1 and ngy % 2 == 0 and S % 2 == 0
        if runs:
            swaps = [swaps[0]] + [(messages[1], run_swaps(places, 2 * S, start)) for start in (0, S)]
        swapped = [lax.ppermute(value, every, pairs) for value, pairs in swaps[::-1]][::-1]
        *own_values, home_lower = call(
            own_kernel,
            [vmem] * 2,
            (
                *[placed(*lead, chunk, S, L) for lead in ((), (), (3,), (4,), (7,), (ITERS,), (), ())],
                placed(SUMS, S, L),
                placed(3, *block),
            ),
            limit=VMEM_LIMIT, step=step, **sizes,
        )(own, home_density)
        velocities, faces = own_values[2:4]
        wide = chunk + 2 * HALO
        levels, lower, sums = call(
            krylov_kernel,
            [vmem] * (9 + len(swapped)),
            (placed(ITERS, wide, S, L), placed(chunk, S, L), placed(devices, LANES)),
            ((2, hops) + message, (wide, S, L), (7, wide, S, L), (chunk, S, L), (wide, S, L)),
            limit=VMEM_LIMIT, hops=hops, margin=margin, step=step, places=devices, runs=int(runs), **sizes,
        )(*own_values, *swapped)
        sums = lax.all_to_all(sums, every, 0, 0, tiled=True)
        height = Slot(zl, xl, chunk).height
        packed = call(
            render_kernel,
            [vmem] * 6,
            placed(S * height, LANES),
            ((chunk + 1, S, L), (yl, L), (zl, xl, yl)),
            step=step, **sizes,
        )(sums, levels, faces, lower, velocities, curves)
        home = lax.all_to_all(packed.reshape(S, height, LANES), ("gz", "gx"), 0, 0, tiled=True)
        return call(
            unpack_kernel,
            [vmem] * 3,
            (shaped(3, *block), shaped(functions, 4, xl, yl)),
            ((yl, L), (yl, LANES)),
            table=table, chunk=chunk,
        )(home, home_lower, kept)

    return jax.shard_map(
        local,
        mesh=mesh,
        in_specs=(P("gz", "gx", "gy"), P("gz", "gx", "gy"), P(None, "gz", "gx", "gy"), P(), P(), P()),
        out_specs=(P(None, "gz", "gx", "gy"), P("gz", None, "gx", "gy")),
        check_vma=False,
    )
```

```python
import math

import jax
import jax.numpy as jnp
from jax import lax
from jax.experimental import pallas as pl
from jax.experimental.pallas import tpu as pltpu
from jax.sharding import PartitionSpec as P


ITERS = 4
HALO = ITERS + 1
FIELDS = 4
LANES = 128
VMEM_LIMIT = 24 << 20
LOG2E = math.log2(math.e)
F32 = jnp.float32


def snake(ngx, ngz):
    order = []
    for x in range(ngx):
        depths = range(ngz) if x % 2 == 0 else reversed(range(ngz))
        order.extend((x, z) for z in depths)
    return order


def chain(ngx, ngy, ngz):
    places = []
    order = snake(ngx, ngz)
    for y in range(ngy):
        for x, z in order if y % 2 == 0 else order[::-1]:
            places.append((x * ngy + y) * ngz + z)
    return places


def both_ways(places, pairs):
    pairs = [(places[a], places[b]) for a, b in pairs]
    return pairs + [(b, a) for a, b in pairs]


def hop_swaps(places, hop, odd):
    return both_ways(places, [(i, i + hop) for i in range(len(places) - hop) if i // hop % 2 == odd])


def run_swaps(places, run, start):
    pairs, rest = [], list(range(start))
    while start + run <= len(places):
        pairs.append((start, start + run - 1))
        pairs.extend((i, i + 1) for i in range(start + 1, start + run - 1, 2))
        start += run
    rest.extend(range(start, len(places)))
    pairs.extend((i, i + 1) for i in rest if i % 2 == 0)
    return both_ways(places, pairs)


def chain_place(ngx, ngz):
    x, y, z = lax.axis_index("gx"), lax.axis_index("gy"), lax.axis_index("gz")
    within = x * ngz + jnp.where(x % 2 == 0, z, ngz - 1 - z)
    group = ngx * ngz
    return y * group + jnp.where(y % 2 == 0, within, group - 1 - within)


def roll(value, shift, axis):
    size = value.shape[axis]
    shift = shift % size
    return value if shift == 0 else pltpu.roll(value, shift, axis)


def owner(table, c):
    forward = lax.axis_index("gy") % 2 == 0
    return jnp.where(forward, table[c], table[len(table) - 1 - c])


def pack_kernel(phase_ref, thermal_ref, velocity_ref, slope_ref, offset_ref, gain_ref, *outs, table, chunk, depth):
    out_ref, curves_ref, density_ref, kept_ref = outs
    zl, xl, yl = thermal_ref.shape
    density = (1.0 + 9.0 * phase_ref[...].astype(F32)) * thermal_ref[...]
    density_ref[...] = density
    kept_ref[...] = velocity_ref[...]
    for f in range(FIELDS):
        field = density if f == 0 else velocity_ref[f - 1]
        turned = field.reshape(zl * xl, yl).T
        for c in range(yl // chunk):
            rows = turned[c * chunk : (c + 1) * chunk]
            out_ref[owner(table, c), pl.ds(f, chunk, stride=FIELDS), :] = rows
    for t in range(curves_ref.shape[0]):
        curves_ref[t, 0:4, :] = jnp.broadcast_to(-LOG2E * slope_ref[:, t : t + 1], (4, LANES))
        curves_ref[t, 4:8, :] = jnp.broadcast_to(-LOG2E * offset_ref[:, t : t + 1], (4, LANES))
        curves_ref[t, 8:9, :] = jnp.broadcast_to(gain_ref[:, t : t + 1] / depth, (1, LANES))


class Slot:
    def __init__(self, zl, xl, chunk):
        self.width = 1
        while self.width < zl + xl:
            self.width *= 2
        groups = LANES // self.width
        self.faces = chunk
        self.deep = -(-chunk // groups)
        self.side = chunk + self.deep
        self.images = -(-(self.side + 1) // 8) * 8
        self.height = -(-(self.images + xl) // 8) * 8


def even_place(ngx, ngz, hop):
    return chain_place(ngx, ngz) // hop % 2 == 0


class Shifts:
    def __init__(self, ngx, ngz, zl, xl):
        self.ngx, self.ngz, self.zl, self.xl = ngx, ngz, zl, xl
        shape = (1, ngx * ngz, zl * xl)
        lane = lax.broadcasted_iota(jnp.int32, shape, 2)
        sub = lax.broadcasted_iota(jnp.int32, shape, 1)
        z, x = lane // xl, lane % xl
        gz, gx = sub // ngx, sub % ngx
        self.z_first, self.z_last = z == 0, z == zl - 1
        self.x_first, self.x_last = x == 0, x == xl - 1
        self.z_low = self.z_first & (gz == 0)
        self.z_high = self.z_last & (gz == ngz - 1)
        self.x_low = self.x_first & (gx == 0)
        self.x_high = self.x_last & (gx == ngx - 1)

    def below_z(self, f):
        near = roll(f, self.xl, 2)
        return jnp.where(self.z_first, roll(near, self.ngx, 1), near)

    def above_z(self, f):
        near = roll(f, -self.xl, 2)
        return jnp.where(self.z_last, roll(near, -self.ngx, 1), near)

    def below_x(self, f):
        far = roll(roll(f, 1 - self.xl, 2), 1, 1)
        return jnp.where(self.x_first, far, roll(f, 1, 2))

    def above_x(self, f):
        far = roll(roll(f, self.xl - 1, 2), -1, 1)
        return jnp.where(self.x_last, far, roll(f, -1, 2))


def divergence(move, velocity, after):
    vz, vx, vy = velocity
    out = -(jnp.where(move.z_high, 0.0, move.above_z(vz)) - vz)
    out = out - (jnp.where(move.x_high, 0.0, move.above_x(vx)) - vx)
    return out + vy if after is None else out - (after - vy)


def column_reader(own_ref, S, chunk):
    def read(k, f):
        return own_ref[pl.ds(k * FIELDS + f, S, stride=chunk * FIELDS), :][None]

    return read


def column(move, read, k, chunk):
    velocity = [read(k, f) for f in (1, 2, 3)]
    return velocity, divergence(move, velocity, read(k + 1, 3) if k + 1 < chunk else None)


def edges_kernel(own_ref, *out_refs, ngx, ngz, zl, xl, chunk, margin):
    move = Shifts(ngx, ngz, zl, xl)
    read = column_reader(own_ref, ngx * ngz, chunk)
    messages = []
    for start in (0, chunk - margin):
        planes = [read(k, 0) for k in range(start, start + margin)]
        planes += [column(move, read, k, chunk)[1] for k in range(start, start + margin)]
        messages.append(jnp.concatenate(planes + [read(0, 3)], axis=0))
    first, last = messages
    for h in range(len(out_refs) // 2):
        ahead_ref, behind_ref = out_refs[2 * h : 2 * h + 2]
        even = even_place(ngx, ngz, h + 1)

        @pl.when(even)
        def _():
            ahead_ref[...], behind_ref[...] = last, first

        @pl.when(jnp.logical_not(even))
        def _():
            ahead_ref[...], behind_ref[...] = first, last


def shared_faces(move, d):
    def face(missing, other):
        return 2.0 / (d + jnp.where(missing, d, other))

    return (
        face(move.z_low, move.below_z(d)),
        face(move.z_high, move.above_z(d)),
        face(move.x_low, move.below_x(d)),
        face(move.x_high, move.above_x(d)),
    )


def differences(levels):
    basis, gaps = [], []
    while len(levels) > 1:
        basis.append(levels[0])
        gaps.append(levels[1])
        levels = [levels[i] - levels[i + 1] for i in range(len(levels) - 1)]
    return basis + levels, gaps


class Operator:
    def __init__(self, move, coef, vec):
        self.move, self.coef, self.vec = move, coef, vec

    def set(self, a, b, faces, d, before, after, source, inside=None):
        move = self.move
        lz, uz, lx, ux = faces
        ly = 2.0 / (d + jnp.where(before > 0.0, before, d))
        uy = 2.0 / (d + jnp.where(after > 0.0, after, d))
        total = lz + uz + lx + ux + ly + uy
        inverse = 1.0 / total
        if inside is not None:
            inverse = jnp.where(inside, inverse, 0.0)
        self.coef[0, a:b] = jnp.where(move.z_low, 0.0, inverse * lz)
        self.coef[1, a:b] = jnp.where(move.z_high, 0.0, inverse * uz)
        self.coef[2, a:b] = jnp.where(move.x_low, 0.0, inverse * lx)
        self.coef[3, a:b] = jnp.where(move.x_high, 0.0, inverse * ux)
        self.coef[4, a:b] = inverse * ly
        self.coef[5, a:b] = inverse * uy
        rim = jnp.where(move.z_low, lz, 0.0) + jnp.where(move.z_high, uz, 0.0)
        rim = rim + (jnp.where(move.x_low, lx, 0.0) + jnp.where(move.x_high, ux, 0.0))
        self.coef[6, a:b] = inverse * rim
        self.vec[0, a:b] = inverse * source
        return total, ly

    def apply(self, k, a, b):
        move, coef, vec = self.move, self.coef, self.vec
        f = vec[k, a:b]
        out = coef[0, a:b] * (f - move.below_z(f)) + coef[1, a:b] * (f - move.above_z(f))
        out = out + (coef[2, a:b] * (f - move.below_x(f)) + coef[3, a:b] * (f - move.above_x(f)))
        out = out + (coef[4, a:b] * (f - vec[k, a - 1 : b - 1]) + coef[5, a:b] * (f - vec[k, a + 1 : b + 1]))
        return out + coef[6, a:b] * f

    def add_sums(self, sums, a, b, weight, right):
        levels = [self.vec[k, a:b] for k in range(ITERS)]
        levels.append(self.apply(ITERS - 1, a, b))
        basis, gaps = differences(levels)
        scaled = [weight * gap for gap in gaps]
        terms = [basis[(k + 1) // 2] * scaled[k // 2] for k in range(2 * ITERS - 1)]
        terms += [right * basis[k] for k in range(ITERS)]
        terms += [weight * levels[k // 2] * levels[(k + 1) // 2] for k in range(2, 2 * ITERS)]
        return [total + jnp.sum(term, axis=0) for total, term in zip(sums, terms)]


SUMS = 2 * ITERS - 1 + ITERS + 2 * ITERS - 2


def pieces(a, b, step):
    return [(i, min(i + step, b)) for i in range(a, b, step)]


def inner(k, chunk):
    return (k + 1, chunk - 1 - k) if chunk - 1 - k > k + 1 else (0, 0)


def own_kernel(
    own_ref, home_ref, density_ref, source_ref, velocity_ref, faces_ref, coef_ref, vec_ref, diag_ref, side_ref, sums_ref, lower_ref,
    *, ngx, ngz, zl, xl, chunk, step
):
    move = Shifts(ngx, ngz, zl, xl)
    read = column_reader(own_ref, ngx * ngz, chunk)
    for k in range(chunk):
        d = read(k, 0)
        velocity, source = column(move, read, k, chunk)
        density_ref[k : k + 1], source_ref[k : k + 1] = d, source
        for f, v in enumerate(velocity):
            velocity_ref[f, k : k + 1] = v
        for f, v in enumerate(shared_faces(move, d)):
            faces_ref[f, k : k + 1] = v
    operator = Operator(move, coef_ref, vec_ref)
    for a, b in pieces(*inner(0, chunk), step):
        faces = [faces_ref[f, a:b] for f in range(4)]
        d, before, after = density_ref[a:b], density_ref[a - 1 : b - 1], density_ref[a + 1 : b + 1]
        diag_ref[a:b], side_ref[a:b] = operator.set(a, b, faces, d, before, after, source_ref[a:b])
    for k in range(1, ITERS):
        for a, b in pieces(*inner(k, chunk), step):
            vec_ref[k, a:b] = operator.apply(k - 1, a, b)
    sums = [jnp.zeros(sums_ref.shape[1:], F32)] * SUMS
    for a, b in pieces(*inner(ITERS, chunk), step):
        sums = operator.add_sums(sums, a, b, diag_ref[a:b], source_ref[a:b])
    for k, value in enumerate(sums):
        sums_ref[k] = value
    d = home_ref[...]
    lower_ref[0] = 2.0 / (d + jnp.concatenate([d[:1], d[:-1]], axis=0))
    lower_ref[1] = 2.0 / (d + roll(d, 1, 1))
    lower_ref[2] = 2.0 / (d + roll(d, 1, 2))


def krylov_kernel(*refs, ngx, ngz, zl, xl, chunk, hops, margin, step, places, runs):
    density_ref, source_ref, velocity_ref, faces_ref, own_coef, own_vec, own_diag, own_side, own_sums = refs[:9]
    count = 2 * hops + runs
    swapped = refs[9 : 9 + count]
    vec, lower_ref, sums_ref, sides, dens, coef, diag, source = refs[9 + count :]
    S, L = ngx * ngz, zl * xl
    E = chunk + 2 * HALO
    move = Shifts(ngx, ngz, zl, xl)

    place = chain_place(ngx, ngz)
    for h in range(hops):
        even = even_place(ngx, ngz, h + 1)
        sides[jnp.where(even, 1, 0), h] = swapped[2 * h][...]
        other = jnp.where(even, 0, 1)
        if not runs:
            sides[other, h] = swapped[2 * h + 1][...]
            continue
        within = place % (2 * S)
        border = (within == 0) | (within == 2 * S - 1)
        end = (place == 0) | (place == places - 1)

        @pl.when(jnp.logical_not(border))
        def _():
            sides[other, h] = swapped[1][...]

        @pl.when(border & jnp.logical_not(end))
        def _():
            sides[other, h] = swapped[2][...]

        @pl.when(end)
        def _():
            sides[other, h] = jnp.zeros(sides.shape[2:], F32)

    def ring(k):
        low, high = inner(k, chunk)
        if low == high:
            return pieces(1 + k, E - 1 - k, step)
        low, high = HALO + low, HALO + high
        return pieces(1 + k, low, step) + pieces(high, E - 1 - k, step)

    def outer(j, up):
        hop, at = j // chunk, j % chunk
        index = at if up else margin - 1 - at
        rhs = sides[up, hop, margin + index]
        if not up and at == 0:
            rhs = rhs - (velocity_ref[2, 0] if hop == 0 else sides[0, hop - 1, 2 * margin])
        if up and at == chunk - 1 and hop + 1 < hops:
            rhs = rhs - sides[1, hop + 1, 2 * margin]
        return sides[up, hop, index], rhs

    for j in range(HALO):
        dens[HALO - 1 - j], low_rhs = outer(j, 0)
        dens[HALO + chunk + j], high_rhs = outer(j, 1)
        source[HALO - 1 - j], source[HALO + chunk + j] = low_rhs, high_rhs
    dens[HALO : HALO + chunk] = density_ref[...]
    source[HALO : HALO + chunk] = source_ref[...]
    top = HALO + chunk - 1
    source[top] = source[top] - sides[1, 0, 2 * margin]
    for k in range(ITERS):
        a, b = inner(k, chunk)
        if a < b:
            vec[k, HALO + a : HALO + b] = own_vec[k, a:b]
    a, b = inner(0, chunk)
    if a < b:
        coef[:, HALO + a : HALO + b] = own_coef[:, a:b]
        lower_ref[a:b], diag[a:b] = own_side[a:b], own_diag[a:b]

    operator = Operator(move, coef, vec)
    for start, stop in ring(0):
        edges = sorted({start, stop, *(e for e in (HALO, HALO + chunk) if start < e < stop)})
        for a, b in zip(edges[:-1], edges[1:]):
            d, before, after = dens[a:b], dens[a - 1 : b - 1], dens[a + 1 : b + 1]
            if HALO <= a < HALO + chunk:
                own = slice(a - HALO, b - HALO)
                faces = [faces_ref[f, own] for f in range(4)]
                diag[own], lower_ref[own] = operator.set(a, b, faces, d, before, after, source[a:b])
            else:
                inside = d > 0.0
                d = jnp.where(inside, d, 1.0)
                operator.set(a, b, shared_faces(move, d), d, before, after, source[a:b], inside)
    for k in range(1, ITERS):
        for a, b in ring(k):
            vec[k, a:b] = operator.apply(k - 1, a, b)
    sums = [own_sums[k] for k in range(SUMS)]
    for a, b in ring(ITERS):
        sums = operator.add_sums(sums, a, b, diag[a - HALO : b - HALO], source[a:b])
    powers, firsts = sums[: 2 * ITERS - 1], sums[2 * ITERS - 1 : 3 * ITERS - 1]
    steps = [firsts[0], powers[0]] + sums[3 * ITERS - 1 :]

    columns = powers + firsts + steps
    rows = [jnp.sum(c, axis=0, keepdims=True) for c in columns]
    high = -(-len(rows) // 8) * 8
    rows = rows + [jnp.zeros((1, L), F32)] * (high - len(rows))
    sums = jnp.sum(jnp.concatenate(rows, axis=0), axis=1, keepdims=True)
    lane = lax.broadcasted_iota(jnp.int32, (high, LANES), 1)
    row = lax.broadcasted_iota(jnp.int32, (high, LANES), 0)
    line = jnp.sum(jnp.where(lane == row, sums, 0.0), axis=0, keepdims=True)
    sums_ref[...] = jnp.broadcast_to(line, sums_ref.shape)


def galerkin(sums):
    n, count = ITERS, 2 * ITERS - 1
    line = jnp.sum(sums, axis=0, keepdims=True)
    lane = lax.broadcasted_iota(jnp.int32, line.shape, 1)

    def pick(k):
        return jnp.sum(jnp.where(lane == k, line, 0.0), axis=1, keepdims=True)

    powers = [pick(k) for k in range(count)]
    firsts = [pick(count + k) for k in range(n)]
    steps = [pick(count + n + k) for k in range(count + 1)]
    matrix = [jnp.concatenate([powers[k], steps[k + 1]], axis=0) for k in range(count)]
    right = [jnp.concatenate([firsts[k], steps[k]], axis=0) for k in range(n)]
    low = [[None] * n for _ in range(n)]
    scale = [None] * n
    quality = None
    for j in range(n):
        pivot = matrix[2 * j]
        for k in range(j):
            pivot = pivot - low[j][k] * low[j][k] * scale[k][0]
        share = pivot / matrix[2 * j]
        fine = share > 1e-7
        quality = jnp.where(fine, share, 0.0) if quality is None else jnp.minimum(quality, jnp.where(fine, share, 0.0))
        inverse = jnp.where(fine, 1.0 / pivot, 0.0)
        scale[j] = (pivot, inverse)
        for r in range(j + 1, n):
            entry = matrix[r + j]
            for k in range(j):
                entry = entry - low[r][k] * low[j][k] * scale[k][0]
            low[r][j] = entry * inverse
    part = list(right)
    for r in range(n):
        for k in range(r):
            part[r] = part[r] - low[r][k] * part[k]
    part = [part[r] * scale[r][1] for r in range(n)]
    for r in reversed(range(n)):
        for k in range(r + 1, n):
            part[r] = part[r] - low[k][r] * part[k]
    first = quality[0:1] >= quality[1:2]
    by_power = [jnp.where(first, p[0:1], 0.0) for p in part]
    by_step = [jnp.where(first, 0.0, p[1:2]) for p in part]
    return by_power, by_step


def render_kernel(
    sums_ref, vec_ref, faces_ref, lower_ref, velocity_ref, table_ref, out_ref, press, flat, turned,
    *, ngx, ngz, zl, xl, chunk, step
):
    S, L = ngx * ngz, zl * xl
    yl = S * chunk
    slot = Slot(zl, xl, chunk)
    height = slot.height
    move = Shifts(ngx, ngz, zl, xl)
    by_power, by_step = galerkin(sums_ref[...])
    by_power = [v.reshape(1, 1, 1) for v in by_power]
    by_step = [v.reshape(1, 1, 1) for v in by_step]
    for a in range(0, chunk + 1, step):
        b = min(a + step, chunk + 1)
        levels = [vec_ref[k, HALO - 1 + a : HALO - 1 + b] for k in range(ITERS)]
        basis = differences(levels)[0]
        value = 0.0
        for k in range(ITERS):
            value = value + by_power[k] * basis[k] + by_step[k] * levels[k]
        press[a:b] = value
    spot = lax.broadcasted_iota(jnp.int32, (S, L), 1)
    sides = [jnp.zeros((S, L), F32) for _ in range(slot.deep)]
    for a in range(0, chunk, step):
        b = min(a + step, chunk)
        p = press[a + 1 : b + 1]
        fronts = (
            jnp.where(move.z_low, 0.0, move.below_z(p)),
            jnp.where(move.x_low, 0.0, move.below_x(p)),
            press[a:b],
        )
        pieces = []
        for k, front in enumerate(fronts):
            lower = lower_ref[a:b] if k == 2 else faces_ref[2 * k, a:b]
            pieces.append(velocity_ref[k, a:b] - lower * (p - front))
        scalar = pieces[0] + pieces[1] + pieces[2]
        if a == 0:
            out_ref[pl.ds(slot.side, S, stride=height), :] = pieces[2][0]
        for c in range(a, b):
            out_ref[pl.ds(c, S, stride=height), :] = p[c - a]
            flat[pl.ds(c, S, stride=chunk), :] = scalar[c - a]
            base = c // slot.deep * slot.width
            deep = roll(pieces[0][c - a], base, 1)
            where = (spot - (base + xl)) * xl
            wide = jnp.take_along_axis(pieces[1][c - a], jnp.clip(where, 0, L - 1), axis=1, mode="promise_in_bounds")
            r = c % slot.deep
            sides[r] = jnp.where(spot >= base, jnp.where(spot >= base + xl, wide, deep), sides[r])
    for r, side in enumerate(sides):
        out_ref[pl.ds(slot.faces + r, S, stride=height), :] = side
    turned[...] = flat[...].T.reshape(zl, xl, yl)

    group = ngx * chunk
    band = LANES // 4
    functions = table_ref.shape[0] // ngz
    lane = lax.broadcasted_iota(jnp.int32, (xl, yl), 1)

    def curve_sums(index):
        rows = [jnp.broadcast_to(table_ref[index, r : r + 1, :], (xl, yl)) for r in range(9)]
        rates, bases, gain = rows[:4], rows[4:8], rows[8]
        through = jnp.ones((xl, yl), F32)
        colors = [jnp.zeros((xl, yl), F32) for _ in range(3)]
        for z in range(zl):
            x = turned[z]
            curves = [1.0 / (1.0 + jnp.exp2(rates[c] * x + bases[c])) for c in range(4)]
            opacity = gain * curves[3]
            weight = through * opacity
            colors = [colors[c] + weight * curves[c] for c in range(3)]
            through = through * (1.0 - opacity)
        return colors + [through]

    for i in range(ngz):
        images = [jnp.zeros((xl, LANES), F32) for _ in range(ngx)]
        for t in range(functions):
            planes = curve_sums(i * functions + t)
            span = 1
            while span < ngz:
                behind = [roll(plane, -span * group, 1) for plane in planes]
                planes = [planes[c] + planes[3] * behind[c] for c in range(3)] + [planes[3] * behind[3]]
                span *= 2
            planes[3] = 1.0 - planes[3]
            merged = planes[0]
            for c in range(1, 4):
                merged = jnp.where(lane >= c * band, roll(planes[c], c * band, 1), merged)
            for k in range(ngx):
                here = (lane % band) // chunk == t
                images[k] = jnp.where(here, roll(merged, (t - k) * chunk, 1), images[k])
        for k in range(ngx):
            place = (i * ngx + k) * height + slot.images
            out_ref[place : place + xl, :] = images[k]


def unpack_kernel(in_ref, lower_ref, velocity_ref, corrected_ref, images_ref, flat, sides, *, table, chunk):
    zl, xl, yl = corrected_ref.shape[1:]
    slot = Slot(zl, xl, chunk)
    functions = images_ref.shape[0]
    band = LANES // 4
    lane = lax.broadcasted_iota(jnp.int32, (xl, yl), 1)
    images = [jnp.zeros((xl, yl), F32) for _ in range(functions * 4)]
    for c in range(yl // chunk):
        place = owner(table, c)
        flat[c * chunk : (c + 1) * chunk, :] = in_ref[place, :chunk, :]
        faces = in_ref[place, slot.faces : slot.faces + 8, :]
        for g in range(-(-chunk // slot.deep)):
            rows = min(slot.deep, chunk - g * slot.deep)
            start = c * chunk + g * slot.deep
            sides[start : start + rows, :] = roll(faces, -g * slot.width, 1)[:rows]
        source = in_ref[place, slot.images : slot.images + xl, :]
        here = (lane >= c * chunk) & (lane < (c + 1) * chunk)
        for k in range(functions * 4):
            shift = c * chunk - (k % 4 * band + k // 4 * chunk)
            images[k] = jnp.where(here, roll(source, shift, 1), images[k])
    for k, image in enumerate(images):
        images_ref[k // 4, k % 4] = image
    p = flat[...].T.reshape(zl, xl, yl)
    faces = sides[...].T
    deep, wide = faces[:xl], faces[xl : xl + zl]
    front = in_ref[owner(table, 0), slot.side : slot.side + 1, :]
    high = jnp.broadcast_to(front, (yl, zl * xl)).T.reshape(zl, xl, yl)
    x = lax.broadcasted_iota(jnp.int32, (zl, xl, yl), 1)
    y = lax.broadcasted_iota(jnp.int32, (zl, xl, yl), 2)
    inner = velocity_ref[0, 1:] - lower_ref[0, 1:] * (p[1:] - p[:-1])
    corrected_ref[0, 0], corrected_ref[0, 1:] = deep, inner
    inner = velocity_ref[1] - lower_ref[1] * (p - roll(p, 1, 1))
    corrected_ref[1] = jnp.where(x == 0, wide[:, None, :], inner)
    inner = velocity_ref[2] - lower_ref[2] * (p - roll(p, 1, 2))
    corrected_ref[2] = jnp.where(y == 0, high, inner)


def solution(mesh):
    ngx, ngy, ngz = mesh.shape["gx"], mesh.shape["gy"], mesh.shape["gz"]
    S, devices = ngx * ngz, ngx * ngy * ngz
    table = [z * ngx + x for x, z in snake(ngx, ngz)]
    places = chain(ngx, ngy, ngz)

    def local(phase_field, thermal, velocity, transfer_slope, transfer_offset, transfer_gain):
        zl, xl, yl = thermal.shape
        L, chunk = zl * xl, yl // S
        functions = transfer_slope.shape[0] // ngz
        assert yl % S == 0 and L == LANES and yl == LANES and max(ngx, functions) * 4 * chunk <= LANES
        assert ngz & (ngz - 1) == 0
        hops = -(-HALO // chunk)
        margin = min(chunk, HALO)
        step = max(1, 4 * 8 // S)

        vmem = pl.BlockSpec(memory_space=pltpu.VMEM)

        def call(body, specs, out, scratch=(), limit=None, **kwargs):
            kernel = pl.pallas_call(
                lambda *refs: body(*refs, **kwargs),
                in_specs=specs,
                out_specs=jax.tree.map(lambda _: vmem, out),
                out_shape=out,
                scratch_shapes=[pltpu.VMEM(s, F32) for s in scratch],
                compiler_params=pltpu.CompilerParams(vmem_limit_bytes=limit),
            )

            def run(*args):
                return kernel(*[near(a) if spec is vmem else a for a, spec in zip(args, specs)])

            return run

        def near(array):
            return pltpu.with_memory_space_constraint(array, pltpu.VMEM)

        def shaped(*shape):
            return jax.ShapeDtypeStruct(shape, F32)

        def placed(*shape):
            return pltpu.VMEM(shape, F32)

        free = pl.BlockSpec()
        tables = (transfer_slope.T, transfer_offset.T, transfer_gain[None, :])
        block = (zl, xl, yl)
        blocks, curves, home_density, kept = call(
            pack_kernel,
            [free] * 6,
            (placed(S, chunk * FIELDS, L), placed(transfer_gain.shape[0], 16, LANES), placed(*block), placed(3, *block)),
            table=table, chunk=chunk, depth=zl * ngz,
        )(phase_field, thermal, velocity, *tables)
        pencils = lax.all_to_all(blocks, ("gz", "gx"), 0, 0, tiled=True)
        every = ("gx", "gy", "gz")
        own = pencils.reshape(-1, L)
        sizes = dict(ngx=ngx, ngz=ngz, zl=zl, xl=xl, chunk=chunk)
        message = (2 * margin + 1, S, L)
        messages = call(edges_kernel, [vmem], [placed(*message)] * (2 * hops), margin=margin, **sizes)(own)
        swaps = [(messages[i], hop_swaps(places, i // 2 + 1, i % 2)) for i in range(2 * hops)]
        runs = hops == 1 and ngy % 2 == 0 and S % 2 == 0
        if runs:
            swaps = [swaps[0]] + [(messages[1], run_swaps(places, 2 * S, start)) for start in (0, S)]
        swapped = []
        for value, pairs in swaps:
            swapped.append(lax.ppermute(value, every, pairs))
        *own_values, home_lower = call(
            own_kernel,
            [vmem] * 2,
            (
                *[placed(*lead, chunk, S, L) for lead in ((), (), (3,), (4,), (7,), (ITERS,), (), ())],
                placed(SUMS, S, L),
                placed(3, *block),
            ),
            limit=VMEM_LIMIT, step=step, **sizes,
        )(own, home_density)
        velocities, faces = own_values[2:4]
        wide = chunk + 2 * HALO
        levels, lower, sums = call(
            krylov_kernel,
            [vmem] * (9 + len(swapped)),
            (placed(ITERS, wide, S, L), placed(chunk, S, L), placed(devices, LANES)),
            ((2, hops) + message, (wide, S, L), (7, wide, S, L), (chunk, S, L), (wide, S, L)),
            limit=VMEM_LIMIT, hops=hops, margin=margin, step=step, places=devices, runs=int(runs), **sizes,
        )(*own_values, *swapped)
        sums = lax.all_to_all(sums, every, 0, 0, tiled=True)
        height = Slot(zl, xl, chunk).height
        packed = call(
            render_kernel,
            [vmem] * 6,
            placed(S * height, LANES),
            ((chunk + 1, S, L), (yl, L), (zl, xl, yl)),
            step=step, **sizes,
        )(sums, levels, faces, lower, velocities, curves)
        home = lax.all_to_all(packed.reshape(S, height, LANES), ("gz", "gx"), 0, 0, tiled=True)
        return call(
            unpack_kernel,
            [vmem] * 3,
            (shaped(3, *block), shaped(functions, 4, xl, yl)),
            ((yl, L), (yl, LANES)),
            table=table, chunk=chunk,
        )(home, home_lower, kept)

    return jax.shard_map(
        local,
        mesh=mesh,
        in_specs=(P("gz", "gx", "gy"), P("gz", "gx", "gy"), P(None, "gz", "gx", "gy"), P(), P(), P()),
        out_specs=(P(None, "gz", "gx", "gy"), P("gz", None, "gx", "gy")),
        check_vma=False,
    )
```

```python
import math

import jax
import jax.numpy as jnp
from jax import lax
from jax.experimental import pallas as pl
from jax.experimental.pallas import tpu as pltpu
from jax.sharding import PartitionSpec as P


ITERS = 4
HALO = ITERS + 1
FIELDS = 4
LANES = 128
VMEM_LIMIT = 24 << 20
LOG2E = math.log2(math.e)
F32 = jnp.float32


def snake(ngx, ngz):
    order = []
    for x in range(ngx):
        depths = range(ngz) if x % 2 == 0 else reversed(range(ngz))
        order.extend((x, z) for z in depths)
    return order


def chain(ngx, ngy, ngz):
    places = []
    order = snake(ngx, ngz)
    for y in range(ngy):
        for x, z in order if y % 2 == 0 else order[::-1]:
            places.append((x * ngy + y) * ngz + z)
    return places


def both_ways(places, pairs):
    pairs = [(places[a], places[b]) for a, b in pairs]
    return pairs + [(b, a) for a, b in pairs]


def hop_swaps(places, hop, odd):
    return both_ways(places, [(i, i + hop) for i in range(len(places) - hop) if i // hop % 2 == odd])


def run_swaps(places, run, start):
    pairs, rest = [], list(range(start))
    while start + run <= len(places):
        pairs.append((start, start + run - 1))
        pairs.extend((i, i + 1) for i in range(start + 1, start + run - 1, 2))
        start += run
    rest.extend(range(start, len(places)))
    pairs.extend((i, i + 1) for i in rest if i % 2 == 0)
    return both_ways(places, pairs)


def chain_place(ngx, ngz):
    x, y, z = lax.axis_index("gx"), lax.axis_index("gy"), lax.axis_index("gz")
    within = x * ngz + jnp.where(x % 2 == 0, z, ngz - 1 - z)
    group = ngx * ngz
    return y * group + jnp.where(y % 2 == 0, within, group - 1 - within)


def roll(value, shift, axis):
    size = value.shape[axis]
    shift = shift % size
    return value if shift == 0 else pltpu.roll(value, shift, axis)


def owner(table, c):
    forward = lax.axis_index("gy") % 2 == 0
    return jnp.where(forward, table[c], table[len(table) - 1 - c])


def pack_kernel(phase_ref, thermal_ref, velocity_ref, out_ref, density_ref, kept_ref, *, table, chunk):
    zl, xl, yl = thermal_ref.shape
    density = (1.0 + 9.0 * phase_ref[...].astype(F32)) * thermal_ref[...]
    density_ref[...] = density
    kept_ref[...] = velocity_ref[...]
    for f in range(FIELDS):
        field = density if f == 0 else velocity_ref[f - 1]
        turned = field.reshape(zl * xl, yl).T
        for c in range(yl // chunk):
            rows = turned[c * chunk : (c + 1) * chunk]
            out_ref[owner(table, c), pl.ds(f, chunk, stride=FIELDS), :] = rows


class Slot:
    def __init__(self, zl, xl, chunk):
        self.width = 1
        while self.width < zl + xl:
            self.width *= 2
        groups = LANES // self.width
        self.faces = chunk
        self.deep = -(-chunk // groups)
        self.side = chunk + self.deep
        self.images = -(-(self.side + 1) // 8) * 8
        self.height = -(-(self.images + xl) // 8) * 8


def even_place(ngx, ngz, hop):
    return chain_place(ngx, ngz) // hop % 2 == 0


class Shifts:
    def __init__(self, ngx, ngz, zl, xl):
        self.ngx, self.ngz, self.zl, self.xl = ngx, ngz, zl, xl
        shape = (1, ngx * ngz, zl * xl)
        lane = lax.broadcasted_iota(jnp.int32, shape, 2)
        sub = lax.broadcasted_iota(jnp.int32, shape, 1)
        z, x = lane // xl, lane % xl
        gz, gx = sub % ngz, sub // ngz
        self.z_first, self.z_last = z == 0, z == zl - 1
        self.x_first, self.x_last = x == 0, x == xl - 1
        self.z_low = self.z_first & (gz == 0)
        self.z_high = self.z_last & (gz == ngz - 1)
        self.x_low = self.x_first & (gx == 0)
        self.x_high = self.x_last & (gx == ngx - 1)

    def below_z(self, f):
        near = roll(f, self.xl, 2)
        return jnp.where(self.z_first, roll(near, 1, 1), near)

    def above_z(self, f):
        near = roll(f, -self.xl, 2)
        return jnp.where(self.z_last, roll(near, -1, 1), near)

    def below_x(self, f):
        far = roll(roll(f, 1 - self.xl, 2), self.ngz, 1)
        return jnp.where(self.x_first, far, roll(f, 1, 2))

    def above_x(self, f):
        far = roll(roll(f, self.xl - 1, 2), -self.ngz, 1)
        return jnp.where(self.x_last, far, roll(f, -1, 2))


def divergence(move, velocity, after):
    vz, vx, vy = velocity
    out = -(jnp.where(move.z_high, 0.0, move.above_z(vz)) - vz)
    out = out - (jnp.where(move.x_high, 0.0, move.above_x(vx)) - vx)
    return out + vy if after is None else out - (after - vy)


def column_reader(own_ref, S, chunk):
    def read(k, f):
        return own_ref[pl.ds(k * FIELDS + f, S, stride=chunk * FIELDS), :][None]

    return read


def column(move, read, k, chunk):
    velocity = [read(k, f) for f in (1, 2, 3)]
    return velocity, divergence(move, velocity, read(k + 1, 3) if k + 1 < chunk else None)


def edges_kernel(own_ref, *out_refs, ngx, ngz, zl, xl, chunk, margin):
    move = Shifts(ngx, ngz, zl, xl)
    read = column_reader(own_ref, ngx * ngz, chunk)
    messages = []
    for start in (0, chunk - margin):
        planes = [read(k, 0) for k in range(start, start + margin)]
        planes += [column(move, read, k, chunk)[1] for k in range(start, start + margin)]
        messages.append(jnp.concatenate(planes + [read(0, 3)], axis=0))
    first, last = messages
    for h in range(len(out_refs) // 2):
        ahead_ref, behind_ref = out_refs[2 * h : 2 * h + 2]
        even = even_place(ngx, ngz, h + 1)

        @pl.when(even)
        def _():
            ahead_ref[...], behind_ref[...] = last, first

        @pl.when(jnp.logical_not(even))
        def _():
            ahead_ref[...], behind_ref[...] = first, last


def shared_faces(move, d):
    def face(missing, other):
        return 2.0 / (d + jnp.where(missing, d, other))

    return (
        face(move.z_low, move.below_z(d)),
        face(move.z_high, move.above_z(d)),
        face(move.x_low, move.below_x(d)),
        face(move.x_high, move.above_x(d)),
    )


def differences(levels):
    basis, gaps = [], []
    while len(levels) > 1:
        basis.append(levels[0])
        gaps.append(levels[1])
        levels = [levels[i] - levels[i + 1] for i in range(len(levels) - 1)]
    return basis + levels, gaps


class Operator:
    def __init__(self, move, coef, vec):
        self.move, self.coef, self.vec = move, coef, vec

    def set(self, a, b, faces, d, before, after, source, inside=None):
        move = self.move
        lz, uz, lx, ux = faces
        ly = 2.0 / (d + jnp.where(before > 0.0, before, d))
        uy = 2.0 / (d + jnp.where(after > 0.0, after, d))
        total = lz + uz + lx + ux + ly + uy
        inverse = 1.0 / total
        if inside is not None:
            inverse = jnp.where(inside, inverse, 0.0)
        self.coef[0, a:b] = jnp.where(move.z_low, 0.0, inverse * lz)
        self.coef[1, a:b] = jnp.where(move.z_high, 0.0, inverse * uz)
        self.coef[2, a:b] = jnp.where(move.x_low, 0.0, inverse * lx)
        self.coef[3, a:b] = jnp.where(move.x_high, 0.0, inverse * ux)
        self.coef[4, a:b] = inverse * ly
        self.coef[5, a:b] = inverse * uy
        rim = jnp.where(move.z_low, lz, 0.0) + jnp.where(move.z_high, uz, 0.0)
        rim = rim + (jnp.where(move.x_low, lx, 0.0) + jnp.where(move.x_high, ux, 0.0))
        self.coef[6, a:b] = inverse * rim
        self.vec[0, a:b] = inverse * source
        return total, ly

    def apply(self, k, a, b):
        move, coef, vec = self.move, self.coef, self.vec
        f = vec[k, a:b]
        out = coef[0, a:b] * (f - move.below_z(f)) + coef[1, a:b] * (f - move.above_z(f))
        out = out + (coef[2, a:b] * (f - move.below_x(f)) + coef[3, a:b] * (f - move.above_x(f)))
        out = out + (coef[4, a:b] * (f - vec[k, a - 1 : b - 1]) + coef[5, a:b] * (f - vec[k, a + 1 : b + 1]))
        return out + coef[6, a:b] * f

    def add_sums(self, sums, a, b, weight, right):
        levels = [self.vec[k, a:b] for k in range(ITERS)]
        levels.append(self.apply(ITERS - 1, a, b))
        basis, gaps = differences(levels)
        scaled = [weight * gap for gap in gaps]
        terms = [basis[(k + 1) // 2] * scaled[k // 2] for k in range(2 * ITERS - 1)]
        terms += [right * basis[k] for k in range(ITERS)]
        terms += [weight * levels[k // 2] * levels[(k + 1) // 2] for k in range(2, 2 * ITERS)]
        return [total + jnp.sum(term, axis=0) for total, term in zip(sums, terms)]


SUMS = 2 * ITERS - 1 + ITERS + 2 * ITERS - 2


def pieces(a, b, step):
    return [(i, min(i + step, b)) for i in range(a, b, step)]


def inner(k, chunk):
    return (k + 1, chunk - 1 - k) if chunk - 1 - k > k + 1 else (0, 0)


def own_kernel(
    own_ref, home_ref, slope_ref, offset_ref, gain_ref, density_ref, source_ref, velocity_ref, faces_ref, coef_ref, vec_ref, diag_ref,
    side_ref, sums_ref, lower_ref, curves_ref, *, ngx, ngz, zl, xl, chunk, step, depth
):
    move = Shifts(ngx, ngz, zl, xl)
    read = column_reader(own_ref, ngx * ngz, chunk)
    for k in range(chunk):
        d = read(k, 0)
        velocity, source = column(move, read, k, chunk)
        density_ref[k : k + 1], source_ref[k : k + 1] = d, source
        for f, v in enumerate(velocity):
            velocity_ref[f, k : k + 1] = v
        for f, v in enumerate(shared_faces(move, d)):
            faces_ref[f, k : k + 1] = v
    operator = Operator(move, coef_ref, vec_ref)
    for a, b in pieces(*inner(0, chunk), step):
        faces = [faces_ref[f, a:b] for f in range(4)]
        d, before, after = density_ref[a:b], density_ref[a - 1 : b - 1], density_ref[a + 1 : b + 1]
        diag_ref[a:b], side_ref[a:b] = operator.set(a, b, faces, d, before, after, source_ref[a:b])
    for k in range(1, ITERS):
        for a, b in pieces(*inner(k, chunk), step):
            vec_ref[k, a:b] = operator.apply(k - 1, a, b)
    sums = [jnp.zeros(sums_ref.shape[1:], F32)] * SUMS
    for a, b in pieces(*inner(ITERS, chunk), step):
        sums = operator.add_sums(sums, a, b, diag_ref[a:b], source_ref[a:b])
    for k, value in enumerate(sums):
        sums_ref[k] = value
    d = home_ref[...]
    lower_ref[0] = 2.0 / (d + jnp.concatenate([d[:1], d[:-1]], axis=0))
    lower_ref[1] = 2.0 / (d + roll(d, 1, 1))
    lower_ref[2] = 2.0 / (d + roll(d, 1, 2))
    for t in range(curves_ref.shape[0]):
        curves_ref[t, 0:4, :] = jnp.broadcast_to(-LOG2E * slope_ref[:, t : t + 1], (4, LANES))
        curves_ref[t, 4:8, :] = jnp.broadcast_to(-LOG2E * offset_ref[:, t : t + 1], (4, LANES))
        curves_ref[t, 8:9, :] = jnp.broadcast_to(gain_ref[:, t : t + 1] / depth, (1, LANES))


def krylov_kernel(*refs, ngx, ngz, zl, xl, chunk, hops, margin, step, places, runs):
    density_ref, source_ref, velocity_ref, faces_ref, own_coef, own_vec, own_diag, own_side, own_sums = refs[:9]
    count = 2 * hops + runs
    swapped = refs[9 : 9 + count]
    vec, lower_ref, sums_ref, sides, dens, coef, diag, source = refs[9 + count :]
    S, L = ngx * ngz, zl * xl
    E = chunk + 2 * HALO
    move = Shifts(ngx, ngz, zl, xl)

    place = chain_place(ngx, ngz)
    for h in range(hops):
        even = even_place(ngx, ngz, h + 1)
        sides[jnp.where(even, 1, 0), h] = swapped[2 * h][...]
        other = jnp.where(even, 0, 1)
        if not runs:
            sides[other, h] = swapped[2 * h + 1][...]
            continue
        within = place % (2 * S)
        border = (within == 0) | (within == 2 * S - 1)
        end = (place == 0) | (place == places - 1)

        @pl.when(jnp.logical_not(border))
        def _():
            sides[other, h] = swapped[1][...]

        @pl.when(border & jnp.logical_not(end))
        def _():
            sides[other, h] = swapped[2][...]

        @pl.when(end)
        def _():
            sides[other, h] = jnp.zeros(sides.shape[2:], F32)

    def ring(k):
        low, high = inner(k, chunk)
        if low == high:
            return pieces(1 + k, E - 1 - k, step)
        low, high = HALO + low, HALO + high
        return pieces(1 + k, low, step) + pieces(high, E - 1 - k, step)

    def outer(j, up):
        hop, at = j // chunk, j % chunk
        index = at if up else margin - 1 - at
        rhs = sides[up, hop, margin + index]
        if not up and at == 0:
            rhs = rhs - (velocity_ref[2, 0] if hop == 0 else sides[0, hop - 1, 2 * margin])
        if up and at == chunk - 1 and hop + 1 < hops:
            rhs = rhs - sides[1, hop + 1, 2 * margin]
        return sides[up, hop, index], rhs

    for j in range(HALO):
        dens[HALO - 1 - j], low_rhs = outer(j, 0)
        dens[HALO + chunk + j], high_rhs = outer(j, 1)
        source[HALO - 1 - j], source[HALO + chunk + j] = low_rhs, high_rhs
    dens[HALO : HALO + chunk] = density_ref[...]
    source[HALO : HALO + chunk] = source_ref[...]
    top = HALO + chunk - 1
    source[top] = source[top] - sides[1, 0, 2 * margin]
    for k in range(ITERS):
        a, b = inner(k, chunk)
        if a < b:
            vec[k, HALO + a : HALO + b] = own_vec[k, a:b]
    a, b = inner(0, chunk)
    if a < b:
        coef[:, HALO + a : HALO + b] = own_coef[:, a:b]
        lower_ref[a:b], diag[a:b] = own_side[a:b], own_diag[a:b]

    operator = Operator(move, coef, vec)
    for start, stop in ring(0):
        edges = sorted({start, stop, *(e for e in (HALO, HALO + chunk) if start < e < stop)})
        for a, b in zip(edges[:-1], edges[1:]):
            d, before, after = dens[a:b], dens[a - 1 : b - 1], dens[a + 1 : b + 1]
            if HALO <= a < HALO + chunk:
                own = slice(a - HALO, b - HALO)
                faces = [faces_ref[f, own] for f in range(4)]
                diag[own], lower_ref[own] = operator.set(a, b, faces, d, before, after, source[a:b])
            else:
                inside = d > 0.0
                d = jnp.where(inside, d, 1.0)
                operator.set(a, b, shared_faces(move, d), d, before, after, source[a:b], inside)
    for k in range(1, ITERS):
        for a, b in ring(k):
            vec[k, a:b] = operator.apply(k - 1, a, b)
    sums = [own_sums[k] for k in range(SUMS)]
    for a, b in ring(ITERS):
        sums = operator.add_sums(sums, a, b, diag[a - HALO : b - HALO], source[a:b])
    powers, firsts = sums[: 2 * ITERS - 1], sums[2 * ITERS - 1 : 3 * ITERS - 1]
    steps = [firsts[0], powers[0]] + sums[3 * ITERS - 1 :]

    columns = powers + firsts + steps
    rows = [jnp.sum(c, axis=0, keepdims=True) for c in columns]
    high = -(-len(rows) // 8) * 8
    rows = rows + [jnp.zeros((1, L), F32)] * (high - len(rows))
    sums = jnp.sum(jnp.concatenate(rows, axis=0), axis=1, keepdims=True)
    lane = lax.broadcasted_iota(jnp.int32, (high, LANES), 1)
    row = lax.broadcasted_iota(jnp.int32, (high, LANES), 0)
    line = jnp.sum(jnp.where(lane == row, sums, 0.0), axis=0, keepdims=True)
    sums_ref[...] = jnp.broadcast_to(line, sums_ref.shape)


def galerkin(sums):
    n, count = ITERS, 2 * ITERS - 1
    line = jnp.sum(sums, axis=0, keepdims=True)
    lane = lax.broadcasted_iota(jnp.int32, line.shape, 1)

    def pick(k):
        return jnp.sum(jnp.where(lane == k, line, 0.0), axis=1, keepdims=True)

    powers = [pick(k) for k in range(count)]
    firsts = [pick(count + k) for k in range(n)]
    steps = [pick(count + n + k) for k in range(count + 1)]
    matrix = [jnp.concatenate([powers[k], steps[k + 1]], axis=0) for k in range(count)]
    right = [jnp.concatenate([firsts[k], steps[k]], axis=0) for k in range(n)]
    low = [[None] * n for _ in range(n)]
    scale = [None] * n
    quality = None
    for j in range(n):
        pivot = matrix[2 * j]
        for k in range(j):
            pivot = pivot - low[j][k] * low[j][k] * scale[k][0]
        share = pivot / matrix[2 * j]
        fine = share > 1e-7
        quality = jnp.where(fine, share, 0.0) if quality is None else jnp.minimum(quality, jnp.where(fine, share, 0.0))
        inverse = jnp.where(fine, 1.0 / pivot, 0.0)
        scale[j] = (pivot, inverse)
        for r in range(j + 1, n):
            entry = matrix[r + j]
            for k in range(j):
                entry = entry - low[r][k] * low[j][k] * scale[k][0]
            low[r][j] = entry * inverse
    part = list(right)
    for r in range(n):
        for k in range(r):
            part[r] = part[r] - low[r][k] * part[k]
    part = [part[r] * scale[r][1] for r in range(n)]
    for r in reversed(range(n)):
        for k in range(r + 1, n):
            part[r] = part[r] - low[k][r] * part[k]
    first = quality[0:1] >= quality[1:2]
    by_power = [jnp.where(first, p[0:1], 0.0) for p in part]
    by_step = [jnp.where(first, 0.0, p[1:2]) for p in part]
    return by_power, by_step


def render_kernel(
    sums_ref, vec_ref, faces_ref, lower_ref, velocity_ref, table_ref, out_ref, press, flat, turned,
    *, ngx, ngz, zl, xl, chunk, step
):
    S, L = ngx * ngz, zl * xl
    yl = S * chunk
    slot = Slot(zl, xl, chunk)
    height = slot.height
    move = Shifts(ngx, ngz, zl, xl)
    by_power, by_step = galerkin(sums_ref[...])
    by_power = [v.reshape(1, 1, 1) for v in by_power]
    by_step = [v.reshape(1, 1, 1) for v in by_step]
    for a in range(0, chunk + 1, step):
        b = min(a + step, chunk + 1)
        levels = [vec_ref[k, HALO - 1 + a : HALO - 1 + b] for k in range(ITERS)]
        basis = differences(levels)[0]
        value = 0.0
        for k in range(ITERS):
            value = value + by_power[k] * basis[k] + by_step[k] * levels[k]
        press[a:b] = value
    spot = lax.broadcasted_iota(jnp.int32, (S, L), 1)
    sides = [jnp.zeros((S, L), F32) for _ in range(slot.deep)]
    for a in range(0, chunk, step):
        b = min(a + step, chunk)
        p = press[a + 1 : b + 1]
        fronts = (
            jnp.where(move.z_low, 0.0, move.below_z(p)),
            jnp.where(move.x_low, 0.0, move.below_x(p)),
            press[a:b],
        )
        pieces = []
        for k, front in enumerate(fronts):
            lower = lower_ref[a:b] if k == 2 else faces_ref[2 * k, a:b]
            pieces.append(velocity_ref[k, a:b] - lower * (p - front))
        scalar = pieces[0] + pieces[1] + pieces[2]
        if a == 0:
            out_ref[pl.ds(slot.side, S, stride=height), :] = pieces[2][0]
        for c in range(a, b):
            out_ref[pl.ds(c, S, stride=height), :] = p[c - a]
            flat[pl.ds(c, S, stride=chunk), :] = scalar[c - a]
            base = c // slot.deep * slot.width
            deep = roll(pieces[0][c - a], base, 1)
            where = (spot - (base + xl)) * xl
            wide = jnp.take_along_axis(pieces[1][c - a], jnp.clip(where, 0, L - 1), axis=1, mode="promise_in_bounds")
            r = c % slot.deep
            sides[r] = jnp.where(spot >= base, jnp.where(spot >= base + xl, wide, deep), sides[r])
    for r, side in enumerate(sides):
        out_ref[pl.ds(slot.faces + r, S, stride=height), :] = side
    turned[...] = flat[...].T.reshape(zl, xl, yl)

    side = ngz * chunk
    band = LANES // 4
    functions = table_ref.shape[0] // ngz
    lane = lax.broadcasted_iota(jnp.int32, (xl, yl), 1)

    def curve_sums(index):
        rows = [jnp.broadcast_to(table_ref[index, r : r + 1, :], (xl, yl)) for r in range(9)]
        rates, bases, gain = rows[:4], rows[4:8], rows[8]
        through = jnp.ones((xl, yl), F32)
        colors = [jnp.zeros((xl, yl), F32) for _ in range(3)]
        for z in range(zl):
            x = turned[z]
            curves = [1.0 / (1.0 + jnp.exp2(rates[c] * x + bases[c])) for c in range(4)]
            opacity = gain * curves[3]
            weight = through * opacity
            colors = [colors[c] + weight * curves[c] for c in range(3)]
            through = through * (1.0 - opacity)
        return colors + [through]

    for i in range(ngz):
        images = [jnp.zeros((xl, LANES), F32) for _ in range(ngx)]
        for t in range(functions):
            planes = curve_sums(i * functions + t)
            span = 1
            while span < ngz:
                behind = [roll(plane, -span * chunk, 1) for plane in planes]
                planes = [planes[c] + planes[3] * behind[c] for c in range(3)] + [planes[3] * behind[3]]
                span *= 2
            planes[3] = 1.0 - planes[3]
            planes = [roll(plane, c * band, 1) for c, plane in enumerate(planes)]
            here = (lane % band) // chunk == t
            for k in range(ngx):
                merged = planes[0]
                for c in range(1, 4):
                    merged = jnp.where((lane + (LANES - k * side) % LANES) % LANES // band == c, planes[c], merged)
                images[k] = jnp.where(here, roll(merged, t * chunk - k * side, 1), images[k])
        for k in range(ngx):
            place = (k * ngz + i) * height + slot.images
            out_ref[place : place + xl, :] = images[k]


def unpack_kernel(in_ref, lower_ref, velocity_ref, corrected_ref, images_ref, flat, sides, *, table, chunk):
    zl, xl, yl = corrected_ref.shape[1:]
    slot = Slot(zl, xl, chunk)
    functions = images_ref.shape[0]
    band = LANES // 4
    lane = lax.broadcasted_iota(jnp.int32, (xl, yl), 1)
    images = [jnp.zeros((xl, yl), F32) for _ in range(functions * 4)]
    for c in range(yl // chunk):
        place = owner(table, c)
        flat[c * chunk : (c + 1) * chunk, :] = in_ref[place, :chunk, :]
        faces = in_ref[place, slot.faces : slot.faces + 8, :]
        for g in range(-(-chunk // slot.deep)):
            rows = min(slot.deep, chunk - g * slot.deep)
            start = c * chunk + g * slot.deep
            sides[start : start + rows, :] = roll(faces, -g * slot.width, 1)[:rows]
        source = in_ref[place, slot.images : slot.images + xl, :]
        here = (lane >= c * chunk) & (lane < (c + 1) * chunk)
        for k in range(functions * 4):
            shift = c * chunk - (k % 4 * band + k // 4 * chunk)
            images[k] = jnp.where(here, roll(source, shift, 1), images[k])
    for k, image in enumerate(images):
        images_ref[k // 4, k % 4] = image
    p = flat[...].T.reshape(zl, xl, yl)
    faces = sides[...].T
    deep, wide = faces[:xl], faces[xl : xl + zl]
    front = in_ref[owner(table, 0), slot.side : slot.side + 1, :]
    high = jnp.broadcast_to(front, (yl, zl * xl)).T.reshape(zl, xl, yl)
    x = lax.broadcasted_iota(jnp.int32, (zl, xl, yl), 1)
    y = lax.broadcasted_iota(jnp.int32, (zl, xl, yl), 2)
    inner = velocity_ref[0, 1:] - lower_ref[0, 1:] * (p[1:] - p[:-1])
    corrected_ref[0, 0], corrected_ref[0, 1:] = deep, inner
    inner = velocity_ref[1] - lower_ref[1] * (p - roll(p, 1, 1))
    corrected_ref[1] = jnp.where(x == 0, wide[:, None, :], inner)
    inner = velocity_ref[2] - lower_ref[2] * (p - roll(p, 1, 2))
    corrected_ref[2] = jnp.where(y == 0, high, inner)


def solution(mesh):
    ngx, ngy, ngz = mesh.shape["gx"], mesh.shape["gy"], mesh.shape["gz"]
    S, devices = ngx * ngz, ngx * ngy * ngz
    table = [x * ngz + z for x, z in snake(ngx, ngz)]
    places = chain(ngx, ngy, ngz)

    def local(phase_field, thermal, velocity, transfer_slope, transfer_offset, transfer_gain):
        zl, xl, yl = thermal.shape
        L, chunk = zl * xl, yl // S
        functions = transfer_slope.shape[0] // ngz
        assert yl % S == 0 and L == LANES and yl == LANES and max(ngx, functions) * 4 * chunk <= LANES
        assert ngz & (ngz - 1) == 0
        hops = -(-HALO // chunk)
        margin = min(chunk, HALO)
        step = max(1, 4 * 8 // S)

        vmem = pl.BlockSpec(memory_space=pltpu.VMEM)

        def call(body, specs, out, scratch=(), limit=None, **kwargs):
            kernel = pl.pallas_call(
                lambda *refs: body(*refs, **kwargs),
                in_specs=specs,
                out_specs=jax.tree.map(lambda _: vmem, out),
                out_shape=out,
                scratch_shapes=[pltpu.VMEM(s, F32) for s in scratch],
                compiler_params=pltpu.CompilerParams(vmem_limit_bytes=limit),
            )

            def run(*args):
                return kernel(*[near(a) if spec is vmem else a for a, spec in zip(args, specs)])

            return run

        def near(array):
            return pltpu.with_memory_space_constraint(array, pltpu.VMEM)

        def shaped(*shape):
            return jax.ShapeDtypeStruct(shape, F32)

        def placed(*shape):
            return pltpu.VMEM(shape, F32)

        free = pl.BlockSpec()
        tables = (transfer_slope.T, transfer_offset.T, transfer_gain[None, :])
        block = (zl, xl, yl)
        blocks, home_density, kept = call(
            pack_kernel,
            [free] * 3,
            (placed(S, chunk * FIELDS, L), placed(*block), placed(3, *block)),
            table=table, chunk=chunk,
        )(phase_field, thermal, velocity)
        pencils = lax.all_to_all(blocks, ("gx", "gz"), 0, 0, tiled=True)
        every = ("gx", "gy", "gz")
        own = pencils.reshape(-1, L)
        sizes = dict(ngx=ngx, ngz=ngz, zl=zl, xl=xl, chunk=chunk)
        message = (2 * margin + 1, S, L)
        messages = call(edges_kernel, [vmem], [placed(*message)] * (2 * hops), margin=margin, **sizes)(own)
        swaps = [(messages[i], hop_swaps(places, i // 2 + 1, i % 2)) for i in range(2 * hops)]
        runs = hops == 1 and ngy % 2 == 0 and S % 2 == 0
        if runs:
            swaps = [swaps[0]] + [(messages[1], run_swaps(places, 2 * S, start)) for start in (0, S)]
        swapped = []
        for value, pairs in swaps:
            swapped.append(lax.ppermute(value, every, pairs))
        *own_values, home_lower, curves = call(
            own_kernel,
            [vmem] * 2 + [free] * 3,
            (
                *[placed(*lead, chunk, S, L) for lead in ((), (), (3,), (4,), (7,), (ITERS,), (), ())],
                placed(SUMS, S, L),
                placed(3, *block),
                placed(transfer_gain.shape[0], 16, LANES),
            ),
            limit=VMEM_LIMIT, step=step, depth=zl * ngz, **sizes,
        )(own, home_density, *tables)
        velocities, faces = own_values[2:4]
        wide = chunk + 2 * HALO
        levels, lower, sums = call(
            krylov_kernel,
            [vmem] * (9 + len(swapped)),
            (placed(ITERS, wide, S, L), placed(chunk, S, L), placed(devices, LANES)),
            ((2, hops) + message, (wide, S, L), (7, wide, S, L), (chunk, S, L), (wide, S, L)),
            limit=VMEM_LIMIT, hops=hops, margin=margin, step=step, places=devices, runs=int(runs), **sizes,
        )(*own_values, *swapped)
        sums = lax.all_to_all(sums, every, 0, 0, tiled=True)
        height = Slot(zl, xl, chunk).height
        packed = call(
            render_kernel,
            [vmem] * 6,
            placed(S * height, LANES),
            ((chunk + 1, S, L), (yl, L), (zl, xl, yl)),
            step=step, **sizes,
        )(sums, levels, faces, lower, velocities, curves)
        home = lax.all_to_all(packed.reshape(S, height, LANES), ("gx", "gz"), 0, 0, tiled=True)
        return call(
            unpack_kernel,
            [vmem] * 3,
            (shaped(3, *block), shaped(functions, 4, xl, yl)),
            ((yl, L), (yl, LANES)),
            table=table, chunk=chunk,
        )(home, home_lower, kept)

    return jax.shard_map(
        local,
        mesh=mesh,
        in_specs=(P("gz", "gx", "gy"), P("gz", "gx", "gy"), P(None, "gz", "gx", "gy"), P(), P(), P()),
        out_specs=(P(None, "gz", "gx", "gy"), P("gz", None, "gx", "gy")),
        check_vma=False,
    )
```

```python
import math

import jax
import jax.numpy as jnp
from jax import lax
from jax.experimental import pallas as pl
from jax.experimental.pallas import tpu as pltpu
from jax.sharding import PartitionSpec as P


ITERS = 4
HALO = ITERS + 1
FIELDS = 4
LANES = 128
VMEM_LIMIT = 24 << 20
LOG2E = math.log2(math.e)
F32 = jnp.float32


def snake(ngx, ngz):
    order = []
    for x in range(ngx):
        depths = range(ngz) if x % 2 == 0 else reversed(range(ngz))
        order.extend((x, z) for z in depths)
    return order


def chain(ngx, ngy, ngz):
    places = []
    order = snake(ngx, ngz)
    for y in range(ngy):
        for x, z in order if y % 2 == 0 else order[::-1]:
            places.append((x * ngy + y) * ngz + z)
    return places


def both_ways(places, pairs):
    pairs = [(places[a], places[b]) for a, b in pairs]
    return pairs + [(b, a) for a, b in pairs]


def hop_swaps(places, hop, odd):
    return both_ways(places, [(i, i + hop) for i in range(len(places) - hop) if i // hop % 2 == odd])


def run_swaps(places, run, start):
    pairs, rest = [], list(range(start))
    while start + run <= len(places):
        pairs.append((start, start + run - 1))
        pairs.extend((i, i + 1) for i in range(start + 1, start + run - 1, 2))
        start += run
    rest.extend(range(start, len(places)))
    pairs.extend((i, i + 1) for i in rest if i % 2 == 0)
    return both_ways(places, pairs)


def chain_place(ngx, ngz):
    x, y, z = lax.axis_index("gx"), lax.axis_index("gy"), lax.axis_index("gz")
    within = x * ngz + jnp.where(x % 2 == 0, z, ngz - 1 - z)
    group = ngx * ngz
    return y * group + jnp.where(y % 2 == 0, within, group - 1 - within)


def roll(value, shift, axis):
    size = value.shape[axis]
    shift = shift % size
    return value if shift == 0 else pltpu.roll(value, shift, axis)


def owner(table, c):
    forward = lax.axis_index("gy") % 2 == 0
    return jnp.where(forward, table[c], table[len(table) - 1 - c])


def pack_kernel(phase_ref, thermal_ref, velocity_ref, out_ref, density_ref, kept_ref, *, table, chunk):
    zl, xl, yl = thermal_ref.shape
    density = (1.0 + 9.0 * phase_ref[...].astype(F32)) * thermal_ref[...]
    density_ref[...] = density
    kept_ref[...] = velocity_ref[...]
    for f in range(FIELDS):
        field = density if f == 0 else velocity_ref[f - 1]
        turned = field.reshape(zl * xl, yl).T
        for c in range(yl // chunk):
            rows = turned[c * chunk : (c + 1) * chunk]
            out_ref[owner(table, c), pl.ds(f, chunk, stride=FIELDS), :] = rows


class Slot:
    def __init__(self, zl, xl, chunk):
        self.width = 1
        while self.width < zl + xl:
            self.width *= 2
        groups = LANES // self.width
        self.faces = chunk
        self.deep = -(-chunk // groups)
        self.side = chunk + self.deep
        self.images = -(-(self.side + 1) // 8) * 8
        self.height = -(-(self.images + xl) // 8) * 8


def even_place(ngx, ngz, hop):
    return chain_place(ngx, ngz) // hop % 2 == 0


class Shifts:
    def __init__(self, ngx, ngz, zl, xl):
        self.ngx, self.ngz, self.zl, self.xl = ngx, ngz, zl, xl
        shape = (1, ngx * ngz, zl * xl)
        lane = lax.broadcasted_iota(jnp.int32, shape, 2)
        sub = lax.broadcasted_iota(jnp.int32, shape, 1)
        z, x = lane // xl, lane % xl
        gz, gx = sub % ngz, sub // ngz
        self.z_first, self.z_last = z == 0, z == zl - 1
        self.x_first, self.x_last = x == 0, x == xl - 1
        self.z_low = self.z_first & (gz == 0)
        self.z_high = self.z_last & (gz == ngz - 1)
        self.x_low = self.x_first & (gx == 0)
        self.x_high = self.x_last & (gx == ngx - 1)

    def below_z(self, f):
        near = roll(f, self.xl, 2)
        return jnp.where(self.z_first, roll(near, 1, 1), near)

    def above_z(self, f):
        near = roll(f, -self.xl, 2)
        return jnp.where(self.z_last, roll(near, -1, 1), near)

    def below_x(self, f):
        far = roll(roll(f, 1 - self.xl, 2), self.ngz, 1)
        return jnp.where(self.x_first, far, roll(f, 1, 2))

    def above_x(self, f):
        far = roll(roll(f, self.xl - 1, 2), -self.ngz, 1)
        return jnp.where(self.x_last, far, roll(f, -1, 2))


def divergence(move, velocity, after):
    vz, vx, vy = velocity
    out = -(jnp.where(move.z_high, 0.0, move.above_z(vz)) - vz)
    out = out - (jnp.where(move.x_high, 0.0, move.above_x(vx)) - vx)
    return out + vy if after is None else out - (after - vy)


def column_reader(own_ref, S, chunk):
    def read(k, f):
        return own_ref[pl.ds(k * FIELDS + f, S, stride=chunk * FIELDS), :][None]

    return read


def column(move, read, k, chunk):
    velocity = [read(k, f) for f in (1, 2, 3)]
    return velocity, divergence(move, velocity, read(k + 1, 3) if k + 1 < chunk else None)


def edges_kernel(own_ref, *out_refs, ngx, ngz, zl, xl, chunk, margin):
    move = Shifts(ngx, ngz, zl, xl)
    read = column_reader(own_ref, ngx * ngz, chunk)
    messages, inner_margin = [], min(margin, HALO - 1)
    for start, skip in ((0, 0), (chunk - margin, margin - inner_margin)):
        planes = [read(k, 0) for k in range(start, start + margin)]
        planes += [column(move, read, k, chunk)[1] for k in range(start + skip, start + skip + inner_margin)]
        messages.append(jnp.concatenate(planes + [read(0, 3)], axis=0))
    first, last = messages
    for h in range(len(out_refs) // 2):
        ahead_ref, behind_ref = out_refs[2 * h : 2 * h + 2]
        even = even_place(ngx, ngz, h + 1)

        @pl.when(even)
        def _():
            ahead_ref[...], behind_ref[...] = last, first

        @pl.when(jnp.logical_not(even))
        def _():
            ahead_ref[...], behind_ref[...] = first, last


def shared_faces(move, d):
    def face(missing, other):
        return 2.0 / (d + jnp.where(missing, d, other))

    return (
        face(move.z_low, move.below_z(d)),
        face(move.z_high, move.above_z(d)),
        face(move.x_low, move.below_x(d)),
        face(move.x_high, move.above_x(d)),
    )


def differences(levels):
    basis, gaps = [], []
    while len(levels) > 1:
        basis.append(levels[0])
        gaps.append(levels[1])
        levels = [levels[i] - levels[i + 1] for i in range(len(levels) - 1)]
    return basis + levels, gaps


class Operator:
    def __init__(self, move, coef, vec):
        self.move, self.coef, self.vec = move, coef, vec

    def set(self, a, b, faces, d, before, after, source, inside=None):
        move = self.move
        lz, uz, lx, ux = faces
        ly = 2.0 / (d + jnp.where(before > 0.0, before, d))
        uy = 2.0 / (d + jnp.where(after > 0.0, after, d))
        total = lz + uz + lx + ux + ly + uy
        inverse = 1.0 / total
        if inside is not None:
            inverse = jnp.where(inside, inverse, 0.0)
        self.coef[0, a:b] = jnp.where(move.z_low, 0.0, inverse * lz)
        self.coef[1, a:b] = jnp.where(move.z_high, 0.0, inverse * uz)
        self.coef[2, a:b] = jnp.where(move.x_low, 0.0, inverse * lx)
        self.coef[3, a:b] = jnp.where(move.x_high, 0.0, inverse * ux)
        self.coef[4, a:b] = inverse * ly
        self.coef[5, a:b] = inverse * uy
        rim = jnp.where(move.z_low, lz, 0.0) + jnp.where(move.z_high, uz, 0.0)
        rim = rim + (jnp.where(move.x_low, lx, 0.0) + jnp.where(move.x_high, ux, 0.0))
        self.coef[6, a:b] = inverse * rim
        self.vec[0, a:b] = inverse * source
        return total, ly

    def apply(self, k, a, b):
        move, coef, vec = self.move, self.coef, self.vec
        f = vec[k, a:b]
        out = coef[0, a:b] * (f - move.below_z(f)) + coef[1, a:b] * (f - move.above_z(f))
        out = out + (coef[2, a:b] * (f - move.below_x(f)) + coef[3, a:b] * (f - move.above_x(f)))
        out = out + (coef[4, a:b] * (f - vec[k, a - 1 : b - 1]) + coef[5, a:b] * (f - vec[k, a + 1 : b + 1]))
        return out + coef[6, a:b] * f

    def add_sums(self, sums, a, b, weight, right):
        levels = [self.vec[k, a:b] for k in range(ITERS)]
        levels.append(self.apply(ITERS - 1, a, b))
        basis, gaps = differences(levels)
        scaled = [weight * gap for gap in gaps]
        terms = [basis[(k + 1) // 2] * scaled[k // 2] for k in range(2 * ITERS - 1)]
        terms += [right * basis[k] for k in range(ITERS)]
        terms += [weight * levels[k // 2] * levels[(k + 1) // 2] for k in range(2, 2 * ITERS)]
        return [total + jnp.sum(term, axis=0) for total, term in zip(sums, terms)]


SUMS = 2 * ITERS - 1 + ITERS + 2 * ITERS - 2


def pieces(a, b, step):
    return [(i, min(i + step, b)) for i in range(a, b, step)]


def inner(k, chunk):
    return (k + 1, chunk - 1 - k) if chunk - 1 - k > k + 1 else (0, 0)


def own_kernel(
    own_ref, home_ref, slope_ref, offset_ref, gain_ref, density_ref, source_ref, velocity_ref, faces_ref, coef_ref, vec_ref, diag_ref,
    side_ref, sums_ref, lower_ref, curves_ref, *, ngx, ngz, zl, xl, chunk, step, depth
):
    move = Shifts(ngx, ngz, zl, xl)
    read = column_reader(own_ref, ngx * ngz, chunk)
    for k in range(chunk):
        d = read(k, 0)
        velocity, source = column(move, read, k, chunk)
        density_ref[k : k + 1], source_ref[k : k + 1] = d, source
        for f, v in enumerate(velocity):
            velocity_ref[f, k : k + 1] = v
        for f, v in enumerate(shared_faces(move, d)):
            faces_ref[f, k : k + 1] = v
    operator = Operator(move, coef_ref, vec_ref)
    for a, b in pieces(*inner(0, chunk), step):
        faces = [faces_ref[f, a:b] for f in range(4)]
        d, before, after = density_ref[a:b], density_ref[a - 1 : b - 1], density_ref[a + 1 : b + 1]
        diag_ref[a:b], side_ref[a:b] = operator.set(a, b, faces, d, before, after, source_ref[a:b])
    for k in range(1, ITERS):
        for a, b in pieces(*inner(k, chunk), step):
            vec_ref[k, a:b] = operator.apply(k - 1, a, b)
    sums = [jnp.zeros(sums_ref.shape[1:], F32)] * SUMS
    for a, b in pieces(*inner(ITERS, chunk), step):
        sums = operator.add_sums(sums, a, b, diag_ref[a:b], source_ref[a:b])
    for k, value in enumerate(sums):
        sums_ref[k] = value
    d = home_ref[...]
    lower_ref[0] = 2.0 / (d + jnp.concatenate([d[:1], d[:-1]], axis=0))
    lower_ref[1] = 2.0 / (d + roll(d, 1, 1))
    lower_ref[2] = 2.0 / (d + roll(d, 1, 2))
    for t in range(curves_ref.shape[0]):
        curves_ref[t, 0:4, :] = jnp.broadcast_to(-LOG2E * slope_ref[:, t : t + 1], (4, LANES))
        curves_ref[t, 4:8, :] = jnp.broadcast_to(-LOG2E * offset_ref[:, t : t + 1], (4, LANES))
        curves_ref[t, 8:9, :] = jnp.broadcast_to(gain_ref[:, t : t + 1] / depth, (1, LANES))


def krylov_kernel(*refs, ngx, ngz, zl, xl, chunk, hops, margin, step, places, runs):
    density_ref, source_ref, velocity_ref, faces_ref, own_coef, own_vec, own_diag, own_side, own_sums = refs[:9]
    count = 2 * hops + runs
    swapped = refs[9 : 9 + count]
    vec, lower_ref, sums_ref, sides, dens, coef, diag, source = refs[9 + count :]
    S, L = ngx * ngz, zl * xl
    E = chunk + 2 * HALO
    move = Shifts(ngx, ngz, zl, xl)

    place = chain_place(ngx, ngz)
    for h in range(hops):
        even = even_place(ngx, ngz, h + 1)
        sides[jnp.where(even, 1, 0), h] = swapped[2 * h][...]
        other = jnp.where(even, 0, 1)
        if not runs:
            sides[other, h] = swapped[2 * h + 1][...]
            continue
        within = place % (2 * S)
        border = (within == 0) | (within == 2 * S - 1)
        end = (place == 0) | (place == places - 1)

        @pl.when(jnp.logical_not(border))
        def _():
            sides[other, h] = swapped[1][...]

        @pl.when(border & jnp.logical_not(end))
        def _():
            sides[other, h] = swapped[2][...]

        @pl.when(end)
        def _():
            sides[other, h] = jnp.zeros(sides.shape[2:], F32)

    def ring(k):
        low, high = inner(k, chunk)
        if low == high:
            return pieces(1 + k, E - 1 - k, step)
        low, high = HALO + low, HALO + high
        return pieces(1 + k, low, step) + pieces(high, E - 1 - k, step)

    inner_margin = min(margin, HALO - 1)

    def outer(j, up):
        hop, at = j // chunk, j % chunk
        index = at if up else margin - 1 - at
        if j == HALO - 1:
            return sides[up, hop, index], None
        rhs = sides[up, hop, margin + (at if up else inner_margin - 1 - at)]
        if not up and at == 0:
            rhs = rhs - (velocity_ref[2, 0] if hop == 0 else sides[0, hop - 1, margin + inner_margin])
        if up and at == chunk - 1 and hop + 1 < hops:
            rhs = rhs - sides[1, hop + 1, margin + inner_margin]
        return sides[up, hop, index], rhs

    for j in range(HALO):
        dens[HALO - 1 - j], low_rhs = outer(j, 0)
        dens[HALO + chunk + j], high_rhs = outer(j, 1)
        if j < HALO - 1:
            source[HALO - 1 - j], source[HALO + chunk + j] = low_rhs, high_rhs
    dens[HALO : HALO + chunk] = density_ref[...]
    source[HALO : HALO + chunk] = source_ref[...]
    top = HALO + chunk - 1
    source[top] = source[top] - sides[1, 0, margin + inner_margin]
    for k in range(ITERS):
        a, b = inner(k, chunk)
        if a < b:
            vec[k, HALO + a : HALO + b] = own_vec[k, a:b]
    a, b = inner(0, chunk)
    if a < b:
        coef[:, HALO + a : HALO + b] = own_coef[:, a:b]
        lower_ref[a:b], diag[a:b] = own_side[a:b], own_diag[a:b]

    operator = Operator(move, coef, vec)
    for start, stop in ring(0):
        edges = sorted({start, stop, *(e for e in (HALO, HALO + chunk) if start < e < stop)})
        for a, b in zip(edges[:-1], edges[1:]):
            d, before, after = dens[a:b], dens[a - 1 : b - 1], dens[a + 1 : b + 1]
            if HALO <= a < HALO + chunk:
                own = slice(a - HALO, b - HALO)
                faces = [faces_ref[f, own] for f in range(4)]
                diag[own], lower_ref[own] = operator.set(a, b, faces, d, before, after, source[a:b])
            else:
                inside = d > 0.0
                d = jnp.where(inside, d, 1.0)
                operator.set(a, b, shared_faces(move, d), d, before, after, source[a:b], inside)
    for k in range(1, ITERS):
        for a, b in ring(k):
            vec[k, a:b] = operator.apply(k - 1, a, b)
    sums = [own_sums[k] for k in range(SUMS)]
    for a, b in ring(ITERS):
        sums = operator.add_sums(sums, a, b, diag[a - HALO : b - HALO], source[a:b])
    powers, firsts = sums[: 2 * ITERS - 1], sums[2 * ITERS - 1 : 3 * ITERS - 1]
    steps = [firsts[0], powers[0]] + sums[3 * ITERS - 1 :]

    columns = powers + firsts + steps
    rows = [jnp.sum(c, axis=0, keepdims=True) for c in columns]
    high = -(-len(rows) // 8) * 8
    rows = rows + [jnp.zeros((1, L), F32)] * (high - len(rows))
    sums = jnp.sum(jnp.concatenate(rows, axis=0), axis=1, keepdims=True)
    lane = lax.broadcasted_iota(jnp.int32, (high, LANES), 1)
    row = lax.broadcasted_iota(jnp.int32, (high, LANES), 0)
    line = jnp.sum(jnp.where(lane == row, sums, 0.0), axis=0, keepdims=True)
    sums_ref[...] = jnp.broadcast_to(line, sums_ref.shape)


def galerkin(sums):
    n, count = ITERS, 2 * ITERS - 1
    line = jnp.sum(sums, axis=0, keepdims=True)
    lane = lax.broadcasted_iota(jnp.int32, line.shape, 1)

    def pick(k):
        return jnp.sum(jnp.where(lane == k, line, 0.0), axis=1, keepdims=True)

    powers = [pick(k) for k in range(count)]
    firsts = [pick(count + k) for k in range(n)]
    steps = [pick(count + n + k) for k in range(count + 1)]
    matrix = [jnp.concatenate([powers[k], steps[k + 1]], axis=0) for k in range(count)]
    right = [jnp.concatenate([firsts[k], steps[k]], axis=0) for k in range(n)]
    low = [[None] * n for _ in range(n)]
    scale = [None] * n
    quality = None
    for j in range(n):
        pivot = matrix[2 * j]
        for k in range(j):
            pivot = pivot - low[j][k] * low[j][k] * scale[k][0]
        share = pivot / matrix[2 * j]
        fine = share > 1e-7
        quality = jnp.where(fine, share, 0.0) if quality is None else jnp.minimum(quality, jnp.where(fine, share, 0.0))
        inverse = jnp.where(fine, 1.0 / pivot, 0.0)
        scale[j] = (pivot, inverse)
        for r in range(j + 1, n):
            entry = matrix[r + j]
            for k in range(j):
                entry = entry - low[r][k] * low[j][k] * scale[k][0]
            low[r][j] = entry * inverse
    part = list(right)
    for r in range(n):
        for k in range(r):
            part[r] = part[r] - low[r][k] * part[k]
    part = [part[r] * scale[r][1] for r in range(n)]
    for r in reversed(range(n)):
        for k in range(r + 1, n):
            part[r] = part[r] - low[k][r] * part[k]
    first = quality[0:1] >= quality[1:2]
    by_power = [jnp.where(first, p[0:1], 0.0) for p in part]
    by_step = [jnp.where(first, 0.0, p[1:2]) for p in part]
    return by_power, by_step


def render_kernel(
    sums_ref, vec_ref, faces_ref, lower_ref, velocity_ref, table_ref, out_ref, press, flat, turned,
    *, ngx, ngz, zl, xl, chunk, step
):
    S, L = ngx * ngz, zl * xl
    yl = S * chunk
    slot = Slot(zl, xl, chunk)
    height = slot.height
    move = Shifts(ngx, ngz, zl, xl)
    by_power, by_step = galerkin(sums_ref[...])
    by_power = [v.reshape(1, 1, 1) for v in by_power]
    by_step = [v.reshape(1, 1, 1) for v in by_step]
    for a in range(0, chunk + 1, step):
        b = min(a + step, chunk + 1)
        levels = [vec_ref[k, HALO - 1 + a : HALO - 1 + b] for k in range(ITERS)]
        basis = differences(levels)[0]
        value = 0.0
        for k in range(ITERS):
            value = value + by_power[k] * basis[k] + by_step[k] * levels[k]
        press[a:b] = value
    spot = lax.broadcasted_iota(jnp.int32, (S, L), 1)
    sides = [jnp.zeros((S, L), F32) for _ in range(slot.deep)]
    for a in range(0, chunk, step):
        b = min(a + step, chunk)
        p = press[a + 1 : b + 1]
        fronts = (
            jnp.where(move.z_low, 0.0, move.below_z(p)),
            jnp.where(move.x_low, 0.0, move.below_x(p)),
            press[a:b],
        )
        pieces = []
        for k, front in enumerate(fronts):
            lower = lower_ref[a:b] if k == 2 else faces_ref[2 * k, a:b]
            pieces.append(velocity_ref[k, a:b] - lower * (p - front))
        scalar = pieces[0] + pieces[1] + pieces[2]
        if a == 0:
            out_ref[pl.ds(slot.side, S, stride=height), :] = pieces[2][0]
        for c in range(a, b):
            out_ref[pl.ds(c, S, stride=height), :] = p[c - a]
            flat[pl.ds(c, S, stride=chunk), :] = scalar[c - a]
            base = c // slot.deep * slot.width
            deep = roll(pieces[0][c - a], base, 1)
            where = (spot - (base + xl)) * xl
            wide = jnp.take_along_axis(pieces[1][c - a], jnp.clip(where, 0, L - 1), axis=1, mode="promise_in_bounds")
            r = c % slot.deep
            sides[r] = jnp.where(spot >= base, jnp.where(spot >= base + xl, wide, deep), sides[r])
    for r, side in enumerate(sides):
        out_ref[pl.ds(slot.faces + r, S, stride=height), :] = side
    turned[...] = flat[...].T.reshape(zl, xl, yl)

    side = ngz * chunk
    band = LANES // 4
    functions = table_ref.shape[0] // ngz
    lane = lax.broadcasted_iota(jnp.int32, (xl, yl), 1)

    def curve_sums(index):
        rows = [jnp.broadcast_to(table_ref[index, r : r + 1, :], (xl, yl)) for r in range(9)]
        rates, bases, gain = rows[:4], rows[4:8], rows[8]
        through = jnp.ones((xl, yl), F32)
        colors = [jnp.zeros((xl, yl), F32) for _ in range(3)]
        for z in range(zl):
            x = turned[z]
            curves = [1.0 / (1.0 + jnp.exp2(rates[c] * x + bases[c])) for c in range(4)]
            opacity = gain * curves[3]
            weight = through * opacity
            colors = [colors[c] + weight * curves[c] for c in range(3)]
            through = through * (1.0 - opacity)
        return colors + [through]

    for i in range(ngz):
        images = [jnp.zeros((xl, LANES), F32) for _ in range(ngx)]
        for t in range(functions):
            planes = curve_sums(i * functions + t)
            span = 1
            while span < ngz:
                behind = [roll(plane, -span * chunk, 1) for plane in planes]
                planes = [planes[c] + planes[3] * behind[c] for c in range(3)] + [planes[3] * behind[3]]
                span *= 2
            planes[3] = 1.0 - planes[3]
            planes = [roll(plane, c * band, 1) for c, plane in enumerate(planes)]
            here = (lane % band) // chunk == t
            for k in range(ngx):
                merged = planes[0]
                for c in range(1, 4):
                    merged = jnp.where((lane + (LANES - k * side) % LANES) % LANES // band == c, planes[c], merged)
                images[k] = jnp.where(here, roll(merged, t * chunk - k * side, 1), images[k])
        for k in range(ngx):
            place = (k * ngz + i) * height + slot.images
            out_ref[place : place + xl, :] = images[k]


def unpack_kernel(in_ref, lower_ref, velocity_ref, corrected_ref, images_ref, flat, sides, *, table, chunk):
    zl, xl, yl = corrected_ref.shape[1:]
    slot = Slot(zl, xl, chunk)
    functions = images_ref.shape[0]
    band = LANES // 4
    lane = lax.broadcasted_iota(jnp.int32, (xl, yl), 1)
    images = [jnp.zeros((xl, yl), F32) for _ in range(functions * 4)]
    for c in range(yl // chunk):
        place = owner(table, c)
        flat[c * chunk : (c + 1) * chunk, :] = in_ref[place, :chunk, :]
        faces = in_ref[place, slot.faces : slot.faces + 8, :]
        for g in range(-(-chunk // slot.deep)):
            rows = min(slot.deep, chunk - g * slot.deep)
            start = c * chunk + g * slot.deep
            sides[start : start + rows, :] = roll(faces, -g * slot.width, 1)[:rows]
        source = in_ref[place, slot.images : slot.images + xl, :]
        here = (lane >= c * chunk) & (lane < (c + 1) * chunk)
        for k in range(functions * 4):
            shift = c * chunk - (k % 4 * band + k // 4 * chunk)
            images[k] = jnp.where(here, roll(source, shift, 1), images[k])
    for k, image in enumerate(images):
        images_ref[k // 4, k % 4] = image
    p = flat[...].T.reshape(zl, xl, yl)
    faces = sides[...].T
    deep, wide = faces[:xl], faces[xl : xl + zl]
    front = in_ref[owner(table, 0), slot.side : slot.side + 1, :]
    high = jnp.broadcast_to(front, (yl, zl * xl)).T.reshape(zl, xl, yl)
    x = lax.broadcasted_iota(jnp.int32, (zl, xl, yl), 1)
    y = lax.broadcasted_iota(jnp.int32, (zl, xl, yl), 2)
    inner = velocity_ref[0, 1:] - lower_ref[0, 1:] * (p[1:] - p[:-1])
    corrected_ref[0, 0], corrected_ref[0, 1:] = deep, inner
    inner = velocity_ref[1] - lower_ref[1] * (p - roll(p, 1, 1))
    corrected_ref[1] = jnp.where(x == 0, wide[:, None, :], inner)
    inner = velocity_ref[2] - lower_ref[2] * (p - roll(p, 1, 2))
    corrected_ref[2] = jnp.where(y == 0, high, inner)


def solution(mesh):
    ngx, ngy, ngz = mesh.shape["gx"], mesh.shape["gy"], mesh.shape["gz"]
    S, devices = ngx * ngz, ngx * ngy * ngz
    table = [x * ngz + z for x, z in snake(ngx, ngz)]
    places = chain(ngx, ngy, ngz)

    def local(phase_field, thermal, velocity, transfer_slope, transfer_offset, transfer_gain):
        zl, xl, yl = thermal.shape
        L, chunk = zl * xl, yl // S
        functions = transfer_slope.shape[0] // ngz
        assert yl % S == 0 and L == LANES and yl == LANES and max(ngx, functions) * 4 * chunk <= LANES
        assert ngz & (ngz - 1) == 0
        hops = -(-HALO // chunk)
        margin = min(chunk, HALO)
        step = max(1, 4 * 8 // S)

        vmem = pl.BlockSpec(memory_space=pltpu.VMEM)

        def call(body, specs, out, scratch=(), limit=None, **kwargs):
            kernel = pl.pallas_call(
                lambda *refs: body(*refs, **kwargs),
                in_specs=specs,
                out_specs=jax.tree.map(lambda _: vmem, out),
                out_shape=out,
                scratch_shapes=[pltpu.VMEM(s, F32) for s in scratch],
                compiler_params=pltpu.CompilerParams(vmem_limit_bytes=limit),
            )

            def run(*args):
                return kernel(*[near(a) if spec is vmem else a for a, spec in zip(args, specs)])

            return run

        def near(array):
            return pltpu.with_memory_space_constraint(array, pltpu.VMEM)

        def shaped(*shape):
            return jax.ShapeDtypeStruct(shape, F32)

        def placed(*shape):
            return pltpu.VMEM(shape, F32)

        free = pl.BlockSpec()
        tables = (transfer_slope.T, transfer_offset.T, transfer_gain[None, :])
        block = (zl, xl, yl)
        blocks, home_density, kept = call(
            pack_kernel,
            [free] * 3,
            (placed(S, chunk * FIELDS, L), placed(*block), placed(3, *block)),
            table=table, chunk=chunk,
        )(phase_field, thermal, velocity)
        pencils = lax.all_to_all(blocks, ("gx", "gz"), 0, 0, tiled=True)
        every = ("gx", "gy", "gz")
        own = pencils.reshape(-1, L)
        sizes = dict(ngx=ngx, ngz=ngz, zl=zl, xl=xl, chunk=chunk)
        message = (margin + min(margin, HALO - 1) + 1, S, L)
        messages = call(edges_kernel, [vmem], [placed(*message)] * (2 * hops), margin=margin, **sizes)(own)
        swaps = [(messages[i], hop_swaps(places, i // 2 + 1, i % 2)) for i in range(2 * hops)]
        runs = hops == 1 and ngy % 2 == 0 and S % 2 == 0
        if runs:
            swaps = [swaps[0]] + [(messages[1], run_swaps(places, 2 * S, start)) for start in (0, S)]
        swapped = []
        for value, pairs in swaps:
            swapped.append(lax.ppermute(value, every, pairs))
        *own_values, home_lower, curves = call(
            own_kernel,
            [vmem] * 2 + [free] * 3,
            (
                *[placed(*lead, chunk, S, L) for lead in ((), (), (3,), (4,), (7,), (ITERS,), (), ())],
                placed(SUMS, S, L),
                placed(3, *block),
                placed(transfer_gain.shape[0], 16, LANES),
            ),
            limit=VMEM_LIMIT, step=step, depth=zl * ngz, **sizes,
        )(own, home_density, *tables)
        velocities, faces = own_values[2:4]
        wide = chunk + 2 * HALO
        levels, lower, sums = call(
            krylov_kernel,
            [vmem] * (9 + len(swapped)),
            (placed(ITERS, wide, S, L), placed(chunk, S, L), placed(devices, LANES)),
            ((2, hops) + message, (wide, S, L), (7, wide, S, L), (chunk, S, L), (wide, S, L)),
            limit=VMEM_LIMIT, hops=hops, margin=margin, step=step, places=devices, runs=int(runs), **sizes,
        )(*own_values, *swapped)
        sums = lax.all_to_all(sums, every, 0, 0, tiled=True)
        height = Slot(zl, xl, chunk).height
        packed = call(
            render_kernel,
            [vmem] * 6,
            placed(S * height, LANES),
            ((chunk + 1, S, L), (yl, L), (zl, xl, yl)),
            step=step, **sizes,
        )(sums, levels, faces, lower, velocities, curves)
        home = lax.all_to_all(packed.reshape(S, height, LANES), ("gx", "gz"), 0, 0, tiled=True)
        return call(
            unpack_kernel,
            [vmem] * 3,
            (shaped(3, *block), shaped(functions, 4, xl, yl)),
            ((yl, L), (yl, LANES)),
            table=table, chunk=chunk,
        )(home, home_lower, kept)

    return jax.shard_map(
        local,
        mesh=mesh,
        in_specs=(P("gz", "gx", "gy"), P("gz", "gx", "gy"), P(None, "gz", "gx", "gy"), P(), P(), P()),
        out_specs=(P(None, "gz", "gx", "gy"), P("gz", None, "gx", "gy")),
        check_vma=False,
    )
```
